32 devices in a mesh: heads: 4 (over x, core), batch: 8 (over z, y).
Axes of the slice: x: 2, y: 2, z: 4, core: 2. Of those that a mesh axis runs over, the one named last changes fastest.
Arguments:
- tokens: bfloat16 [8192, 2048], P('batch'), may hold values from -6 to 6
- lengths: int32 [8], P('batch'), may hold values from 256 to 1024, as said below
- cotangent: bfloat16 [8192, 2048], P('batch'), may hold values from -6 to 6
- attn_norm_gain: bfloat16 [2048], P('batch'), may hold values from 0.5 to 1.5
- query_norm_gain: bfloat16 [128], replicated, may hold values from 0.5 to 1.5
- key_norm_gain: bfloat16 [128], replicated, may hold values from 0.5 to 1.5
- w_query: bfloat16 [2048, 2048], P('batch', 'heads'), may hold values from -0.125 to 0.125
- w_gate_attn: bfloat16 [2048, 2048], P('batch', 'heads'), may hold values from -0.125 to 0.125
- w_key: bfloat16 [2048, 1024], P('batch', 'heads'), may hold values from -0.125 to 0.125
- w_value: bfloat16 [2048, 1024], P('batch', 'heads'), may hold values from -0.125 to 0.125
- w_out: bfloat16 [2048, 2048], P('batch', 'heads'), may hold values from -2 to 2
- mlp_norm_gain: bfloat16 [2048], P('batch'), may hold values from 0.5 to 1.5
- w_gate: bfloat16 [2048, 6144], P('batch', 'heads'), may hold values from -0.125 to 0.125
- w_up: bfloat16 [2048, 6144], P('batch', 'heads'), may hold values from -0.125 to 0.125
- w_down: bfloat16 [2048, 6144], P('batch', 'heads'), may hold values from -0.078125 to 0.078125
Outputs:
- output: bfloat16 [8192, 2048], P('batch')
- grad_tokens: bfloat16 [8192, 2048], P('batch')
- grad_attn_norm_gain: float32 [2048], P('batch')
- grad_query_norm_gain: float32 [128], replicated
- grad_key_norm_gain: float32 [128], replicated
- grad_w_query: float32 [2048, 2048], P('batch', 'heads')
- grad_w_gate_attn: float32 [2048, 2048], P('batch', 'heads')
- grad_w_key: float32 [2048, 1024], P('batch', 'heads')
- grad_w_value: float32 [2048, 1024], P('batch', 'heads')
- grad_w_out: float32 [2048, 2048], P('batch', 'heads')
- grad_mlp_norm_gain: float32 [2048], P('batch')
- grad_w_gate: float32 [2048, 6144], P('batch', 'heads')
- grad_w_up: float32 [2048, 6144], P('batch', 'heads')
- grad_w_down: float32 [2048, 6144], P('batch', 'heads')
- block_rms: float32 [5], replicated
The draws below stay inside these ranges and needn't reach their ends.
Inputs may be any that keep to these rules, and one draw needn't show every extreme that they name: The sequence of slot s takes the first lengths[s] rows of its 1024 rows, the rest are padding; some sequence fills its slot.
All inputs are finite; a program needn't handle non-finite values.
Results may differ from the reference program's by a relative error of at most 0.024.
Values may be sent and summed in bfloat16 or wider, within the bound.
A program may use at most 256 MiB of HBM per device.

```python
import jax
import jax.numpy as jnp
from jax import lax

D = 2048
HEADS = 16
KV = 8
HD = 128
FF = 6144
SLOT_LEN = 1024
TOKENS = 8192
SEQS = 8


def draw_lengths(key, part):
    span_top = SLOT_LEN - SLOT_LEN // 4 + 1
    first_draw = jax.random.randint(jax.random.fold_in(key, 11), (SEQS,), 0, span_top)
    second_draw = jax.random.randint(jax.random.fold_in(key, 12), (SEQS,), 0, span_top)
    drawn = SLOT_LEN // 4 + jnp.minimum(first_draw, second_draw)
    chosen = jax.random.randint(jax.random.fold_in(key, 13), (), 0, SEQS)
    return jnp.where(jnp.arange(SEQS) == chosen, SLOT_LEN, drawn).astype(jnp.int32)


def block_levels(own_key, shape, cuts, smallest, top_value):
    loudness = 1.0
    for axis_at, shards_of in cuts:
        steps = jax.random.uniform(jax.random.fold_in(jax.random.fold_in(own_key, 6), axis_at), (shards_of,), jnp.float32, smallest / len(cuts), top_value / len(cuts))
        loudness = loudness * jnp.repeat(jnp.exp(steps), shape[axis_at] // shards_of).reshape((-1,) + (1,) * (len(shape) - 1 - axis_at))
    return loudness


def normal_values(stream_key, dims, width, most, cuts=(), kind=jnp.bfloat16):
    factor_of = block_levels(stream_key, dims, cuts, -0.22, 0.18) if cuts else 1.0
    result = jax.random.normal(stream_key, dims, jnp.float32) * width * factor_of
    return jnp.minimum(jnp.maximum(result, -most), most).astype(kind)


def setup_inputs(seed: int = 0) -> dict:
    key_of = jax.random.split(jax.random.key(seed), 16)
    return {
        "tokens": normal_values(key_of[0], (TOKENS, D), 1.0, 6.0, ((0, 8),)),
        "lengths": draw_lengths(jax.random.fold_in(key_of[15], 71), 0),
        "cotangent": normal_values(key_of[2], (TOKENS, D), 1.0, 6.0, ((0, 8),)),
        "attn_norm_gain": jnp.clip(1.0 + 0.1 * jax.random.normal(key_of[3], (D,), jnp.float32), 0.5, 1.5).astype(jnp.bfloat16),
        "query_norm_gain": jnp.clip(1.0 + 0.1 * jax.random.normal(key_of[4], (HD,), jnp.float32), 0.5, 1.5).astype(jnp.bfloat16),
        "key_norm_gain": jnp.clip(1.0 + 0.1 * jax.random.normal(key_of[5], (HD,), jnp.float32), 0.5, 1.5).astype(jnp.bfloat16),
        "w_query": normal_values(key_of[6], (D, HEADS * HD), D ** -0.5, 0.125, ((0, 8), (1, 4))),
        "w_gate_attn": normal_values(key_of[7], (D, HEADS * HD), D ** -0.5, 0.125, ((0, 8), (1, 4))),
        "w_key": normal_values(key_of[8], (D, KV * HD), D ** -0.5, 0.125, ((0, 8), (1, 4))),
        "w_value": normal_values(key_of[9], (D, KV * HD), D ** -0.5, 0.125, ((0, 8), (1, 4))),
        "w_out": normal_values(key_of[10], (D, HEADS * HD), (4 * HEADS * HD // SLOT_LEN) ** -0.5, 2.0, ((0, 8), (1, 4))),
        "mlp_norm_gain": jnp.clip(1.0 + 0.1 * jax.random.normal(key_of[11], (D,), jnp.float32), 0.5, 1.5).astype(jnp.bfloat16),
        "w_gate": normal_values(key_of[12], (D, FF), D ** -0.5, 0.125, ((0, 8), (1, 4))),
        "w_up": normal_values(key_of[13], (D, FF), D ** -0.5, 0.125, ((0, 8), (1, 4))),
        "w_down": normal_values(key_of[14], (D, FF), FF ** -0.5, 0.078125, ((0, 8), (1, 4))),
    }


NORM_EPS = 1e-06
ROPE_THETA = 1000000.0
MASKED = -1e+30

@jax.custom_vjp
def low(v):
    return lax.optimization_barrier(v.astype(jnp.bfloat16)).astype(jnp.float32)

@jax.custom_vjp
def low_back(v):
    return v

def low_keep(v):
    return (low(v), None)

def low_pass(kept, grad):
    return (grad,)

def back_keep(v):
    return (v, None)

def back_low(kept, grad):
    return (low(grad),)
low.defvjp(low_keep, low_pass)
low_back.defvjp(back_keep, back_low)

def norm_rows(in_value, gain):
    return in_value * lax.rsqrt(lax.optimization_barrier(jnp.mean(in_value * in_value, axis=-1, keepdims=True)) + NORM_EPS) * gain

def rotary_tables(row_count, head_width):
    half_width = head_width // 2
    positions = (jnp.arange(row_count) % SLOT_LEN).astype(jnp.float32)
    inverse = ROPE_THETA ** (-(jnp.arange(half_width).astype(jnp.float32) * 2.0 / head_width))
    angles = positions[:, None] * inverse[None, :]
    angles = jnp.concatenate([angles, angles], axis=1)
    return (jnp.cos(angles), jnp.sin(angles))

def rotate_rows(in_value, cos_table, sin_table):
    half_width = in_value.shape[-1] // 2
    turned = jnp.concatenate([-in_value[..., half_width:], in_value[..., :half_width]], axis=-1)
    return in_value * cos_table[:, None, :] + turned * sin_table[:, None, :]

def attend_slot(operands):
    slot_queries, slot_keys, slot_values, seq_length = operands
    highest = lax.Precision.HIGHEST
    grouped = slot_queries.reshape(SLOT_LEN, KV, HEADS // KV, HD)
    scores = jnp.einsum('qkgd,ckd->kgqc', grouped, slot_keys, precision=highest) * HD ** (-0.5)
    scores = low_back(scores)
    places = jnp.arange(SLOT_LEN)
    allowed = (places[None, :] <= places[:, None]) & (places[None, :] < seq_length)
    scores = jnp.where(allowed, scores, MASKED)
    soft_weights = low(jax.nn.softmax(scores, axis=-1))
    attended = low_back(jnp.einsum('kgqc,ckd->qkgd', soft_weights, slot_values, precision=highest))
    return attended.reshape(SLOT_LEN, HEADS, HD)

def forward_pass(tokens_f, attn_gain, query_gain, key_gain, query_weight, gate_attn_weight, key_weight, value_weight, out_weight, mlp_gain, gate_weight, up_weight, down_weight, valid, lengths):
    highest = lax.Precision.HIGHEST

    def matmul(left_side, right_side):
        return jnp.dot(left_side, right_side, precision=highest, preferred_element_type=jnp.float32)
    row_count = tokens_f.shape[0]
    normed_one = low(norm_rows(tokens_f, attn_gain))
    queries = low_back(matmul(normed_one, query_weight))
    gate_logit = low_back(matmul(normed_one, gate_attn_weight))
    keys_pre = low_back(matmul(normed_one, key_weight))
    values = low(low_back(matmul(normed_one, value_weight)))
    cos_table, sin_table = rotary_tables(row_count, HD)
    query_rot = low(rotate_rows(norm_rows(queries.reshape(row_count, HEADS, HD), query_gain), cos_table, sin_table))
    key_rot = low(rotate_rows(norm_rows(keys_pre.reshape(row_count, KV, HD), key_gain), cos_table, sin_table))
    slot_count = row_count // SLOT_LEN
    attended = lax.map(jax.checkpoint(attend_slot), (query_rot.reshape(slot_count, SLOT_LEN, HEADS, HD), key_rot.reshape(slot_count, SLOT_LEN, KV, HD), values.reshape(slot_count, SLOT_LEN, KV, HD), lengths))
    gate_sig = jax.nn.sigmoid(gate_logit.reshape(row_count, HEADS, HD))
    gated = low((attended.reshape(row_count, HEADS, HD) * gate_sig).reshape(row_count, HEADS * HD))
    attn_out = low_back(matmul(gated, out_weight.T))
    hidden_res = tokens_f + attn_out
    normed_two = low(norm_rows(hidden_res, mlp_gain))
    gate_pre = low_back(matmul(normed_two, gate_weight))
    up_pre = low_back(matmul(normed_two, up_weight))
    activated = low(jax.nn.silu(gate_pre) * up_pre)
    mlp_out = low_back(matmul(activated, down_weight.T))
    return (valid * (hidden_res + mlp_out), (hidden_res, attn_out, mlp_out))

def reference(tokens, lengths, cotangent, attn_norm_gain, query_norm_gain, key_norm_gain, w_query, w_gate_attn, w_key, w_value, w_out, mlp_norm_gain, w_gate, w_up, w_down):
    row_count = tokens.shape[0]
    valid = (jnp.arange(SLOT_LEN)[None, :] < lengths[:, None]).reshape(row_count, 1).astype(jnp.float32)
    floats = [member.astype(jnp.float32) for member in (tokens, attn_norm_gain, query_norm_gain, key_norm_gain, w_query, w_gate_attn, w_key, w_value, w_out, mlp_norm_gain, w_gate, w_up, w_down)]
    output_f, pullback, extras = jax.vjp(lambda *pieces: forward_pass(*pieces, valid, lengths), *floats, has_aux=True)
    grads = pullback(cotangent.astype(jnp.float32))
    hidden_res, attn_out, mlp_out = extras
    tokens_f = floats[0]
    token_count = jnp.sum(lengths).astype(jnp.float32)

    def mean_square(field):
        return jnp.sum(valid * field * field) / (token_count * D)
    block_rms = jnp.sqrt(jnp.stack([mean_square(tokens_f), mean_square(hidden_res), mean_square(hidden_res + mlp_out), mean_square(attn_out), mean_square(mlp_out)]))
    return (output_f.astype(jnp.bfloat16), grads[0].astype(jnp.bfloat16), grads[1], grads[2], grads[3], grads[4], grads[5], grads[6], grads[7], grads[8], grads[9], grads[10], grads[11], grads[12], block_rms)
```

```python
import functools

import jax
import jax.numpy as jnp
from jax import lax
from jax.experimental import pallas as pl
from jax.experimental.pallas import tpu as pltpu
from jax.sharding import PartitionSpec as P

SLOT_LEN = 1024
MESH = pl.DeviceIdType.MESH


NORM_EPS = 1e-06
ROPE_THETA = 1000000.0
MASKED = -1e30


def matmul(left_side, right_side):
    return jnp.dot(left_side, right_side, preferred_element_type=jnp.float32)


def contract_last(left_side, right_side):
    return lax.dot_general(
        left_side, right_side, (((1,), (1,)), ((), ())), preferred_element_type=jnp.float32
    )


def contract_rows(left_side, right_side):
    return lax.dot_general(
        left_side, right_side, (((0,), (0,)), ((), ())), preferred_element_type=jnp.float32
    )


def norm_rows(in_value, gain):
    scale_rows = lax.rsqrt(jnp.mean(in_value * in_value, axis=-1, keepdims=True) + NORM_EPS)
    return (in_value * scale_rows * gain, scale_rows)


def norm_back(in_value, scale_rows, gain, grad_normed):
    normed = in_value * scale_rows
    grad_gain = jnp.sum(grad_normed * normed, axis=tuple(range(in_value.ndim - 1)))
    grad_scaled = grad_normed * gain
    grad_value = scale_rows * (
        grad_scaled - normed * jnp.mean(grad_scaled * normed, axis=-1, keepdims=True)
    )
    return (grad_value, grad_gain)


def rotary_tables(row_count, head_width):
    half_width = head_width // 2
    positions = (lax.iota(jnp.int32, row_count) % SLOT_LEN).astype(jnp.float32)
    inverse = ROPE_THETA ** (
        -(lax.iota(jnp.int32, half_width).astype(jnp.float32) * 2.0 / head_width)
    )
    angles = positions[:, None] * inverse[None, :]
    angles = jnp.concatenate([angles, angles], axis=1)
    return (jnp.cos(angles), jnp.sin(angles))


def turn_half(in_value):
    half_width = in_value.shape[-1] // 2
    return jnp.concatenate([-in_value[..., half_width:], in_value[..., :half_width]], axis=-1)


def rotate_rows(in_value, cos_table, sin_table):
    return in_value * cos_table[:, None, :] + turn_half(in_value) * sin_table[:, None, :]


def unrotate_rows(in_value, cos_table, sin_table):
    return in_value * cos_table[:, None, :] - turn_half(in_value) * sin_table[:, None, :]


def block_scores(block_queries, slot_keys, block_index, block_rows, seq_length, scale_factor):
    scores = (
        jnp.einsum("qkgd,ckd->kgqc", block_queries, slot_keys, preferred_element_type=jnp.float32)
        * scale_factor
    )
    key_places = lax.iota(jnp.int32, SLOT_LEN)
    query_places = block_index * block_rows + lax.iota(jnp.int32, block_rows)
    allowed = (key_places[None, :] <= query_places[:, None]) & (key_places[None, :] < seq_length)
    return jnp.where(allowed, scores, MASKED)


def attend_forward(query_rot, key_rot, value_heads, lengths):
    row_count, head_count, head_width = query_rot.shape
    kv_count = key_rot.shape[1]
    group_size = head_count // kv_count
    block_rows = min(512, SLOT_LEN)
    block_count = SLOT_LEN // block_rows
    slot_count = row_count // SLOT_LEN
    scale_factor = head_width ** (-0.5)

    def one_slot(operands):
        slot_queries, slot_keys, slot_values, seq_length = operands
        grouped = slot_queries.reshape(SLOT_LEN, kv_count, group_size, head_width)
        outputs = []
        totals = []
        for block_index in range(block_count):
            lower = block_index * block_rows
            scores = block_scores(
                grouped[lower : lower + block_rows],
                slot_keys,
                block_index,
                block_rows,
                seq_length,
                scale_factor,
            )
            largest = jnp.max(scores, axis=-1, keepdims=True)
            exponent = jnp.exp(scores - largest)
            denominator = jnp.sum(exponent, axis=-1, keepdims=True)
            soft_weights = (exponent / denominator).astype(jnp.bfloat16)
            outputs.append(
                jnp.einsum(
                    "kgqc,ckd->qkgd", soft_weights, slot_values, preferred_element_type=jnp.float32
                )
            )
            totals.append(largest + jnp.log(denominator))
        return (jnp.concatenate(outputs, axis=0), jnp.concatenate(totals, axis=2))

    attended, log_totals = lax.map(
        one_slot,
        (
            query_rot.reshape(slot_count, SLOT_LEN, head_count, head_width),
            key_rot.reshape(slot_count, SLOT_LEN, kv_count, head_width),
            value_heads.reshape(slot_count, SLOT_LEN, kv_count, head_width),
            lengths,
        ),
    )
    return (attended.reshape(row_count, head_count, head_width), log_totals)


def attend_backward(query_rot, key_rot, value_heads, grad_attended, log_totals, lengths):
    row_count, head_count, head_width = query_rot.shape
    kv_count = key_rot.shape[1]
    group_size = head_count // kv_count
    block_rows = min(512, SLOT_LEN)
    block_count = SLOT_LEN // block_rows
    slot_count = row_count // SLOT_LEN
    scale_factor = head_width ** (-0.5)

    def one_slot(operands):
        slot_queries, slot_keys, slot_values, slot_grads, slot_totals, seq_length = operands
        grouped = slot_queries.reshape(SLOT_LEN, kv_count, group_size, head_width)
        grouped_grads = slot_grads.reshape(SLOT_LEN, kv_count, group_size, head_width)
        grad_keys = jnp.zeros((SLOT_LEN, kv_count, head_width), jnp.float32)
        grad_values = jnp.zeros((SLOT_LEN, kv_count, head_width), jnp.float32)
        query_parts = []
        for block_index in range(block_count):
            lower = block_index * block_rows
            block_queries = grouped[lower : lower + block_rows]
            block_grads = grouped_grads[lower : lower + block_rows]
            scores = block_scores(
                block_queries, slot_keys, block_index, block_rows, seq_length, scale_factor
            )
            probs_true = jnp.exp(scores - slot_totals[:, :, lower : lower + block_rows])
            grad_probs = jnp.einsum(
                "qkgd,ckd->kgqc", block_grads, slot_values, preferred_element_type=jnp.float32
            )
            inner_sum = jnp.sum(grad_probs * probs_true, axis=-1, keepdims=True)
            grad_scores = (probs_true * (grad_probs - inner_sum)).astype(jnp.bfloat16)
            query_parts.append(
                jnp.einsum(
                    "kgqc,ckd->qkgd", grad_scores, slot_keys, preferred_element_type=jnp.float32
                )
                * scale_factor
            )
            grad_keys = (
                grad_keys
                + jnp.einsum(
                    "kgqc,qkgd->ckd", grad_scores, block_queries, preferred_element_type=jnp.float32
                )
                * scale_factor
            )
            grad_values = grad_values + jnp.einsum(
                "kgqc,qkgd->ckd",
                probs_true.astype(jnp.bfloat16),
                block_grads,
                preferred_element_type=jnp.float32,
            )
        return (jnp.concatenate(query_parts, axis=0), grad_keys, grad_values)

    grad_queries, grad_keys, grad_values = lax.map(
        one_slot,
        (
            query_rot.reshape(slot_count, SLOT_LEN, head_count, head_width),
            key_rot.reshape(slot_count, SLOT_LEN, kv_count, head_width),
            value_heads.reshape(slot_count, SLOT_LEN, kv_count, head_width),
            grad_attended.reshape(slot_count, SLOT_LEN, head_count, head_width),
            log_totals,
            lengths,
        ),
    )
    return (
        grad_queries.reshape(row_count, head_count, head_width),
        grad_keys.reshape(row_count, kv_count, head_width),
        grad_values.reshape(row_count, kv_count, head_width),
    )


def grid_of(n):
    inner = 2 if n <= 8 else 4
    return (n // inner, inner)

def gather_kernel(plan, rows_n, cols_n, *refs):
    count = plan["count"]
    ins, outs = refs[:count], refs[count:2*count]
    send_up, send_down, send_side, recv, local_sem = refs[2*count:]
    A, B = rows_n, cols_n
    me = lax.axis_index("batch")
    a, b = me // B, me % B
    units = plan["units"]

    def block(u, blk):
        i, lo, width = units[u][:3]
        ref = outs[i].at[blk]
        return ref if lo is None else ref.at[:, pl.ds(lo, width)]

    def own(u):
        i, lo, width = units[u][:3]
        return ins[i] if lo is None else ins[i].at[:, pl.ds(lo, width)]

    def put(u, src, blk, sem, target):
        pltpu.make_async_remote_copy(src, block(u, blk), sem, recv.at[u, blk], device_id={"batch": target}, device_id_type=pl.DeviceIdType.MESH).start()

    def arrived(u, blk):
        pltpu.make_async_copy(block(u, blk), block(u, blk), recv.at[u, blk]).wait()

    def sent(u, sem):
        pltpu.make_async_copy(own(u), own(u), sem).wait()

    barrier = pltpu.get_barrier_semaphore()
    def greet(target):
        pl.semaphore_signal(barrier, inc=1, device_id={"batch": target}, device_id_type=pl.DeviceIdType.MESH)
    up_ok, down_ok = a < A - 1, a > 0
    pl.when(up_ok)(lambda: greet(me + B))
    pl.when(down_ok)(lambda: greet(me - B))
    for k in range(1, B):
        greet(a * B + (b + k) % B)
    pl.semaphore_wait(barrier, up_ok.astype(jnp.int32) + down_ok.astype(jnp.int32) + (B - 1))

    nu = len(units)
    def up(u, src, blk, slot):
        @pl.when(up_ok)
        def _():
            put(u, src, blk, send_up.at[u, slot], me + B)
    def down(u, src, blk, slot):
        @pl.when(down_ok)
        def _():
            put(u, src, blk, send_down.at[u, slot], me - B)
    def side(u, src, blk, step):
        for k in range(1, B):
            put(u, src, blk, send_side.at[u, step * (B - 1) + k - 1], a * B + (b + k) % B)

    for u in range(nu):
        up(u, own(u), me, b)
        down(u, own(u), me, b)
        side(u, own(u), me, 0)
    for i in range(count):
        pltpu.make_async_copy(ins[i], outs[i].at[me], local_sem.at[i]).start()

    for u in range(nu):
        if units[u][3]:
            for k in range(1, B):
                bb = (b + k) % B
                blk = a * B + bb
                arrived(u, blk)
                up(u, block(u, blk), blk, bb)
                down(u, block(u, blk), blk, bb)
    for s in range(1, A):
        for u in range(nu):
            first = units[u][3]
            @pl.when(a - s >= 0)
            def _(u=u, first=first):
                for k in range(B if first else 1):
                    bb = (b + k) % B
                    blk = (a - s) * B + bb
                    arrived(u, blk)
                    up(u, block(u, blk), blk, s * B + bb)
                    if not first:
                        side(u, block(u, blk), blk, 2 * s - 1)
            @pl.when(a + s < A)
            def _(u=u, first=first):
                for k in range(B if first else 1):
                    bb = (b + k) % B
                    blk = (a + s) * B + bb
                    arrived(u, blk)
                    down(u, block(u, blk), blk, s * B + bb)
                    if not first:
                        side(u, block(u, blk), blk, 2 * s)
    for u in range(nu):
        if not units[u][3]:
            for s in range(A):
                for k in range(1, B):
                    bb = (b + k) % B
                    @pl.when(a - s >= 0)
                    def _(u=u, s=s, bb=bb):
                        arrived(u, (a - s) * B + bb)
                    if s:
                        @pl.when(a + s < A)
                        def _(u=u, s=s, bb=bb):
                            arrived(u, (a + s) * B + bb)
    for u in range(nu):
        first = units[u][3]
        for s in range(A):
            for k in range(B if first else 1):
                bb = (b + k) % B
                @pl.when((a - s >= 0) & up_ok)
                def _(u=u, s=s, bb=bb):
                    sent(u, send_up.at[u, s * B + bb])
                @pl.when((a + s < A) & down_ok)
                def _(u=u, s=s, bb=bb):
                    sent(u, send_down.at[u, s * B + bb])
            if s == 0 or not first:
                for k in range(1, B):
                    if s == 0:
                        sent(u, send_side.at[u, k - 1])
                    else:
                        @pl.when(a - s >= 0)
                        def _(u=u, s=s, k=k):
                            sent(u, send_side.at[u, (2 * s - 1) * (B - 1) + k - 1])
                        @pl.when(a + s < A)
                        def _(u=u, s=s, k=k):
                            sent(u, send_side.at[u, (2 * s) * (B - 1) + k - 1])
    for i in range(count):
        pltpu.make_async_copy(ins[i], outs[i].at[me], local_sem.at[i]).wait()


def gather_all(shards, plan_units, cid):
    n = lax.axis_size("batch")
    A, B = grid_of(n)
    nu = len(plan_units)
    plan = {"count": len(shards), "units": plan_units}
    outs = [jax.ShapeDtypeStruct((n,) + s.shape, s.dtype) for s in shards]
    res = pl.pallas_call(
        functools.partial(gather_kernel, plan, A, B),
        out_shape=outs,
        in_specs=[pl.BlockSpec(memory_space=pltpu.VMEM)] * len(shards),
        out_specs=[pl.BlockSpec(memory_space=pl.ANY)] * len(shards),
        scratch_shapes=[
            pltpu.SemaphoreType.DMA((nu, A * B)),
            pltpu.SemaphoreType.DMA((nu, A * B)),
            pltpu.SemaphoreType.DMA((nu, (2 * A - 1) * (B - 1))),
            pltpu.SemaphoreType.DMA((nu, n)),
            pltpu.SemaphoreType.DMA((len(shards),)),
        ],
        compiler_params=pltpu.CompilerParams(collective_id=cid, has_side_effects=True),
        cost_estimate=pl.CostEstimate(flops=0, bytes_accessed=sum(s.size for s in shards) * 60, transcendentals=0),
    )(*shards)
    return [r.reshape((n * r.shape[1],) + r.shape[2:]) if r.shape[1] > 1 else r.reshape(-1) for r in res]


def scatter_kernel(units, count, A, B, *refs):
    nu = len(units)
    ins, outs = refs[:count], refs[count:2 * count]
    rest = list(refs[2 * count:])
    own, side_in, up_in, down_in = (rest[k * nu:(k + 1) * nu] for k in range(4))
    load_sem, side_send, side_recv, up_send, up_recv, down_send, down_recv = rest[4 * nu:]
    me = lax.axis_index("batch")
    a, b = me // B, me % B
    up_ok, down_ok = a < A - 1, a > 0

    def piece(u, blk):
        i, lo, width, _ = units[u]
        return ins[i].at[blk, :, pl.ds(lo, width)]

    barrier = pltpu.get_barrier_semaphore()
    def greet(target):
        pl.semaphore_signal(barrier, inc=1, device_id={"batch": target}, device_id_type=MESH)
    pl.when(up_ok)(lambda: greet(me + B))
    pl.when(down_ok)(lambda: greet(me - B))
    for k in range(1, B):
        greet(a * B + (b + k) % B)

    def at_distance(d, fn):
        if d == 0:
            return
        @pl.when(a + d < A)
        def _():
            fn(a + d, True)
        @pl.when(a - d >= 0)
        def _():
            fn(a - d, False)

    def load(u, slot, blk):
        return pltpu.make_async_copy(piece(u, blk), own[u].at[slot], load_sem.at[u, slot])

    for d in range(A - 1, -1, -1):
        for u in range(nu):
            first = units[u][3]
            def start(dest, _=None, u=u, first=first):
                if first:
                    for bb in range(B):
                        load(u, dest * B + bb, dest * B + bb).start()
                else:
                    load(u, dest, dest * B + b).start()
            at_distance(d, start) if d else start(a)
    pl.semaphore_wait(barrier, up_ok.astype(jnp.int32) + down_ok.astype(jnp.int32) + (B - 1))

    for d in range(A - 1, -1, -1):
        for u in range(nu):
            if units[u][3]:
                continue
            def start(dest, _=None, u=u):
                for k in range(1, B):
                    bb = (b + k) % B
                    pltpu.make_async_remote_copy(
                        piece(u, dest * B + bb), side_in[u].at[k - 1, dest], side_send.at[u, k - 1, dest],
                        side_recv.at[u, k - 1, dest], device_id={"batch": a * B + bb}, device_id_type=MESH).start()
            at_distance(d, start) if d else start(a)

    def await_bytes(ref, sem):
        pltpu.make_async_copy(ref, ref, sem).wait()

    R = own[0].shape[1]
    step_rows = min(R, 32)

    def add_into(target, terms):
        def body(t, carry):
            rows = pl.ds(pl.multiple_of(t * step_rows, step_rows), step_rows)
            total = terms[0][rows, :].astype(jnp.float32)
            for term in terms[1:]:
                total = total + term[rows, :].astype(jnp.float32)
            target[rows, :] = total.astype(target.dtype)
            return carry
        lax.fori_loop(0, R // step_rows, body, 0)

    def local_terms(u, dest, bb):
        if units[u][3]:
            slot = dest * B + bb
            load(u, slot, slot).wait()
            return [own[u].at[slot]], slot
        load(u, dest, dest * B + b).wait()
        for k in range(1, B):
            await_bytes(side_in[u].at[k - 1, dest], side_recv.at[u, k - 1, dest])
        return [own[u].at[dest]] + [side_in[u].at[k - 1, dest] for k in range(1, B)], dest

    order = [u for u in range(nu) if units[u][3]] + [u for u in range(nu) if not units[u][3]]
    for d in range(A - 1, 0, -1):
        for u in order:
            def flow(dest, goes_up, u=u):
                for k in range(B if units[u][3] else 1):
                    terms, slot = local_terms(u, dest, (b + k) % B)
                    buf = (up_in if goes_up else down_in)[u].at[slot]
                    send, recv = (up_send, up_recv) if goes_up else (down_send, down_recv)
                    fed = down_ok if goes_up else up_ok
                    @pl.when(fed)
                    def _():
                        await_bytes(buf, recv.at[u, slot])
                        add_into(buf, [buf] + terms)
                    @pl.when(jnp.logical_not(fed))
                    def _():
                        add_into(buf, terms)
                    pltpu.make_async_remote_copy(
                        buf, buf, send.at[u, slot], recv.at[u, slot],
                        device_id={"batch": me + B if goes_up else me - B}, device_id_type=MESH).start()
            at_distance(d, flow)

    def out_piece(u):
        i, lo, width, _ = units[u]
        return outs[i].at[:, pl.ds(lo, width)]

    def arrive_home(u, bb, target):
        terms, slot = local_terms(u, a, bb)
        @pl.when(down_ok)
        def _():
            await_bytes(up_in[u].at[slot], up_recv.at[u, slot])
        @pl.when(up_ok)
        def _():
            await_bytes(down_in[u].at[slot], down_recv.at[u, slot])
        @pl.when(down_ok & up_ok)
        def _():
            add_into(target, terms + [up_in[u].at[slot], down_in[u].at[slot]])
        @pl.when(down_ok & jnp.logical_not(up_ok))
        def _():
            add_into(target, terms + [up_in[u].at[slot]])
        @pl.when(up_ok & jnp.logical_not(down_ok))
        def _():
            add_into(target, terms + [down_in[u].at[slot]])

    for u in order:
        if units[u][3]:
            for k in range(1, B):
                bb = (b + k) % B
                slot = a * B + bb
                arrive_home(u, bb, own[u].at[slot])
                pltpu.make_async_remote_copy(
                    own[u].at[slot], side_in[u].at[k - 1, 0], side_send.at[u, k - 1, 0], side_recv.at[u, k - 1, 0],
                    device_id={"batch": slot}, device_id_type=MESH).start()
            arrive_home(u, b, own[u].at[a * B + b])
        else:
            arrive_home(u, b, out_piece(u))
    for u in order:
        if units[u][3]:
            for k in range(1, B):
                await_bytes(side_in[u].at[k - 1, 0], side_recv.at[u, k - 1, 0])
            add_into(out_piece(u), [own[u].at[a * B + b]] + [side_in[u].at[k - 1, 0] for k in range(1, B)])

    for u in range(nu):
        first = units[u][3]
        for k in range(1, B):
            if first:
                await_bytes(side_in[u].at[k - 1, 0], side_send.at[u, k - 1, 0])
            else:
                for dest in range(A):
                    await_bytes(side_in[u].at[k - 1, dest], side_send.at[u, k - 1, dest])
        for d in range(A - 1, 0, -1):
            def done(dest, goes_up, u=u, first=first):
                send = up_send if goes_up else down_send
                for k in range(B if first else 1):
                    slot = dest * B + k if first else dest
                    await_bytes(up_in[u].at[slot], send.at[u, slot])
            at_distance(d, done)


def scatter_all(grads, units, cid, out_dtype=jnp.bfloat16):
    n = lax.axis_size("batch")
    A, B = grid_of(n)
    nu = len(units)
    R = grads[0].shape[0] // n
    views = [g.reshape(n, R, g.shape[1]) for g in grads]
    def slots(u):
        return n if units[u][3] else A
    scratch = []
    scratch += [pltpu.VMEM((slots(u), R, units[u][2]), jnp.bfloat16) for u in range(nu)]
    scratch += [pltpu.VMEM((B - 1, 1 if units[u][3] else A, R, units[u][2]), jnp.bfloat16) for u in range(nu)]
    scratch += [pltpu.VMEM((slots(u), R, units[u][2]), jnp.bfloat16) for u in range(nu)]
    scratch += [pltpu.VMEM((slots(u), R, units[u][2]), jnp.bfloat16) for u in range(nu)]
    dma = pltpu.SemaphoreType.DMA
    scratch += [dma((nu, n)), dma((nu, B - 1, A)), dma((nu, B - 1, A)), dma((nu, n)), dma((nu, n)), dma((nu, n)), dma((nu, n))]
    res = pl.pallas_call(
        functools.partial(scatter_kernel, units, len(grads), A, B),
        out_shape=[jax.ShapeDtypeStruct((R, g.shape[1]), out_dtype) for g in grads],
        in_specs=[pl.BlockSpec(memory_space=pl.ANY)] * len(grads),
        out_specs=[pl.BlockSpec(memory_space=pltpu.VMEM)] * len(grads),
        scratch_shapes=scratch,
        compiler_params=pltpu.CompilerParams(collective_id=cid, has_side_effects=True, vmem_limit_bytes=64 * 1024 * 1024 - 65536),
        cost_estimate=pl.CostEstimate(flops=0, bytes_accessed=sum(g.size for g in grads) * 8, transcendentals=0),
    )(*views)
    return list(res)


def column_units(widths, side_first, chunk=512):
    units = []
    for index, width in enumerate(widths):
        for low in range(0, width, chunk):
            units.append((index, low, min(chunk, width - low), (index, low) in side_first))
    return units


def local(
    tokens,
    lengths,
    cotangent,
    attn_norm_gain,
    query_norm_gain,
    key_norm_gain,
    w_query,
    w_gate_attn,
    w_key,
    w_value,
    w_out,
    mlp_norm_gain,
    w_gate,
    w_up,
    w_down,
):
    row_count, model_width = tokens.shape
    head_width = query_norm_gain.shape[0]
    shard_rows = w_query.shape[0]
    attn_shards = [w_query, w_gate_attn, w_key, w_value, w_out]
    attn_units = column_units([w.shape[1] for w in attn_shards], {(2, 0)})
    gain_shards = [attn_norm_gain.reshape(1, -1), mlp_norm_gain.reshape(1, -1)]
    query_full, gate_attn_full, key_full, value_full, out_full, gain_raw_one, gain_raw_two = gather_all(
        attn_shards + gain_shards,
        [(5, None, None, False), (6, None, None, False)] + attn_units,
        0,
    )
    gain_one = gain_raw_one.astype(jnp.float32)
    gain_two = gain_raw_two.astype(jnp.float32)
    query_gain = query_norm_gain.astype(jnp.float32)
    key_gain = key_norm_gain.astype(jnp.float32)
    valid = (
        (lax.iota(jnp.int32, SLOT_LEN)[None, :] < lengths[:, None])
        .reshape(row_count, 1)
        .astype(jnp.float32)
    )
    tokens_f = tokens.astype(jnp.float32)
    normed_one, scale_one = norm_rows(tokens_f, gain_one)
    input_one = normed_one.astype(jnp.bfloat16)
    queries = matmul(input_one, query_full)
    gate_logit = matmul(input_one, gate_attn_full)
    keys_pre = matmul(input_one, key_full)
    values = matmul(input_one, value_full).astype(jnp.bfloat16)
    head_count = queries.shape[1] // head_width
    kv_count = keys_pre.shape[1] // head_width
    cos_table, sin_table = rotary_tables(row_count, head_width)
    queries = queries.reshape(row_count, head_count, head_width)
    keys_pre = keys_pre.reshape(row_count, kv_count, head_width)
    query_normed, query_scale = norm_rows(queries, query_gain)
    key_normed, key_scale = norm_rows(keys_pre, key_gain)
    query_rot = rotate_rows(query_normed, cos_table, sin_table).astype(jnp.bfloat16)
    key_rot = rotate_rows(key_normed, cos_table, sin_table).astype(jnp.bfloat16)
    value_heads = values.reshape(row_count, kv_count, head_width)
    attended, log_totals = attend_forward(query_rot, key_rot, value_heads, lengths)
    gate_sig = jax.nn.sigmoid(gate_logit.reshape(row_count, head_count, head_width))
    gated = (attended * gate_sig).reshape(row_count, head_count * head_width).astype(jnp.bfloat16)
    attn_part = contract_last(gated, out_full).astype(jnp.bfloat16)
    attn_part, w_gate, w_up, w_down = lax.optimization_barrier((attn_part, w_gate, w_up, w_down))
    attn_out = lax.psum(attn_part, "heads").astype(jnp.float32)
    mlp_shards = [w_gate, w_up, w_down]
    mlp_widths = [w.shape[1] for w in mlp_shards]
    gate_full, up_full, down_full = gather_all(
        mlp_shards, column_units(mlp_widths, {(2, 0), (2, 512)}), 1
    )
    hidden_res = tokens_f + attn_out
    normed_two, scale_two = norm_rows(hidden_res, gain_two)
    input_two = normed_two.astype(jnp.bfloat16)
    gate_pre = matmul(input_two, gate_full)
    up_pre = matmul(input_two, up_full)
    gate_act = jax.nn.sigmoid(gate_pre)
    activated = (gate_pre * gate_act * up_pre).astype(jnp.bfloat16)
    mlp_part = contract_last(activated, down_full).astype(jnp.bfloat16)
    grad_out = cotangent.astype(jnp.float32) * valid
    grad_mlp = grad_out.astype(jnp.bfloat16)
    grad_activated = matmul(grad_mlp, down_full)
    grad_w_down = contract_rows(grad_mlp, activated).astype(jnp.bfloat16)
    grad_gate_pre = (
        grad_activated * up_pre * gate_act * (1.0 + gate_pre * (1.0 - gate_act))
    ).astype(jnp.bfloat16)
    grad_up_pre = (grad_activated * gate_pre * gate_act).astype(jnp.bfloat16)
    grad_w_gate = contract_rows(input_two, grad_gate_pre).astype(jnp.bfloat16)
    grad_w_up = contract_rows(input_two, grad_up_pre).astype(jnp.bfloat16)
    grad_two_part = contract_last(grad_gate_pre, gate_full) + contract_last(grad_up_pre, up_full)
    gain_two_part = jnp.sum(grad_two_part * (hidden_res * scale_two), axis=0)
    grad_two_send, mlp_part, grad_w_gate, grad_w_up, grad_w_down = lax.optimization_barrier(
        (grad_two_part.astype(jnp.bfloat16), mlp_part, grad_w_gate, grad_w_up, grad_w_down)
    )
    mlp_out = lax.psum(mlp_part, "heads").astype(jnp.float32)
    grad_input_two = lax.psum(grad_two_send, "heads").astype(jnp.float32)
    mlp_grads = scatter_all(
        [grad_w_gate, grad_w_up, grad_w_down], column_units(mlp_widths, {(2, 512), (2, 1024)}), 2
    )
    summed = hidden_res + mlp_out
    output = (summed * valid).astype(jnp.bfloat16)

    def masked_square(field):
        return jnp.sum(valid * field * field)

    squares = jnp.stack(
        [
            masked_square(tokens_f),
            masked_square(hidden_res),
            masked_square(summed),
            masked_square(attn_out),
            masked_square(mlp_out),
            jnp.sum(lengths).astype(jnp.float32),
        ]
    )
    grad_norm_two, _ = norm_back(hidden_res, scale_two, gain_two, grad_input_two)
    grad_hidden = grad_out + grad_norm_two
    grad_attn = grad_hidden.astype(jnp.bfloat16)
    grad_gated = matmul(grad_attn, out_full).reshape(row_count, head_count, head_width)
    grad_w_out = contract_rows(grad_attn, gated).astype(jnp.bfloat16)
    grad_attended = (grad_gated * gate_sig).astype(jnp.bfloat16)
    grad_gate_logit = (
        (grad_gated * attended * gate_sig * (1.0 - gate_sig))
        .astype(jnp.bfloat16)
        .reshape(row_count, head_count * head_width)
    )
    grad_query_rot, grad_key_rot, grad_value_heads = attend_backward(
        query_rot, key_rot, value_heads, grad_attended, log_totals, lengths
    )
    grad_values = grad_value_heads.reshape(row_count, kv_count * head_width).astype(jnp.bfloat16)
    grad_query_pre, grad_query_gain = norm_back(
        queries, query_scale, query_gain, unrotate_rows(grad_query_rot, cos_table, sin_table)
    )
    grad_key_pre, grad_key_gain = norm_back(
        keys_pre, key_scale, key_gain, unrotate_rows(grad_key_rot, cos_table, sin_table)
    )
    grad_queries = grad_query_pre.reshape(row_count, head_count * head_width).astype(jnp.bfloat16)
    grad_keys = grad_key_pre.reshape(row_count, kv_count * head_width).astype(jnp.bfloat16)
    attn_locals = [
        contract_rows(input_one, grad_queries).astype(jnp.bfloat16),
        contract_rows(input_one, grad_gate_logit).astype(jnp.bfloat16),
        contract_rows(input_one, grad_keys).astype(jnp.bfloat16),
        contract_rows(input_one, grad_values).astype(jnp.bfloat16),
        grad_w_out,
    ]
    grad_one_part = (
        contract_last(grad_queries, query_full)
        + contract_last(grad_gate_logit, gate_attn_full)
        + contract_last(grad_keys, key_full)
        + contract_last(grad_values, value_full)
    )
    gain_one_part = jnp.sum(grad_one_part * (tokens_f * scale_one), axis=0)
    grad_one_send, *attn_locals = lax.optimization_barrier(
        (grad_one_part.astype(jnp.bfloat16), *attn_locals)
    )
    grad_input_one = lax.psum(grad_one_send, "heads").astype(jnp.float32)
    attn_grads = scatter_all(attn_locals, attn_units, 3)
    once = (lax.axis_index("heads") == 0).astype(jnp.float32)
    sums = lax.psum(
        jnp.concatenate(
            [gain_one_part, gain_two_part, grad_query_gain, grad_key_gain, squares * once]
        ),
        ("heads", "batch"),
    )
    mine = lax.axis_index("batch") * shard_rows
    gain_one_grad = lax.dynamic_slice(sums, (mine,), (shard_rows,))
    gain_two_grad = lax.dynamic_slice(sums, (model_width + mine,), (shard_rows,))
    low = 2 * model_width
    query_gain_all = sums[low : low + head_width]
    key_gain_all = sums[low + head_width : low + 2 * head_width]
    squares_all = sums[low + 2 * head_width :]
    block_rms = jnp.sqrt(squares_all[:5] / (squares_all[5] * model_width))
    grad_norm_one, _ = norm_back(tokens_f, scale_one, gain_one, grad_input_one)
    grad_tokens = (grad_hidden + grad_norm_one).astype(jnp.bfloat16)
    attn_grads = [g.astype(jnp.float32) for g in attn_grads]
    mlp_grads = [g.astype(jnp.float32) for g in mlp_grads]
    return (
        output,
        grad_tokens,
        gain_one_grad,
        query_gain_all,
        key_gain_all,
        attn_grads[0],
        attn_grads[1],
        attn_grads[2],
        attn_grads[3],
        attn_grads[4],
        gain_two_grad,
        mlp_grads[0],
        mlp_grads[1],
        mlp_grads[2],
        block_rms,
    )


def solution(mesh):
    return jax.shard_map(
        local,
        mesh=mesh,
        in_specs=(
            P("batch", None),
            P("batch"),
            P("batch", None),
            P("batch"),
            P(),
            P(),
            P("batch", "heads"),
            P("batch", "heads"),
            P("batch", "heads"),
            P("batch", "heads"),
            P("batch", "heads"),
            P("batch"),
            P("batch", "heads"),
            P("batch", "heads"),
            P("batch", "heads"),
        ),
        out_specs=(
            P("batch", None),
            P("batch", None),
            P("batch"),
            P(),
            P(),
            P("batch", "heads"),
            P("batch", "heads"),
            P("batch", "heads"),
            P("batch", "heads"),
            P("batch", "heads"),
            P("batch"),
            P("batch", "heads"),
            P("batch", "heads"),
            P("batch", "heads"),
            P(),
        ),
        check_vma=False,
    )
```

```python
import functools

import jax
import jax.numpy as jnp
from jax import lax
from jax.experimental import pallas as pl
from jax.experimental.pallas import tpu as pltpu
from jax.sharding import PartitionSpec as P

SLOT_LEN = 1024
MESH = pl.DeviceIdType.MESH


NORM_EPS = 1e-06
ROPE_THETA = 1000000.0
MASKED = -1e30


def contract_rows(left_side, right_side):
    return lax.dot_general(
        left_side, right_side, (((0,), (0,)), ((), ())), preferred_element_type=jnp.float32
    )


def rotary_tables(row_count, head_width):
    half_width = head_width // 2
    positions = (lax.iota(jnp.int32, row_count) % SLOT_LEN).astype(jnp.float32)
    inverse = ROPE_THETA ** (
        -(lax.iota(jnp.int32, half_width).astype(jnp.float32) * 2.0 / head_width)
    )
    angles = positions[:, None] * inverse[None, :]
    angles = jnp.concatenate([angles, angles], axis=1)
    return (jnp.cos(angles), jnp.sin(angles))


VMEM_LIMIT = 64 * 1024 * 1024 - 65536


def grid_of(n):
    inner = 2 if n <= 8 else 4
    return (n // inner, inner)


class HeadSum:
    def __init__(self, refs):
        (self.src, self.out, self.core_in, self.mid, self.far_in,
         self.load_sem, self.core_send, self.core_recv, self.far_send, self.far_recv,
         self.back_send, self.back_recv, self.keep_sem) = refs
        head = lax.axis_index("heads")
        self.core = head % 2
        self.near = head + 1 - 2 * self.core
        self.far = (head + 2) % 4
        self.pieces, self.rows = self.mid.shape[0], self.mid.shape[1]

    def greet(self, barrier):
        for other in (self.near, self.far):
            pl.semaphore_signal(barrier, inc=1, device_id={"heads": other}, device_id_type=MESH)

    def part(self, ref, half, k):
        return ref.at[pl.ds(pl.multiple_of((half * self.pieces + k) * self.rows, self.rows), self.rows), :]

    def load(self, k):
        return pltpu.make_async_copy(self.part(self.src, self.core, k), self.mid.at[k], self.load_sem.at[k])

    def to_core(self, k):
        return pltpu.make_async_remote_copy(
            self.part(self.src, 1 - self.core, k), self.core_in.at[k], self.core_send.at[k], self.core_recv.at[k],
            device_id={"heads": self.near}, device_id_type=MESH)

    def to_far(self, k):
        return pltpu.make_async_remote_copy(
            self.mid.at[k], self.far_in.at[k], self.far_send.at[k], self.far_recv.at[k],
            device_id={"heads": self.far}, device_id_type=MESH)

    def keep(self, k):
        return pltpu.make_async_copy(self.far_in.at[k], self.part(self.out, self.core, k), self.keep_sem.at[k])

    def back(self, k):
        return pltpu.make_async_remote_copy(
            self.far_in.at[k], self.part(self.out, self.core, k), self.back_send.at[k], self.back_recv.at[k],
            device_id={"heads": self.near}, device_id_type=MESH)

    def start(self):
        for k in range(self.pieces):
            self.to_core(k).start()
            self.load(k).start()

    def add(self, target, other):
        tile = min(self.rows, 16)

        def body(t, carry):
            rows = pl.ds(pl.multiple_of(t * tile, tile), tile)
            total = target[rows, :].astype(jnp.float32) + other[rows, :].astype(jnp.float32)
            target[rows, :] = total.astype(target.dtype)
            return carry

        lax.fori_loop(0, self.rows // tile, body, 0)

    def cross(self):
        for k in range(self.pieces):
            self.load(k).wait()
            pltpu.make_async_copy(self.core_in.at[k], self.core_in.at[k], self.core_recv.at[k]).wait()
            self.add(self.mid.at[k], self.core_in.at[k])
            self.to_far(k).start()

    def settle(self):
        for k in range(self.pieces):
            pltpu.make_async_copy(self.far_in.at[k], self.far_in.at[k], self.far_recv.at[k]).wait()
            self.add(self.far_in.at[k], self.mid.at[k])
            self.keep(k).start()
            self.back(k).start()

    def finish(self):
        for k in range(self.pieces):
            other = self.part(self.out, 1 - self.core, k)
            pltpu.make_async_copy(other, other, self.back_recv.at[k]).wait()
            self.keep(k).wait()
            self.to_core(k).wait_send()
            self.to_far(k).wait_send()
            self.back(k).wait_send()


SUM_REFS = 13
SUM_PIECES = 4


def head_sum_scratch(array):
    rows, width = array.shape
    shape = (SUM_PIECES, rows // 2 // SUM_PIECES, width)
    return [pltpu.VMEM(shape, array.dtype)] * 3 + [pltpu.SemaphoreType.DMA((SUM_PIECES,))] * 8


def gather_kernel(plan, rows_n, cols_n, *refs):
    count, sums = plan["count"], plan["sums"]
    ins, sum_ins, refs = refs[:count], refs[count : count + sums], refs[count + sums :]
    outs, sum_outs, refs = refs[:count], refs[count : count + sums], refs[count + sums :]
    send_up, send_down, send_side, recv, local_sem = refs[:5]
    each = SUM_REFS - 2
    totals = [
        HeadSum((sum_ins[i], sum_outs[i]) + tuple(refs[5 + i * each : 5 + (i + 1) * each])) for i in range(sums)
    ]
    A, B = rows_n, cols_n
    me = lax.axis_index("batch")
    a, b = me // B, me % B
    units = plan["units"]

    def block(u, blk):
        i, lo, width = units[u][:3]
        ref = outs[i].at[blk]
        return ref if lo is None else ref.at[:, pl.ds(lo, width)]

    def own(u):
        i, lo, width = units[u][:3]
        return ins[i] if lo is None else ins[i].at[:, pl.ds(lo, width)]

    def put(u, src, blk, sem, target):
        pltpu.make_async_remote_copy(src, block(u, blk), sem, recv.at[u, blk], device_id={"batch": target}, device_id_type=pl.DeviceIdType.MESH).start()

    def arrived(u, blk):
        pltpu.make_async_copy(block(u, blk), block(u, blk), recv.at[u, blk]).wait()

    def sent(u, sem):
        pltpu.make_async_copy(own(u), own(u), sem).wait()

    barrier = pltpu.get_barrier_semaphore()

    def greet(target):
        pl.semaphore_signal(barrier, inc=1, device_id={"batch": target}, device_id_type=pl.DeviceIdType.MESH)

    up_ok, down_ok = a < A - 1, a > 0
    pl.when(up_ok)(lambda: greet(me + B))
    pl.when(down_ok)(lambda: greet(me - B))
    for k in range(1, B):
        greet(a * B + (b + k) % B)
    if totals:
        totals[0].greet(barrier)
    pl.semaphore_wait(barrier, up_ok.astype(jnp.int32) + down_ok.astype(jnp.int32) + (B - 1) + (2 if totals else 0))
    for total in totals:
        total.start()

    nu = len(units)

    def up(u, src, blk, slot):
        @pl.when(up_ok)
        def _():
            put(u, src, blk, send_up.at[u, slot], me + B)

    def down(u, src, blk, slot):
        @pl.when(down_ok)
        def _():
            put(u, src, blk, send_down.at[u, slot], me - B)

    def side(u, src, blk, step):
        for k in range(1, B):
            put(u, src, blk, send_side.at[u, step * (B - 1) + k - 1], a * B + (b + k) % B)

    for u in range(nu):
        up(u, own(u), me, b)
        down(u, own(u), me, b)
        side(u, own(u), me, 0)
    for i in range(count):
        pltpu.make_async_copy(ins[i], outs[i].at[me], local_sem.at[i]).start()

    for total in totals:
        total.cross()
    for u in range(nu):
        if units[u][3]:
            for k in range(1, B):
                bb = (b + k) % B
                blk = a * B + bb
                arrived(u, blk)
                up(u, block(u, blk), blk, bb)
                down(u, block(u, blk), blk, bb)
    for s in range(1, A):
        if s == A - 1:
            for total in totals:
                total.settle()
        for u in range(nu):
            first = units[u][3]

            @pl.when(a - s >= 0)
            def _(u=u, first=first):
                for k in range(B if first else 1):
                    bb = (b + k) % B
                    blk = (a - s) * B + bb
                    arrived(u, blk)
                    up(u, block(u, blk), blk, s * B + bb)
                    if not first:
                        side(u, block(u, blk), blk, 2 * s - 1)

            @pl.when(a + s < A)
            def _(u=u, first=first):
                for k in range(B if first else 1):
                    bb = (b + k) % B
                    blk = (a + s) * B + bb
                    arrived(u, blk)
                    down(u, block(u, blk), blk, s * B + bb)
                    if not first:
                        side(u, block(u, blk), blk, 2 * s)
    for total in totals:
        total.finish()
    for u in range(nu):
        if not units[u][3]:
            for s in range(A):
                for k in range(1, B):
                    bb = (b + k) % B

                    @pl.when(a - s >= 0)
                    def _(u=u, s=s, bb=bb):
                        arrived(u, (a - s) * B + bb)

                    if s:
                        @pl.when(a + s < A)
                        def _(u=u, s=s, bb=bb):
                            arrived(u, (a + s) * B + bb)
    for u in range(nu):
        first = units[u][3]
        for s in range(A):
            for k in range(B if first else 1):
                bb = (b + k) % B

                @pl.when((a - s >= 0) & up_ok)
                def _(u=u, s=s, bb=bb):
                    sent(u, send_up.at[u, s * B + bb])

                @pl.when((a + s < A) & down_ok)
                def _(u=u, s=s, bb=bb):
                    sent(u, send_down.at[u, s * B + bb])
            if s == 0 or not first:
                for k in range(1, B):
                    if s == 0:
                        sent(u, send_side.at[u, k - 1])
                    else:
                        @pl.when(a - s >= 0)
                        def _(u=u, s=s, k=k):
                            sent(u, send_side.at[u, (2 * s - 1) * (B - 1) + k - 1])

                        @pl.when(a + s < A)
                        def _(u=u, s=s, k=k):
                            sent(u, send_side.at[u, (2 * s) * (B - 1) + k - 1])
    for i in range(count):
        pltpu.make_async_copy(ins[i], outs[i].at[me], local_sem.at[i]).wait()


def gather_all(shards, plan_units, cid, sums=()):
    n = lax.axis_size("batch")
    A, B = grid_of(n)
    nu = len(plan_units)
    plan = {"count": len(shards), "units": plan_units, "sums": len(sums)}
    outs = [jax.ShapeDtypeStruct((n,) + s.shape, s.dtype) for s in shards]
    outs += [jax.ShapeDtypeStruct(s.shape, s.dtype) for s in sums]
    sum_scratch = [ref for s in sums for ref in head_sum_scratch(s)]
    res = pl.pallas_call(
        functools.partial(gather_kernel, plan, A, B),
        out_shape=outs,
        in_specs=[pl.BlockSpec(memory_space=pltpu.VMEM)] * len(shards) + [pl.BlockSpec(memory_space=pl.ANY)] * len(sums),
        out_specs=[pl.BlockSpec(memory_space=pl.ANY)] * len(outs),
        scratch_shapes=[
            pltpu.SemaphoreType.DMA((nu, A * B)),
            pltpu.SemaphoreType.DMA((nu, A * B)),
            pltpu.SemaphoreType.DMA((nu, (2 * A - 1) * (B - 1))),
            pltpu.SemaphoreType.DMA((nu, n)),
            pltpu.SemaphoreType.DMA((len(shards),)),
        ] + sum_scratch,
        compiler_params=pltpu.CompilerParams(collective_id=cid, has_side_effects=True, vmem_limit_bytes=VMEM_LIMIT),
        cost_estimate=pl.CostEstimate(flops=0, bytes_accessed=sum(s.size for s in shards) * 60, transcendentals=0),
    )(*shards, *sums)
    full = [r.reshape((n * r.shape[1],) + r.shape[2:]) if r.shape[1] > 1 else r.reshape(-1) for r in res[: len(shards)]]
    return full + list(res[len(shards) :])


TILE = 256


def nt(left_side, right_side):
    return lax.dot_general(left_side, right_side, (((1,), (1,)), ((), ())), preferred_element_type=jnp.float32)


def nn(left_side, right_side):
    return lax.dot_general(left_side, right_side, (((1,), (0,)), ((), ())), preferred_element_type=jnp.float32)


def rms_scale(value):
    return lax.rsqrt(jnp.mean(value * value, axis=-1, keepdims=True) + NORM_EPS)


def gain_row(gains, which):
    return jnp.concatenate(
        [gains[blk, which : which + 1, :].astype(jnp.float32) for blk in range(gains.shape[0])], axis=1
    )


def allowed_keys(key_count, lane_count, first_query, seq_length):
    keys = lax.broadcasted_iota(jnp.int32, (key_count, lane_count), 0)
    queries = first_query + lax.broadcasted_iota(jnp.int32, (key_count, lane_count), 1) % TILE
    return (keys <= queries) & (keys < seq_length)


def attn_forward_kernel(
    lengths, x, gain, query_gain, key_gain, cos, sin, wq, wg, wk, wv, wo,
    a1_out, qr_out, kr_out, v_out, q_out, k_out, gate_out, o_out, lse_out, part_out,
    kr_all, vt_all,
):
    step = pl.program_id(0)
    hd = query_gain.shape[1]
    heads, kv = wq.shape[1] // hd, wk.shape[1] // hd
    group = heads // kv
    xf = x[...].astype(jnp.float32)
    a1 = (xf * rms_scale(xf) * gain_row(gain, 0)).astype(jnp.bfloat16)
    a1_out[...] = a1
    k = nn(a1, wk[...])
    k_out[...] = k
    v = nn(a1, wv[...])
    v_out[...] = v.astype(jnp.bfloat16)
    q = nn(a1, wq[...])
    q_out[...] = q
    gate = nn(a1, wg[...])
    gate_out[...] = gate

    def rope(u, g):
        n = u * rms_scale(u) * g
        return (n * cos[...] + pltpu.roll(n, hd // 2, 1) * sin[...]).astype(jnp.bfloat16)

    rows = pl.ds(pl.multiple_of(step * TILE, TILE), TILE)
    for j in range(kv):
        cols = slice(j * hd, (j + 1) * hd)
        kr = rope(k[:, cols], key_gain[...])
        kr_out[:, cols] = kr
        kr_all[rows, cols] = kr
    vt_all[:, rows] = v.T.astype(jnp.bfloat16)
    qr = [rope(q[:, h * hd : (h + 1) * hd], query_gain[...]) for h in range(heads)]
    for h in range(heads):
        qr_out[:, h * hd : (h + 1) * hd] = qr[h]
    seq_length = lengths[0]
    scale = hd ** -0.5
    for i in range(SLOT_LEN // TILE):
        @pl.when(step == i)
        def _(i=i):
            count = (i + 1) * TILE
            mask = allowed_keys(count, group * TILE, i * TILE, seq_length)
            for j in range(kv):
                cols = slice(j * hd, (j + 1) * hd)
                stack = jnp.concatenate(qr[j * group : (j + 1) * group], axis=0)
                scores = jnp.where(mask, nt(kr_all[:count, cols], stack) * scale, MASKED)
                top = jnp.max(scores, axis=0, keepdims=True)
                weights = jnp.exp(scores - top)
                total = jnp.sum(weights, axis=0, keepdims=True)
                lse_out[0, j : j + 1, :] = top + jnp.log(total)
                probs = (weights * (1.0 / total)).astype(jnp.bfloat16)
                ot = nn(vt_all[cols, :count], probs)
                o = ot.T
                for g in range(group):
                    h = j * group + g
                    o_out[:, h * hd : (h + 1) * hd] = o[g * TILE : (g + 1) * TILE, :]
    og = (o_out[...] * jax.nn.sigmoid(gate)).astype(jnp.bfloat16)
    part_out[...] = nt(og, wo[...]).astype(jnp.bfloat16)


def whole(shape):
    return pl.BlockSpec(shape, lambda i: (0,) * len(shape), pipeline_mode=pl.Buffered(1))


def attn_forward(lengths, x, gain, query_gain, key_gain, cos, sin, wq, wg, wk, wv, wo):
    rows, width = x.shape
    steps = rows // TILE
    q_width, k_width = wq.shape[1], wk.shape[1]
    hd = query_gain.shape[1]
    tile = lambda w: pl.BlockSpec((TILE, w), lambda i: (i, 0))
    kv = k_width // hd
    lanes = q_width // k_width * TILE
    bf, f32 = jnp.bfloat16, jnp.float32
    shapes = [
        ((rows, width), bf), ((rows, q_width), bf), ((rows, k_width), bf), ((rows, k_width), bf),
        ((rows, q_width), f32), ((rows, k_width), f32), ((rows, q_width), f32), ((rows, q_width), f32),
        ((steps, kv, lanes), f32), ((rows, width), bf),
    ]
    out_specs = [tile(s[1]) for s, _ in shapes]
    out_specs[8] = pl.BlockSpec((1, kv, lanes), lambda i: (i, 0, 0))
    return pl.pallas_call(
        attn_forward_kernel,
        grid=(steps,),
        out_shape=[jax.ShapeDtypeStruct(*s) for s in shapes],
        in_specs=[pl.BlockSpec(memory_space=pltpu.SMEM), tile(width), whole(gain.shape), whole((1, hd)), whole((1, hd)),
                  tile(hd), tile(hd)] + [whole(w.shape) for w in (wq, wg, wk, wv, wo)],
        out_specs=out_specs,
        scratch_shapes=[pltpu.VMEM((rows, k_width), bf), pltpu.VMEM((k_width, rows), bf)],
        compiler_params=pltpu.CompilerParams(vmem_limit_bytes=60 * 1024 * 1024),
        cost_estimate=pl.CostEstimate(flops=2 * rows * width * (3 * q_width + 2 * k_width), bytes_accessed=40 << 20, transcendentals=4 << 20),
        name="attn_forward",
    )(lengths, x, gain, query_gain, key_gain, cos, sin, wq, wg, wk, wv, wo)


def mlp_forward_kernel(lengths, x, attn, cot, gain, wg, wu, a2_out, gm_out, hid_out, gu_out, up_out):
    t, c = pl.program_id(0), pl.program_id(1)
    rows = x.shape[0]

    @pl.when(c == 0)
    def _():
        h = x[...].astype(jnp.float32) + attn[...].astype(jnp.float32)
        a2_out[...] = (h * rms_scale(h) * gain_row(gain, 1)).astype(jnp.bfloat16)
        places = t * rows + lax.broadcasted_iota(jnp.int32, (rows, 1), 0)
        gm_out[...] = jnp.where(places < lengths[0], cot[...], 0.0).astype(jnp.bfloat16)

    a2 = a2_out[...]
    gu = nn(a2, wg[...])
    up = nn(a2, wu[...])
    gu_out[...] = gu.astype(jnp.bfloat16)
    up_out[...] = up.astype(jnp.bfloat16)
    hid_out[...] = (gu * jax.nn.sigmoid(gu) * up).astype(jnp.bfloat16)


def mlp_backward_kernel(
    x, attn, gm, hid, gu_in, up_in, wg, wu, wd_first, wd_last,
    ggu_out, gup_first, gup_last, part_out, ga2_out, gain_out, part_s, ga2_s,
):
    t, c = pl.program_id(0), pl.program_id(1)

    def half(wd, gup_out):
        gu, up = gu_in[...].astype(jnp.float32), up_in[...].astype(jnp.float32)
        sg = jax.nn.sigmoid(gu)
        g_hid = nn(gm[...], wd[...])
        g_gu = (g_hid * up * sg * (1.0 + gu * (1.0 - sg))).astype(jnp.bfloat16)
        g_up = (g_hid * (gu * sg)).astype(jnp.bfloat16)
        ggu_out[...] = g_gu
        gup_out[...] = g_up
        return nt(hid[...], wd[...]), nt(g_gu, wg[...]) + nt(g_up, wu[...])

    @pl.when(c == 0)
    def _():
        part_s[...], ga2_s[...] = half(wd_first, gup_first)

    @pl.when(c == 1)
    def _():
        part, ga2 = half(wd_last, gup_last)
        part_out[...] = (part_s[...] + part).astype(jnp.bfloat16)
        ga2 = ga2_s[...] + ga2
        ga2_out[...] = ga2.astype(jnp.bfloat16)
        h = x[...].astype(jnp.float32) + attn[...].astype(jnp.float32)
        mine = jnp.sum(ga2 * (h * rms_scale(h)), axis=0, keepdims=True)

        @pl.when(t == 0)
        def _():
            gain_out[...] = mine

        @pl.when(t > 0)
        def _():
            gain_out[...] += mine


def mlp_specs(width, row_tile, col_tile):
    wide = pl.BlockSpec((row_tile, width), lambda t, c: (t, 0))
    wcol = pl.BlockSpec((width, col_tile), lambda t, c: (0, c))
    narrow = pl.BlockSpec((row_tile, col_tile), lambda t, c: (t, c))
    one = pl.BlockSpec((1, width), lambda t, c: (0, 0))
    return wide, wcol, narrow, one


def mlp_forward(lengths, x, attn, cot, gain, wg, wu, row_tile=512, col_tile=512):
    rows, width = x.shape
    ff = wg.shape[1]
    wide, wcol, narrow, _ = mlp_specs(width, row_tile, col_tile)
    return pl.pallas_call(
        mlp_forward_kernel,
        grid=(rows // row_tile, ff // col_tile),
        out_shape=[jax.ShapeDtypeStruct((rows, width), jnp.bfloat16)] * 2
        + [jax.ShapeDtypeStruct((rows, ff), jnp.bfloat16)] * 3,
        in_specs=[pl.BlockSpec(memory_space=pltpu.SMEM), wide, wide, wide,
                  pl.BlockSpec(gain.shape, lambda t, c: (0, 0, 0)), wcol, wcol],
        out_specs=[wide, wide, narrow, narrow, narrow],
        compiler_params=pltpu.CompilerParams(vmem_limit_bytes=60 * 1024 * 1024),
        cost_estimate=pl.CostEstimate(flops=4 * rows * width * ff, bytes_accessed=50 << 20, transcendentals=rows * ff),
        name="mlp_forward",
    )(lengths, x, attn, cot, gain, wg, wu)


def mlp_backward(x, attn, gm, hid, gu, up, wg, wu, wd_first, wd_last, row_tile=512):
    rows, width = x.shape
    ff = wg.shape[1]
    col_tile = ff // 2
    wide, wcol, narrow, one = mlp_specs(width, row_tile, col_tile)
    alone = pl.BlockSpec((row_tile, col_tile), lambda t, c: (t, 0))
    fixed = pl.BlockSpec((width, col_tile), lambda t, c: (0, 0), pipeline_mode=pl.Buffered(1))
    bf, f32 = jnp.bfloat16, jnp.float32
    return pl.pallas_call(
        mlp_backward_kernel,
        grid=(rows // row_tile, 2),
        out_shape=[jax.ShapeDtypeStruct((rows, ff), bf)] + [jax.ShapeDtypeStruct((rows, col_tile), bf)] * 2
        + [jax.ShapeDtypeStruct((rows, width), bf)] * 2 + [jax.ShapeDtypeStruct((1, width), f32)],
        in_specs=[wide, wide, wide, narrow, narrow, narrow, wcol, wcol, fixed, fixed],
        out_specs=[narrow, alone, alone, wide, wide, one],
        scratch_shapes=[pltpu.VMEM((row_tile, width), f32), pltpu.VMEM((row_tile, width), f32)],
        compiler_params=pltpu.CompilerParams(vmem_limit_bytes=VMEM_LIMIT),
        cost_estimate=pl.CostEstimate(flops=8 * rows * width * ff, bytes_accessed=60 << 20, transcendentals=rows * ff),
        name="mlp_backward",
    )(x, attn, gm, hid, gu, up, wg, wu, wd_first, wd_last)


def attn_backward_kernel(
    lengths, g2, x, attn, mlp, cot, gain_two, query_gain, key_gain, cos, sin,
    qr, kr, v, q, k, gate, o, lse, wq, wg, wk, wv, wo,
    y_out, ghb_out, og_out, gall_out, ga1_out, gain_out, small_out,
    krt, gk, gv, gq_s,
):
    step = pl.program_id(0)
    steps = SLOT_LEN // TILE
    tile = steps - 1 - step
    hd = query_gain.shape[1]
    heads, kv = wq.shape[1] // hd, wk.shape[1] // hd
    group = heads // kv
    seq_length = lengths[0]
    scale = hd ** -0.5

    @pl.when(step == 0)
    def _():
        krt[...] = kr[...].astype(jnp.float32).T.astype(jnp.bfloat16)
        gk[...] = jnp.zeros_like(gk)
        gv[...] = jnp.zeros_like(gv)
        gain_out[...] = jnp.zeros_like(gain_out)
        small_out[...] = jnp.zeros_like(small_out)

    places = tile * TILE + lax.broadcasted_iota(jnp.int32, (TILE, 1), 0)
    live = places < seq_length
    xf = x[...].astype(jnp.float32)
    attn_f = attn[...].astype(jnp.float32)
    mlp_f = mlp[...].astype(jnp.float32)
    h = xf + attn_f
    y = h + mlp_f
    y_out[...] = jnp.where(live, y, 0.0).astype(jnp.bfloat16)
    for r, field in enumerate((xf, h, y, attn_f, mlp_f)):
        by_lane = jnp.sum(jnp.where(live, field * field, 0.0), axis=0, keepdims=True)
        folded = by_lane[:, :hd]
        for low in range(hd, by_lane.shape[1], hd):
            folded = folded + by_lane[:, low : low + hd]
        small_out[2 + r : 3 + r, :] += folded
    rho = rms_scale(h)
    n = h * rho
    gs = g2[...].astype(jnp.float32) * gain_row(gain_two, 1)
    g_out = jnp.where(live, cot[...].astype(jnp.float32), 0.0)
    ghb = (g_out + rho * (gs - n * jnp.mean(gs * n, axis=-1, keepdims=True))).astype(jnp.bfloat16)
    ghb_out[...] = ghb
    g_og = nn(ghb, wo[...])
    sig = jax.nn.sigmoid(gate[...])
    of = o[...]
    og_out[...] = (of * sig).astype(jnp.bfloat16)
    g_o = (g_og * sig).astype(jnp.bfloat16)
    q_width, k_width = heads * hd, kv * hd
    gall_out[:, q_width : 2 * q_width] = (g_og * of * sig * (1.0 - sig)).astype(jnp.bfloat16)

    for i in range(steps):
        @pl.when(tile == i)
        def _(i=i):
            count = (i + 1) * TILE
            mask = allowed_keys(count, group * TILE, i * TILE, seq_length)
            for j in range(kv):
                cols = slice(j * hd, (j + 1) * hd)
                mine = [slice((j * group + g) * hd, (j * group + g + 1) * hd) for g in range(group)]
                stack = jnp.concatenate([qr[:, s] for s in mine], axis=0)
                g_stack = jnp.concatenate([g_o[:, s] for s in mine], axis=0)
                scores = nt(kr[:count, cols], stack) * scale
                probs = jnp.where(mask, jnp.exp(jnp.where(mask, scores, MASKED) - lse[0, j : j + 1, :]), 0.0)
                g_p = nt(v[:count, cols], g_stack)
                inner = jnp.sum(probs * g_p, axis=0, keepdims=True)
                g_s = (probs * (g_p - inner)).astype(jnp.bfloat16)
                gk[:count, cols] += nn(g_s, stack) * scale
                gv[:count, cols] += nn(probs.astype(jnp.bfloat16), g_stack)
                gqt = nn(krt[cols, :count], g_s) * scale
                back = gqt.T
                for g in range(group):
                    gq_s[:, mine[g]] = back[g * TILE : (g + 1) * TILE, :]

    def unrope(g, u, gain):
        g = g * cos[...] - pltpu.roll(g, hd // 2, 1) * sin[...]
        r = rms_scale(u)
        nu = u * r
        gain_grad = jnp.sum(g * nu, axis=0, keepdims=True)
        ga = g * gain
        return r * (ga - nu * jnp.mean(ga * nu, axis=-1, keepdims=True)), gain_grad

    for head in range(heads):
        cols = slice(head * hd, (head + 1) * hd)
        g, gain_grad = unrope(gq_s[:, cols], q[:, cols], query_gain[...])
        gall_out[:, cols] = g.astype(jnp.bfloat16)
        small_out[0:1, :] += gain_grad
    rows = pl.ds(pl.multiple_of(tile * TILE, TILE), TILE)
    for j in range(kv):
        cols = slice(j * hd, (j + 1) * hd)
        g, gain_grad = unrope(gk[rows, cols], k[:, cols], key_gain[...])
        gall_out[:, 2 * q_width + j * hd : 2 * q_width + (j + 1) * hd] = g.astype(jnp.bfloat16)
        small_out[1:2, :] += gain_grad
    gall_out[:, 2 * q_width + k_width :] = gv[rows, :].astype(jnp.bfloat16)
    ga1 = (
        nt(gall_out[:, :q_width], wq[...])
        + nt(gall_out[:, q_width : 2 * q_width], wg[...])
        + nt(gall_out[:, 2 * q_width : 2 * q_width + k_width], wk[...])
        + nt(gall_out[:, 2 * q_width + k_width :], wv[...])
    )
    ga1_out[...] = ga1.astype(jnp.bfloat16)
    gain_out[...] += jnp.sum(ga1 * (xf * rms_scale(xf)), axis=0, keepdims=True)


def attn_backward(lengths, g2, x, attn, mlp, cot, gain_two, query_gain, key_gain, cos, sin,
                  qr, kr, v, q, k, gate, o, lse, wq, wg, wk, wv, wo):
    rows, width = x.shape
    steps = rows // TILE
    q_width, k_width = wq.shape[1], wk.shape[1]
    hd = query_gain.shape[1]
    tile = lambda w: pl.BlockSpec((TILE, w), lambda i: (steps - 1 - i, 0))
    bf, f32 = jnp.bfloat16, jnp.float32
    total = 2 * q_width + 2 * k_width
    return pl.pallas_call(
        attn_backward_kernel,
        grid=(steps,),
        out_shape=[
            jax.ShapeDtypeStruct((rows, width), bf), jax.ShapeDtypeStruct((rows, width), bf),
            jax.ShapeDtypeStruct((rows, q_width), bf), jax.ShapeDtypeStruct((rows, total), bf),
            jax.ShapeDtypeStruct((rows, width), bf), jax.ShapeDtypeStruct((1, width), f32),
            jax.ShapeDtypeStruct((8, hd), f32),
        ],
        in_specs=[pl.BlockSpec(memory_space=pltpu.SMEM)] + [tile(width)] * 5
        + [whole(gain_two.shape), whole((1, hd)), whole((1, hd)), tile(hd), tile(hd),
                  tile(q_width), whole((rows, k_width)), whole((rows, k_width)), tile(q_width), tile(k_width),
                  tile(q_width), tile(q_width), pl.BlockSpec((1,) + lse.shape[1:], lambda i: (steps - 1 - i, 0, 0))]
        + [whole(w.shape) for w in (wq, wg, wk, wv, wo)],
        out_specs=[tile(width), tile(width), tile(q_width), tile(total), tile(width), whole((1, width)), whole((8, hd))],
        scratch_shapes=[pltpu.VMEM((k_width, rows), bf), pltpu.VMEM((rows, k_width), f32),
                        pltpu.VMEM((rows, k_width), f32), pltpu.VMEM((TILE, q_width), f32)],
        compiler_params=pltpu.CompilerParams(vmem_limit_bytes=60 * 1024 * 1024),
        cost_estimate=pl.CostEstimate(flops=2 * rows * width * (3 * q_width + 2 * k_width) + (12 << 30), bytes_accessed=50 << 20, transcendentals=4 << 20),
        name="attn_backward",
    )(lengths, g2, x, attn, mlp, cot, gain_two, query_gain, key_gain, cos, sin,
      qr, kr, v, q, k, gate, o, lse, wq, wg, wk, wv, wo)


def finish_kernel(moves, count, x, gain, grad_hidden, grad_sum, *refs):
    ins, tokens_out, outs = refs[:count], refs[count], refs[count + 1 :]
    xf = x[...].astype(jnp.float32)
    rho = rms_scale(xf)
    n = xf * rho
    gs = grad_sum[...].astype(jnp.float32) * gain_row(gain, 0)
    back = rho * (gs - n * jnp.mean(gs * n, axis=-1, keepdims=True))
    tokens_out[...] = (grad_hidden[...].astype(jnp.float32) + back).astype(jnp.bfloat16)
    for source, low, width, target, place in moves:
        outs[target][:, place : place + width] = ins[source][:, low : low + width].astype(jnp.float32)


def finish(x, gain, grad_hidden, grad_sum, grads, moves, widths):
    rows, width = x.shape
    steps = 4
    shard = grads[0].shape[0]
    tile = pl.BlockSpec((rows // steps, width), lambda i: (i, 0))
    part = lambda w: pl.BlockSpec((shard // steps, w), lambda i: (i, 0))
    return pl.pallas_call(
        functools.partial(finish_kernel, moves, len(grads)),
        grid=(steps,),
        out_shape=[jax.ShapeDtypeStruct((rows, width), jnp.bfloat16)]
        + [jax.ShapeDtypeStruct((shard, w), jnp.float32) for w in widths],
        in_specs=[tile, whole(gain.shape), tile, tile] + [part(g.shape[1]) for g in grads],
        out_specs=[tile] + [part(w) for w in widths],
        compiler_params=pltpu.CompilerParams(vmem_limit_bytes=60 * 1024 * 1024),
        cost_estimate=pl.CostEstimate(flops=20 * rows * width, bytes_accessed=30 << 20, transcendentals=0),
        name="finish",
    )(x, gain, grad_hidden, grad_sum, *grads)


def scatter_kernel(units, sources, lefts, count, A, B, H, small_count, sums, *refs):
    nu = len(units)
    left_refs, refs = refs[:lefts], refs[lefts:]
    ins, refs = refs[:count], refs[count:]
    if H:
        pieces, refs = refs[:small_count], refs[small_count:]
    sum_ins, refs = refs[:sums], refs[sums:]
    outs, sum_outs, refs = refs[:count], refs[count : count + sums], refs[count + sums :]
    if H:
        small_out, refs = refs[0], refs[1:]
    rest = list(refs)
    each = SUM_REFS - 2
    totals = [HeadSum((sum_ins[i], sum_outs[i]) + tuple(rest[i * each : (i + 1) * each])) for i in range(sums)]
    rest = rest[sums * each :]
    if H:
        small, row_in, col_in, row_send, row_recv, col_send, col_recv = rest[-7:]
        rest = rest[:-7]
    turned, rest = rest[:lefts], rest[lefts:]
    own, side_in, up_in, down_in, stage = (rest[k * nu:(k + 1) * nu] for k in range(5))
    side_send, side_recv, up_send, up_recv, down_send, down_recv = rest[5 * nu:]
    me = lax.axis_index("batch")
    a, b = me // B, me % B
    up_ok, down_ok = a < A - 1, a > 0

    R = own[0].shape[1]

    def product(u, blk, target):
        i, lo, width, _ = units[u]
        left = turned[sources[i]][pl.ds(pl.multiple_of(blk * R, R), R), :]
        target[...] = nn(left, ins[i][:, lo : lo + width]).astype(jnp.bfloat16)

    def turn(blk):
        for left, flat in zip(left_refs, turned):
            flat[pl.ds(pl.multiple_of(blk * R, R), R), :] = left[:, pl.ds(pl.multiple_of(blk * R, R), R)].T

    barrier = pltpu.get_barrier_semaphore()

    def greet(target):
        pl.semaphore_signal(barrier, inc=1, device_id={"batch": target}, device_id_type=MESH)

    n = A * B
    if H:
        head = lax.axis_index("heads")
        for k in range(1, n):
            greet((me + k) % n)
        for k in range(1, H):
            pl.semaphore_signal(barrier, inc=1, device_id={"heads": (head + k) % H}, device_id_type=MESH)
        guests = n - 1 + H - 1
    else:
        pl.when(up_ok)(lambda: greet(me + B))
        pl.when(down_ok)(lambda: greet(me - B))
        for k in range(1, B):
            greet(a * B + (b + k) % B)
        guests = up_ok.astype(jnp.int32) + down_ok.astype(jnp.int32) + (B - 1)
        if totals:
            totals[0].greet(barrier)
            guests = guests + 2

    def at_distance(d, fn):
        if d == 0:
            return

        @pl.when(a + d < A)
        def _():
            fn(a + d, True)

        @pl.when(a - d >= 0)
        def _():
            fn(a - d, False)

    if R % 128:
        for left, flat in zip(left_refs, turned):
            for low in range(0, flat.shape[0], 256):
                flat[low : low + 256, :] = left[:, low : low + 256].T
    pl.semaphore_wait(barrier, guests)
    for total in totals:
        total.start()

    def to_heads(k):
        return pltpu.make_async_remote_copy(
            small, row_in.at[head], row_send.at[k - 1], row_recv.at[head],
            device_id={"heads": (head + k) % H}, device_id_type=MESH)

    def to_batch(k):
        return pltpu.make_async_remote_copy(
            col_in.at[me], col_in.at[me], col_send.at[k - 1], col_recv.at[me],
            device_id={"batch": (me + k) % n}, device_id_type=MESH)

    if H:
        low = 0
        for piece_ref in pieces:
            rows = piece_ref.shape[0]
            small[low : low + rows, :] = piece_ref[...]
            low += rows
        for k in range(1, H):
            to_heads(k).start()
        row_in[head] = small[...]

    for d in range(A - 1, -1, -1):
        def start(dest, _=None):
            for k in range(1, B):
                bb = (b + k) % B
                if R % 128 == 0:
                    turn(dest * B + bb)
                for u in range(nu):
                    if units[u][3]:
                        continue
                    product(u, dest * B + bb, stage[u].at[k - 1, dest])
                    pltpu.make_async_remote_copy(
                        stage[u].at[k - 1, dest], side_in[u].at[k - 1, dest], side_send.at[u, k - 1, dest],
                        side_recv.at[u, k - 1, dest], device_id={"batch": a * B + bb}, device_id_type=MESH).start()

        at_distance(d, start) if d else start(a)
        if d == A - 1:
            for total in totals:
                total.cross()
    if R % 128 == 0:
        for dest in range(A):
            turn(dest * B + b)

    def await_bytes(ref, sem):
        pltpu.make_async_copy(ref, ref, sem).wait()

    if H:
        for k in range(1, H):
            other = (head + k) % H
            await_bytes(row_in.at[other], row_recv.at[other])
        group_sum = row_in[0]
        for k in range(1, H):
            group_sum = group_sum + row_in[k]
        col_in[me] = group_sum
        for k in range(1, n):
            to_batch(k).start()

    step_rows = min(R, 32)

    def add_into(target, terms):
        def body(t, carry):
            rows = pl.ds(pl.multiple_of(t * step_rows, step_rows), step_rows)
            total = terms[0][rows, :].astype(jnp.float32)
            for term in terms[1:]:
                total = total + term[rows, :].astype(jnp.float32)
            target[rows, :] = total.astype(target.dtype)
            return carry

        lax.fori_loop(0, R // step_rows, body, 0)

    def local_terms(u, dest, bb):
        if units[u][3]:
            slot = dest * B + bb
            product(u, slot, own[u].at[slot])
            return [own[u].at[slot]], slot
        product(u, dest * B + b, own[u].at[dest])
        for k in range(1, B):
            await_bytes(side_in[u].at[k - 1, dest], side_recv.at[u, k - 1, dest])
        return [own[u].at[dest]] + [side_in[u].at[k - 1, dest] for k in range(1, B)], dest

    order = [u for u in range(nu) if units[u][3]] + [u for u in range(nu) if not units[u][3]]
    for d in range(A - 1, 0, -1):
        for u in order:
            def flow(dest, goes_up, u=u):
                for k in range(B if units[u][3] else 1):
                    terms, slot = local_terms(u, dest, (b + k) % B)
                    buf = (up_in if goes_up else down_in)[u].at[slot]
                    send, recv = (up_send, up_recv) if goes_up else (down_send, down_recv)
                    fed = down_ok if goes_up else up_ok

                    @pl.when(fed)
                    def _():
                        await_bytes(buf, recv.at[u, slot])
                        add_into(buf, [buf] + terms)

                    @pl.when(jnp.logical_not(fed))
                    def _():
                        add_into(buf, terms)

                    pltpu.make_async_remote_copy(
                        buf, buf, send.at[u, slot], recv.at[u, slot],
                        device_id={"batch": me + B if goes_up else me - B}, device_id_type=MESH).start()

            at_distance(d, flow)

    def out_piece(u):
        i, lo, width, _ = units[u]
        return outs[i].at[:, pl.ds(lo, width)]

    def arrive_home(u, bb, target):
        terms, slot = local_terms(u, a, bb)

        @pl.when(down_ok)
        def _():
            await_bytes(up_in[u].at[slot], up_recv.at[u, slot])

        @pl.when(up_ok)
        def _():
            await_bytes(down_in[u].at[slot], down_recv.at[u, slot])

        @pl.when(down_ok & up_ok)
        def _():
            add_into(target, terms + [up_in[u].at[slot], down_in[u].at[slot]])

        @pl.when(down_ok & jnp.logical_not(up_ok))
        def _():
            add_into(target, terms + [up_in[u].at[slot]])

        @pl.when(up_ok & jnp.logical_not(down_ok))
        def _():
            add_into(target, terms + [down_in[u].at[slot]])

    for total in totals:
        total.settle()
    for u in order:
        if units[u][3]:
            for k in range(1, B):
                bb = (b + k) % B
                slot = a * B + bb
                arrive_home(u, bb, own[u].at[slot])
                pltpu.make_async_remote_copy(
                    own[u].at[slot], side_in[u].at[k - 1, 0], side_send.at[u, k - 1, 0], side_recv.at[u, k - 1, 0],
                    device_id={"batch": slot}, device_id_type=MESH).start()
            arrive_home(u, b, own[u].at[a * B + b])
        else:
            arrive_home(u, b, out_piece(u))
    for u in order:
        if units[u][3]:
            for k in range(1, B):
                await_bytes(side_in[u].at[k - 1, 0], side_recv.at[u, k - 1, 0])
            add_into(out_piece(u), [own[u].at[a * B + b]] + [side_in[u].at[k - 1, 0] for k in range(1, B)])

    for total in totals:
        total.finish()
    if H:
        for k in range(1, n):
            other = (me + k) % n
            await_bytes(col_in.at[other], col_recv.at[other])
        whole_sum = col_in[0]
        for k in range(1, n):
            whole_sum = whole_sum + col_in[k]
        small_out[...] = whole_sum
        for k in range(1, H):
            to_heads(k).wait_send()
        for k in range(1, n):
            to_batch(k).wait_send()

    for u in range(nu):
        first = units[u][3]
        for k in range(1, B):
            if first:
                await_bytes(side_in[u].at[k - 1, 0], side_send.at[u, k - 1, 0])
            else:
                for dest in range(A):
                    await_bytes(side_in[u].at[k - 1, dest], side_send.at[u, k - 1, dest])
        for d in range(A - 1, 0, -1):
            def done(dest, goes_up, u=u, first=first):
                send = up_send if goes_up else down_send
                for k in range(B if first else 1):
                    slot = dest * B + k if first else dest
                    await_bytes(up_in[u].at[slot], send.at[u, slot])

            at_distance(d, done)


def scatter_all(lefts, rights, sources, units, cid, small=None, sums=(), out_dtype=jnp.bfloat16):
    n = lax.axis_size("batch")
    A, B = grid_of(n)
    nu = len(units)
    R = lefts[0].shape[1] // n

    def slots(u):
        return n if units[u][3] else A

    scratch = [ref for s in sums for ref in head_sum_scratch(s)]
    scratch += [pltpu.VMEM(left.shape[::-1], left.dtype) for left in lefts]
    scratch += [pltpu.VMEM((slots(u), R, units[u][2]), jnp.bfloat16) for u in range(nu)]
    scratch += [pltpu.VMEM((B - 1, 1 if units[u][3] else A, R, units[u][2]), jnp.bfloat16) for u in range(nu)]
    scratch += [pltpu.VMEM((slots(u), R, units[u][2]), jnp.bfloat16) for u in range(nu)]
    scratch += [pltpu.VMEM((slots(u), R, units[u][2]), jnp.bfloat16) for u in range(nu)]
    scratch += [pltpu.VMEM((B - 1, 1 if units[u][3] else A, R, units[u][2]), jnp.bfloat16) for u in range(nu)]
    dma = pltpu.SemaphoreType.DMA
    scratch += [dma((nu, B - 1, A)), dma((nu, B - 1, A)), dma((nu, n)), dma((nu, n)), dma((nu, n)), dma((nu, n))]
    H = 0
    extra, small_outs = [], []
    if small is not None:
        H = lax.axis_size("heads")
        extra = list(small)
        small_shape = (sum(e.shape[0] for e in extra), extra[0].shape[1])
        small_outs = [jax.ShapeDtypeStruct(small_shape, jnp.float32)]
        scratch += [
            pltpu.VMEM(small_shape, jnp.float32),
            pltpu.VMEM((H,) + small_shape, jnp.float32), pltpu.VMEM((n,) + small_shape, jnp.float32),
            dma((H - 1,)), dma((H,)), dma((n - 1,)), dma((n,)),
        ]
    res = pl.pallas_call(
        functools.partial(scatter_kernel, units, sources, len(lefts), len(rights), A, B, H, len(extra), len(sums)),
        out_shape=[jax.ShapeDtypeStruct((R, g.shape[1]), out_dtype) for g in rights]
        + [jax.ShapeDtypeStruct(s.shape, s.dtype) for s in sums]
        + small_outs,
        in_specs=[pl.BlockSpec(memory_space=pltpu.VMEM)] * (len(lefts) + len(rights)) + [pl.BlockSpec(memory_space=pltpu.VMEM)] * len(extra) + [pl.BlockSpec(memory_space=pl.ANY)] * len(sums),
        out_specs=[pl.BlockSpec(memory_space=pltpu.VMEM)] * len(rights) + [pl.BlockSpec(memory_space=pl.ANY)] * len(sums)
        + [pl.BlockSpec(memory_space=pltpu.VMEM)] * len(small_outs),
        scratch_shapes=scratch,
        compiler_params=pltpu.CompilerParams(collective_id=cid, has_side_effects=True, vmem_limit_bytes=VMEM_LIMIT),
        cost_estimate=pl.CostEstimate(flops=0, bytes_accessed=sum(g.size for g in rights) * 16, transcendentals=0),
    )(*lefts, *rights, *extra, *sums)
    return list(res)


def column_units(widths, side_first, chunk=512):
    units = []
    for index, width in enumerate(widths):
        for low in range(0, width, chunk):
            units.append((index, low, min(chunk, width - low), (index, low) in side_first))
    return units


def local(
    tokens,
    lengths,
    cotangent,
    attn_norm_gain,
    query_norm_gain,
    key_norm_gain,
    w_query,
    w_gate_attn,
    w_key,
    w_value,
    w_out,
    mlp_norm_gain,
    w_gate,
    w_up,
    w_down,
):
    row_count, model_width = tokens.shape
    head_width = query_norm_gain.shape[0]
    shard_rows = w_query.shape[0]
    attn_shards = [w_query, w_gate_attn, w_key, w_value, w_out]
    gain_shards = [jnp.stack([attn_norm_gain, mlp_norm_gain])]
    query_full, gate_attn_full, key_full, value_full, out_full, gains = gather_all(
        attn_shards + gain_shards,
        [(5, None, None, False)] + column_units([w.shape[1] for w in attn_shards], {(2, 0)}),
        0,
    )
    cut = w_down.shape[1] // 2
    down_first, down_last = w_down[:, :cut], w_down[:, cut:]
    down_first, query_full = lax.optimization_barrier((down_first, query_full))
    down_first = lax.all_gather(down_first, "batch", axis=0, tiled=True)
    gains = gains.reshape(-1, 2, shard_rows)
    query_gain = query_norm_gain.astype(jnp.float32).reshape(1, -1)
    key_gain = key_norm_gain.astype(jnp.float32).reshape(1, -1)
    cos_table, sin_table = rotary_tables(row_count, head_width)
    turn_sign = jnp.where(lax.iota(jnp.int32, head_width) < head_width // 2, -1.0, 1.0)
    sin_table = sin_table * turn_sign
    attn_weights = (query_full, gate_attn_full, key_full, value_full, out_full)
    input_one, query_rot, key_rot, values, queries, keys_pre, gate_logit, attended, log_totals, attn_part = attn_forward(
        lengths, tokens, gains, query_gain, key_gain, cos_table, sin_table, *attn_weights
    )
    mlp_widths = [w_gate.shape[1], w_up.shape[1]]
    gate_full, up_full, attn_sum = gather_all(
        [w_gate, w_up], column_units(mlp_widths, {(1, 0)}), 1, sums=[attn_part]
    )
    down_last, attn_sum = lax.optimization_barrier((down_last, attn_sum))
    down_last = lax.all_gather(down_last, "batch", axis=0, tiled=True)
    input_two, grad_mlp, activated, gate_pre, up_pre = mlp_forward(
        lengths, tokens, attn_sum, cotangent, gains, gate_full, up_full
    )
    grad_w_down = contract_rows(grad_mlp, activated).astype(jnp.bfloat16)
    grad_w_down, grad_mlp, activated = lax.optimization_barrier((grad_w_down, grad_mlp, activated))
    grad_down = lax.psum_scatter(grad_w_down, "batch", scatter_dimension=0, tiled=True)
    grad_gate_pre, grad_up_first, grad_up_last, mlp_part, grad_two_send, gain_two_part = mlp_backward(
        tokens, attn_sum, grad_mlp, activated, gate_pre, up_pre, gate_full, up_full, down_first, down_last
    )
    grad_w_late = contract_rows(input_two, grad_up_last).astype(jnp.bfloat16)
    input_two, grad_w_late = lax.optimization_barrier((input_two, grad_w_late))
    grad_gate, grad_up, grad_two_sum, mlp_sum = scatter_all(
        [input_two],
        [grad_gate_pre, grad_up_first],
        (0, 0),
        column_units([w_gate.shape[1], cut], {(1, 512)}),
        2,
        sums=[grad_two_send, mlp_part],
    )
    grad_two_sum, grad_w_late = lax.optimization_barrier((grad_two_sum, grad_w_late))
    grad_late = lax.psum_scatter(grad_w_late, "batch", scatter_dimension=0, tiled=True)
    output, grad_hidden, gated, grad_all, grad_one_send, gain_one_part, head_gains = attn_backward(
        lengths, grad_two_sum, tokens, attn_sum, mlp_sum, cotangent, gains, query_gain, key_gain,
        cos_table, sin_table, query_rot, key_rot, values, queries, keys_pre, gate_logit, attended, log_totals,
        *attn_weights,
    )
    counts = jnp.where(lax.iota(jnp.int32, head_width) == 0, jnp.sum(lengths), 0).astype(jnp.float32)
    once = (lax.axis_index("heads") == 0).astype(jnp.float32)
    own_sums = jnp.concatenate([head_gains[2:7], counts.reshape(1, -1)], axis=0) * once
    small = [
        gain_one_part.reshape(-1, head_width), gain_two_part.reshape(-1, head_width), head_gains[:2], own_sums,
    ]
    q_width, k_width = w_query.shape[1], w_key.shape[1]
    attn_units = [
        (0, 0, q_width, False),
        (0, q_width, q_width, False),
        (0, 2 * q_width, k_width, True),
        (0, 2 * q_width + k_width, k_width, False),
        (1, 0, q_width, False),
    ]
    grad_all_sum, grad_out_sum, grad_one_sum, sums = scatter_all(
        [input_one, grad_hidden],
        [grad_all, gated],
        (0, 1),
        attn_units,
        3,
        small,
        sums=[grad_one_send],
    )
    gain_rows = model_width // head_width
    mine = lax.axis_index("batch") * shard_rows
    gain_one_grad = lax.dynamic_slice(sums[:gain_rows].reshape(-1), (mine,), (shard_rows,))
    gain_two_grad = lax.dynamic_slice(sums[gain_rows : 2 * gain_rows].reshape(-1), (mine,), (shard_rows,))
    query_gain_all = sums[2 * gain_rows]
    key_gain_all = sums[2 * gain_rows + 1]
    squares_all = jnp.sum(sums[2 * gain_rows + 2 :], axis=1)
    block_rms = jnp.sqrt(squares_all[:5] / (squares_all[5] * model_width))
    widths = [w.shape[1] for w in attn_shards] + [w_gate.shape[1], w_up.shape[1], w_down.shape[1]]
    moves, low = [], 0
    for index in range(4):
        moves.append((0, low, widths[index], index, 0))
        low += widths[index]
    moves += [
        (1, 0, widths[4], 4, 0),
        (2, 0, widths[5], 5, 0),
        (3, 0, cut, 6, 0),
        (4, 0, widths[6] - cut, 6, cut),
        (5, 0, widths[7], 7, 0),
    ]
    grad_tokens, *weight_grads = finish(
        tokens, gains, grad_hidden, grad_one_sum,
        [grad_all_sum, grad_out_sum, grad_gate, grad_up, grad_late, grad_down], moves, widths,
    )
    return (
        output,
        grad_tokens,
        gain_one_grad,
        query_gain_all,
        key_gain_all,
        *weight_grads[:5],
        gain_two_grad,
        *weight_grads[5:],
        block_rms,
    )


def solution(mesh):
    return jax.shard_map(
        local,
        mesh=mesh,
        in_specs=(
            P("batch", None),
            P("batch"),
            P("batch", None),
            P("batch"),
            P(),
            P(),
            P("batch", "heads"),
            P("batch", "heads"),
            P("batch", "heads"),
            P("batch", "heads"),
            P("batch", "heads"),
            P("batch"),
            P("batch", "heads"),
            P("batch", "heads"),
            P("batch", "heads"),
        ),
        out_specs=(
            P("batch", None),
            P("batch", None),
            P("batch"),
            P(),
            P(),
            P("batch", "heads"),
            P("batch", "heads"),
            P("batch", "heads"),
            P("batch", "heads"),
            P("batch", "heads"),
            P("batch"),
            P("batch", "heads"),
            P("batch", "heads"),
            P("batch", "heads"),
            P(),
        ),
        check_vma=False,
    )
```

```python
import functools
import math

import jax
import jax.numpy as jnp
from jax import lax
from jax.experimental import pallas as pl
from jax.experimental.pallas import tpu as pltpu
from jax.sharding import PartitionSpec as P

SLOT_LEN = 1024
MESH = pl.DeviceIdType.MESH


NORM_EPS = 1e-06
ROPE_THETA = 1000000.0
MASKED = -1e30


def contract_rows(left_side, right_side):
    return lax.dot_general(
        left_side, right_side, (((0,), (0,)), ((), ())), preferred_element_type=jnp.float32
    )


VMEM_LIMIT = 64 * 1024 * 1024 - 65536


def grid_of(n):
    inner = 2 if n <= 8 else 4
    return (n // inner, inner)


class HeadSum:
    def __init__(self, refs):
        (self.src, self.out, self.core_in, self.mid, self.far_in,
         self.load_sem, self.core_send, self.core_recv, self.far_send, self.far_recv,
         self.back_send, self.back_recv, self.keep_sem) = refs
        head = lax.axis_index("heads")
        self.core = head % 2
        self.near = head + 1 - 2 * self.core
        self.far = (head + 2) % 4
        self.pieces, self.rows = self.mid.shape[0], self.mid.shape[1]

    def greet(self, barrier):
        for other in (self.near, self.far):
            pl.semaphore_signal(barrier, inc=1, device_id={"heads": other}, device_id_type=MESH)

    def part(self, ref, half, k):
        return ref.at[pl.ds(pl.multiple_of((half * self.pieces + k) * self.rows, self.rows), self.rows), :]

    def load(self, k):
        return pltpu.make_async_copy(self.part(self.src, self.core, k), self.mid.at[k], self.load_sem.at[k])

    def to_core(self, k):
        return pltpu.make_async_remote_copy(
            self.part(self.src, 1 - self.core, k), self.core_in.at[k], self.core_send.at[k], self.core_recv.at[k],
            device_id={"heads": self.near}, device_id_type=MESH)

    def to_far(self, k):
        return pltpu.make_async_remote_copy(
            self.mid.at[k], self.far_in.at[k], self.far_send.at[k], self.far_recv.at[k],
            device_id={"heads": self.far}, device_id_type=MESH)

    def keep(self, k):
        return pltpu.make_async_copy(self.far_in.at[k], self.part(self.out, self.core, k), self.keep_sem.at[k])

    def back(self, k):
        return pltpu.make_async_remote_copy(
            self.far_in.at[k], self.part(self.out, self.core, k), self.back_send.at[k], self.back_recv.at[k],
            device_id={"heads": self.near}, device_id_type=MESH)

    def start(self):
        for k in range(self.pieces):
            self.to_core(k).start()
            self.load(k).start()

    def add(self, target, other):
        tile = min(self.rows, 16)

        def body(t, carry):
            rows = pl.ds(pl.multiple_of(t * tile, tile), tile)
            total = target[rows, :].astype(jnp.float32) + other[rows, :].astype(jnp.float32)
            target[rows, :] = total.astype(target.dtype)
            return carry

        lax.fori_loop(0, self.rows // tile, body, 0)

    def cross(self):
        for k in range(self.pieces):
            self.load(k).wait()
            pltpu.make_async_copy(self.core_in.at[k], self.core_in.at[k], self.core_recv.at[k]).wait()
            self.add(self.mid.at[k], self.core_in.at[k])
            self.to_far(k).start()

    def settle(self):
        for k in range(self.pieces):
            pltpu.make_async_copy(self.far_in.at[k], self.far_in.at[k], self.far_recv.at[k]).wait()
            self.add(self.far_in.at[k], self.mid.at[k])
            self.keep(k).start()
            self.back(k).start()

    def finish(self):
        for k in range(self.pieces):
            other = self.part(self.out, 1 - self.core, k)
            pltpu.make_async_copy(other, other, self.back_recv.at[k]).wait()
            self.keep(k).wait()
            self.to_core(k).wait_send()
            self.to_far(k).wait_send()
            self.back(k).wait_send()


SUM_REFS = 13
SUM_PIECES = 4


def head_sum_scratch(array):
    rows, width = array.shape
    shape = (SUM_PIECES, rows // 2 // SUM_PIECES, width)
    return [pltpu.VMEM(shape, array.dtype)] * 3 + [pltpu.SemaphoreType.DMA((SUM_PIECES,))] * 8


def gather_kernel(plan, rows_n, cols_n, *refs):
    count, sums = plan["count"], plan["sums"]
    ins, sum_ins, refs = refs[:count], refs[count : count + sums], refs[count + sums :]
    outs, sum_outs, refs = refs[:count], refs[count : count + sums], refs[count + sums :]
    if plan["tables"]:
        cos_out, sin_out, refs = refs[0], refs[1], refs[2:]
    send_up, send_down, send_side, recv, local_sem = refs[:5]
    each = SUM_REFS - 2
    totals = [
        HeadSum((sum_ins[i], sum_outs[i]) + tuple(refs[5 + i * each : 5 + (i + 1) * each])) for i in range(sums)
    ]
    A, B = rows_n, cols_n
    me = lax.axis_index("batch")
    a, b = me // B, me % B
    units = plan["units"]

    def block(u, blk):
        i, lo, width = units[u][:3]
        ref = outs[i].at[blk]
        return ref if lo is None else ref.at[:, pl.ds(lo, width)]

    def own(u):
        i, lo, width = units[u][:3]
        return ins[i] if lo is None else ins[i].at[:, pl.ds(lo, width)]

    def put(u, src, blk, sem, target):
        pltpu.make_async_remote_copy(src, block(u, blk), sem, recv.at[u, blk], device_id={"batch": target}, device_id_type=pl.DeviceIdType.MESH).start()

    def arrived(u, blk):
        pltpu.make_async_copy(block(u, blk), block(u, blk), recv.at[u, blk]).wait()

    def sent(u, sem):
        pltpu.make_async_copy(own(u), own(u), sem).wait()

    barrier = pltpu.get_barrier_semaphore()

    def greet(target):
        pl.semaphore_signal(barrier, inc=1, device_id={"batch": target}, device_id_type=pl.DeviceIdType.MESH)

    up_ok, down_ok = a < A - 1, a > 0
    pl.when(up_ok)(lambda: greet(me + B))
    pl.when(down_ok)(lambda: greet(me - B))
    for k in range(1, B):
        greet(a * B + (b + k) % B)
    if totals:
        totals[0].greet(barrier)
    pl.semaphore_wait(barrier, up_ok.astype(jnp.int32) + down_ok.astype(jnp.int32) + (B - 1) + (2 if totals else 0))
    for total in totals:
        total.start()

    nu = len(units)

    def up(u, src, blk, slot):
        @pl.when(up_ok)
        def _():
            put(u, src, blk, send_up.at[u, slot], me + B)

    def down(u, src, blk, slot):
        @pl.when(down_ok)
        def _():
            put(u, src, blk, send_down.at[u, slot], me - B)

    def side(u, src, blk, step):
        for k in range(1, B):
            put(u, src, blk, send_side.at[u, step * (B - 1) + k - 1], a * B + (b + k) % B)

    for u in range(nu):
        up(u, own(u), me, b)
        down(u, own(u), me, b)
        side(u, own(u), me, 0)
    for i in range(count):
        pltpu.make_async_copy(ins[i], outs[i].at[me], local_sem.at[i]).start()

    for total in totals:
        total.cross()
    for u in range(nu):
        if units[u][3]:
            for k in range(1, B):
                bb = (b + k) % B
                blk = a * B + bb
                arrived(u, blk)
                up(u, block(u, blk), blk, bb)
                down(u, block(u, blk), blk, bb)
    for s in range(1, A):
        if s == A - 1:
            for total in totals:
                total.settle()
        for u in range(nu):
            first = units[u][3]

            @pl.when(a - s >= 0)
            def _(u=u, first=first):
                for k in range(B if first else 1):
                    bb = (b + k) % B
                    blk = (a - s) * B + bb
                    arrived(u, blk)
                    up(u, block(u, blk), blk, s * B + bb)
                    if not first:
                        side(u, block(u, blk), blk, 2 * s - 1)

            @pl.when(a + s < A)
            def _(u=u, first=first):
                for k in range(B if first else 1):
                    bb = (b + k) % B
                    blk = (a + s) * B + bb
                    arrived(u, blk)
                    down(u, block(u, blk), blk, s * B + bb)
                    if not first:
                        side(u, block(u, blk), blk, 2 * s)
    for total in totals:
        total.finish()
    if plan["tables"]:
        rows, width = cos_out.shape
        tile = min(rows, 128)
        lane = lax.broadcasted_iota(jnp.int32, (1, width), 1)
        column = (lane % (width // 2)).astype(jnp.float32)
        inverse = jnp.exp(column * (-2.0 * math.log(ROPE_THETA) / width))
        sign = jnp.where(lane < width // 2, -1.0, 1.0)

        def fill(t, carry):
            first = pl.multiple_of(t * tile, tile)
            place = (first + lax.broadcasted_iota(jnp.int32, (tile, 1), 0)) % SLOT_LEN
            angles = place.astype(jnp.float32) * inverse
            cos_out[pl.ds(first, tile), :] = jnp.cos(angles)
            sin_out[pl.ds(first, tile), :] = jnp.sin(angles) * sign
            return carry

        lax.fori_loop(0, rows // tile, fill, 0)
    for u in range(nu):
        if not units[u][3]:
            for s in range(A):
                for k in range(1, B):
                    bb = (b + k) % B

                    @pl.when(a - s >= 0)
                    def _(u=u, s=s, bb=bb):
                        arrived(u, (a - s) * B + bb)

                    if s:
                        @pl.when(a + s < A)
                        def _(u=u, s=s, bb=bb):
                            arrived(u, (a + s) * B + bb)
    for u in range(nu):
        first = units[u][3]
        for s in range(A):
            for k in range(B if first else 1):
                bb = (b + k) % B

                @pl.when((a - s >= 0) & up_ok)
                def _(u=u, s=s, bb=bb):
                    sent(u, send_up.at[u, s * B + bb])

                @pl.when((a + s < A) & down_ok)
                def _(u=u, s=s, bb=bb):
                    sent(u, send_down.at[u, s * B + bb])
            if s == 0 or not first:
                for k in range(1, B):
                    if s == 0:
                        sent(u, send_side.at[u, k - 1])
                    else:
                        @pl.when(a - s >= 0)
                        def _(u=u, s=s, k=k):
                            sent(u, send_side.at[u, (2 * s - 1) * (B - 1) + k - 1])

                        @pl.when(a + s < A)
                        def _(u=u, s=s, k=k):
                            sent(u, send_side.at[u, (2 * s) * (B - 1) + k - 1])
    for i in range(count):
        pltpu.make_async_copy(ins[i], outs[i].at[me], local_sem.at[i]).wait()


def gather_all(shards, plan_units, cid, sums=(), tables=None):
    n = lax.axis_size("batch")
    A, B = grid_of(n)
    nu = len(plan_units)
    plan = {"count": len(shards), "units": plan_units, "sums": len(sums), "tables": tables is not None}
    outs = [jax.ShapeDtypeStruct((n,) + s.shape, s.dtype) for s in shards]
    outs += [jax.ShapeDtypeStruct(s.shape, s.dtype) for s in sums]
    table_outs = [jax.ShapeDtypeStruct(tables, jnp.float32)] * 2 if tables else []
    sum_scratch = [ref for s in sums for ref in head_sum_scratch(s)]
    res = pl.pallas_call(
        functools.partial(gather_kernel, plan, A, B),
        out_shape=outs + table_outs,
        in_specs=[pl.BlockSpec(memory_space=pltpu.VMEM)] * len(shards) + [pl.BlockSpec(memory_space=pl.ANY)] * len(sums),
        out_specs=[pl.BlockSpec(memory_space=pl.ANY)] * len(outs) + [pl.BlockSpec(memory_space=pltpu.VMEM)] * len(table_outs),
        scratch_shapes=[
            pltpu.SemaphoreType.DMA((nu, A * B)),
            pltpu.SemaphoreType.DMA((nu, A * B)),
            pltpu.SemaphoreType.DMA((nu, (2 * A - 1) * (B - 1))),
            pltpu.SemaphoreType.DMA((nu, n)),
            pltpu.SemaphoreType.DMA((len(shards),)),
        ] + sum_scratch,
        compiler_params=pltpu.CompilerParams(collective_id=cid, has_side_effects=True, vmem_limit_bytes=VMEM_LIMIT),
        cost_estimate=pl.CostEstimate(flops=0, bytes_accessed=sum(s.size for s in shards) * 60, transcendentals=0),
    )(*shards, *sums)
    full = [r.reshape((n * r.shape[1],) + r.shape[2:]) if r.shape[1] > 1 else r.reshape(-1) for r in res[: len(shards)]]
    return full + list(res[len(shards) :])


TILE = 256


def nt(left_side, right_side):
    return lax.dot_general(left_side, right_side, (((1,), (1,)), ((), ())), preferred_element_type=jnp.float32)


def nn(left_side, right_side):
    return lax.dot_general(left_side, right_side, (((1,), (0,)), ((), ())), preferred_element_type=jnp.float32)


def rms_scale(value):
    return lax.rsqrt(jnp.mean(value * value, axis=-1, keepdims=True) + NORM_EPS)


def gain_row(gains, which):
    return jnp.concatenate(
        [gains[blk, which : which + 1, :].astype(jnp.float32) for blk in range(gains.shape[0])], axis=1
    )


def allowed_keys(key_count, lane_count, first_query, seq_length):
    keys = lax.broadcasted_iota(jnp.int32, (key_count, lane_count), 0)
    queries = first_query + lax.broadcasted_iota(jnp.int32, (key_count, lane_count), 1) % TILE
    return (keys <= queries) & (keys < seq_length)


def attn_forward_kernel(
    lengths, x, gain, query_gain, key_gain, cos, sin, wq, wg, wk, wv, wo,
    a1_out, qr_out, kr_out, v_out, q_out, k_out, gate_out, o_out, lse_out, part_out,
    kr_all, vt_all,
):
    step = pl.program_id(0)
    hd = query_gain.shape[1]
    heads, kv = wq.shape[1] // hd, wk.shape[1] // hd
    group = heads // kv
    xf = x[...].astype(jnp.float32)
    a1 = (xf * rms_scale(xf) * gain_row(gain, 0)).astype(jnp.bfloat16)
    a1_out[...] = a1
    k = nn(a1, wk[...])
    k_out[...] = k
    v = nn(a1, wv[...])
    v_out[...] = v.astype(jnp.bfloat16)
    q = nn(a1, wq[...])
    q_out[...] = q
    gate = nn(a1, wg[...])
    gate_out[...] = gate

    def rope(u, g):
        n = u * rms_scale(u) * g[...].astype(jnp.float32)
        return (n * cos[...] + pltpu.roll(n, hd // 2, 1) * sin[...]).astype(jnp.bfloat16)

    rows = pl.ds(pl.multiple_of(step * TILE, TILE), TILE)
    for j in range(kv):
        cols = slice(j * hd, (j + 1) * hd)
        kr = rope(k[:, cols], key_gain)
        kr_out[:, cols] = kr
        kr_all[rows, cols] = kr
    vt_all[:, rows] = v.T.astype(jnp.bfloat16)
    qr = [rope(q[:, h * hd : (h + 1) * hd], query_gain) for h in range(heads)]
    for h in range(heads):
        qr_out[:, h * hd : (h + 1) * hd] = qr[h]
    seq_length = lengths[0]
    scale = hd ** -0.5
    for i in range(SLOT_LEN // TILE):
        @pl.when(step == i)
        def _(i=i):
            count = (i + 1) * TILE
            mask = allowed_keys(count, group * TILE, i * TILE, seq_length)
            for j in range(kv):
                cols = slice(j * hd, (j + 1) * hd)
                stack = jnp.concatenate(qr[j * group : (j + 1) * group], axis=0)
                scores = jnp.where(mask, nt(kr_all[:count, cols], stack) * scale, MASKED)
                top = jnp.max(scores, axis=0, keepdims=True)
                weights = jnp.exp(scores - top)
                total = jnp.sum(weights, axis=0, keepdims=True)
                lse_out[0, j : j + 1, :] = top + jnp.log(total)
                probs = (weights * (1.0 / total)).astype(jnp.bfloat16)
                ot = nn(vt_all[cols, :count], probs)
                o = ot.T
                for g in range(group):
                    h = j * group + g
                    o_out[:, h * hd : (h + 1) * hd] = o[g * TILE : (g + 1) * TILE, :]
    og = (o_out[...] * jax.nn.sigmoid(gate)).astype(jnp.bfloat16)
    part_out[...] = nt(og, wo[...]).astype(jnp.bfloat16)


def whole(shape):
    return pl.BlockSpec(shape, lambda i: (0,) * len(shape), pipeline_mode=pl.Buffered(1))


def attn_forward(lengths, x, gain, query_gain, key_gain, cos, sin, wq, wg, wk, wv, wo):
    rows, width = x.shape
    steps = rows // TILE
    q_width, k_width = wq.shape[1], wk.shape[1]
    hd = query_gain.shape[1]
    tile = lambda w: pl.BlockSpec((TILE, w), lambda i: (i, 0))
    kv = k_width // hd
    lanes = q_width // k_width * TILE
    bf, f32 = jnp.bfloat16, jnp.float32
    shapes = [
        ((rows, width), bf), ((rows, q_width), bf), ((rows, k_width), bf), ((rows, k_width), bf),
        ((rows, q_width), f32), ((rows, k_width), f32), ((rows, q_width), f32), ((rows, q_width), f32),
        ((steps, kv, lanes), f32), ((rows, width), bf),
    ]
    out_specs = [tile(s[1]) for s, _ in shapes]
    out_specs[8] = pl.BlockSpec((1, kv, lanes), lambda i: (i, 0, 0))
    return pl.pallas_call(
        attn_forward_kernel,
        grid=(steps,),
        out_shape=[jax.ShapeDtypeStruct(*s) for s in shapes],
        in_specs=[pl.BlockSpec(memory_space=pltpu.SMEM), tile(width), whole(gain.shape), whole((1, hd)), whole((1, hd)),
                  tile(hd), tile(hd)] + [whole(w.shape) for w in (wq, wg, wk, wv, wo)],
        out_specs=out_specs,
        scratch_shapes=[pltpu.VMEM((rows, k_width), bf), pltpu.VMEM((k_width, rows), bf)],
        compiler_params=pltpu.CompilerParams(vmem_limit_bytes=60 * 1024 * 1024),
        cost_estimate=pl.CostEstimate(flops=2 * rows * width * (3 * q_width + 2 * k_width), bytes_accessed=40 << 20, transcendentals=4 << 20),
        name="attn_forward",
    )(lengths, x, gain, query_gain, key_gain, cos, sin, wq, wg, wk, wv, wo)


def mlp_forward_kernel(lengths, x, attn, cot, gain, wg, wu, a2_out, gm_out, hid_out, gu_out, up_out):
    t, c = pl.program_id(0), pl.program_id(1)
    rows = x.shape[0]

    @pl.when(c == 0)
    def _():
        h = x[...].astype(jnp.float32) + attn[...].astype(jnp.float32)
        a2_out[...] = (h * rms_scale(h) * gain_row(gain, 1)).astype(jnp.bfloat16)
        places = t * rows + lax.broadcasted_iota(jnp.int32, (rows, 1), 0)
        gm_out[...] = jnp.where(places < lengths[0], cot[...], 0.0).astype(jnp.bfloat16)

    a2 = a2_out[...]
    gu = nn(a2, wg[...])
    up = nn(a2, wu[...])
    gu_out[...] = gu.astype(jnp.bfloat16)
    up_out[...] = up.astype(jnp.bfloat16)
    hid_out[...] = (gu * jax.nn.sigmoid(gu) * up).astype(jnp.bfloat16)


def mlp_backward_kernel(
    x, attn, gm, hid, gu_in, up_in, wg, wu, wd_first, wd_last,
    ggu_out, gup_first, gup_last, part_out, ga2_out, gain_out, part_s, ga2_s,
):
    t, c = pl.program_id(0), pl.program_id(1)

    def half(wd, gup_out):
        gu, up = gu_in[...].astype(jnp.float32), up_in[...].astype(jnp.float32)
        sg = jax.nn.sigmoid(gu)
        g_hid = nn(gm[...], wd[...])
        g_gu = (g_hid * up * sg * (1.0 + gu * (1.0 - sg))).astype(jnp.bfloat16)
        g_up = (g_hid * (gu * sg)).astype(jnp.bfloat16)
        ggu_out[...] = g_gu
        gup_out[...] = g_up
        return nt(hid[...], wd[...]), nt(g_gu, wg[...]) + nt(g_up, wu[...])

    @pl.when(c == 0)
    def _():
        part_s[...], ga2_s[...] = half(wd_first, gup_first)

    @pl.when(c == 1)
    def _():
        part, ga2 = half(wd_last, gup_last)
        part_out[...] = (part_s[...] + part).astype(jnp.bfloat16)
        ga2 = ga2_s[...] + ga2
        ga2_out[...] = ga2.astype(jnp.bfloat16)
        h = x[...].astype(jnp.float32) + attn[...].astype(jnp.float32)
        mine = jnp.sum(ga2 * (h * rms_scale(h)), axis=0, keepdims=True)

        @pl.when(t == 0)
        def _():
            gain_out[...] = mine

        @pl.when(t > 0)
        def _():
            gain_out[...] += mine


def mlp_specs(width, row_tile, col_tile):
    wide = pl.BlockSpec((row_tile, width), lambda t, c: (t, 0))
    wcol = pl.BlockSpec((width, col_tile), lambda t, c: (0, c))
    narrow = pl.BlockSpec((row_tile, col_tile), lambda t, c: (t, c))
    one = pl.BlockSpec((1, width), lambda t, c: (0, 0))
    return wide, wcol, narrow, one


def mlp_forward(lengths, x, attn, cot, gain, wg, wu, row_tile=512, col_tile=512):
    rows, width = x.shape
    ff = wg.shape[1]
    wide, wcol, narrow, _ = mlp_specs(width, row_tile, col_tile)
    return pl.pallas_call(
        mlp_forward_kernel,
        grid=(rows // row_tile, ff // col_tile),
        out_shape=[jax.ShapeDtypeStruct((rows, width), jnp.bfloat16)] * 2
        + [jax.ShapeDtypeStruct((rows, ff), jnp.bfloat16)] * 3,
        in_specs=[pl.BlockSpec(memory_space=pltpu.SMEM), wide, wide, wide,
                  pl.BlockSpec(gain.shape, lambda t, c: (0, 0, 0)), wcol, wcol],
        out_specs=[wide, wide, narrow, narrow, narrow],
        compiler_params=pltpu.CompilerParams(vmem_limit_bytes=60 * 1024 * 1024),
        cost_estimate=pl.CostEstimate(flops=4 * rows * width * ff, bytes_accessed=50 << 20, transcendentals=rows * ff),
        name="mlp_forward",
    )(lengths, x, attn, cot, gain, wg, wu)


def mlp_backward(x, attn, gm, hid, gu, up, wg, wu, wd_first, wd_last, row_tile=512):
    rows, width = x.shape
    ff = wg.shape[1]
    col_tile = ff // 2
    wide, wcol, narrow, one = mlp_specs(width, row_tile, col_tile)
    alone = pl.BlockSpec((row_tile, col_tile), lambda t, c: (t, 0))
    fixed = pl.BlockSpec((width, col_tile), lambda t, c: (0, 0), pipeline_mode=pl.Buffered(1))
    bf, f32 = jnp.bfloat16, jnp.float32
    return pl.pallas_call(
        mlp_backward_kernel,
        grid=(rows // row_tile, 2),
        out_shape=[jax.ShapeDtypeStruct((rows, ff), bf)] + [jax.ShapeDtypeStruct((rows, col_tile), bf)] * 2
        + [jax.ShapeDtypeStruct((rows, width), bf)] * 2 + [jax.ShapeDtypeStruct((1, width), f32)],
        in_specs=[wide, wide, wide, narrow, narrow, narrow, wcol, wcol, fixed, fixed],
        out_specs=[narrow, alone, alone, wide, wide, one],
        scratch_shapes=[pltpu.VMEM((row_tile, width), f32), pltpu.VMEM((row_tile, width), f32)],
        compiler_params=pltpu.CompilerParams(vmem_limit_bytes=VMEM_LIMIT),
        cost_estimate=pl.CostEstimate(flops=8 * rows * width * ff, bytes_accessed=60 << 20, transcendentals=rows * ff),
        name="mlp_backward",
    )(x, attn, gm, hid, gu, up, wg, wu, wd_first, wd_last)


def attn_backward_kernel(
    lengths, g2, x, attn, mlp, cot, gain_two, query_gain, key_gain, cos, sin,
    qr, kr, v, q, k, gate, o, lse, wq, wg, wk, wv, wo,
    y_out, ghb_out, og_out, gall_out, ga1_out, gain_out, small_out, square_out,
    krt, gk, gv, gq_s,
):
    step = pl.program_id(0)
    steps = SLOT_LEN // TILE
    tile = steps - 1 - step
    hd = query_gain.shape[1]
    heads, kv = wq.shape[1] // hd, wk.shape[1] // hd
    group = heads // kv
    seq_length = lengths[0]
    scale = hd ** -0.5

    @pl.when(step == 0)
    def _():
        krt[...] = kr[...].astype(jnp.float32).T.astype(jnp.bfloat16)
        gk[...] = jnp.zeros_like(gk)
        gv[...] = jnp.zeros_like(gv)
        gain_out[...] = jnp.zeros_like(gain_out)
        small_out[...] = jnp.zeros_like(small_out)
        square_out[...] = jnp.zeros_like(square_out)

    places = tile * TILE + lax.broadcasted_iota(jnp.int32, (TILE, 1), 0)
    live = places < seq_length
    xf = x[...].astype(jnp.float32)
    attn_f = attn[...].astype(jnp.float32)
    mlp_f = mlp[...].astype(jnp.float32)
    h = xf + attn_f
    y = h + mlp_f
    y_out[...] = jnp.where(live, y, 0.0).astype(jnp.bfloat16)
    first_lane = (lax.broadcasted_iota(jnp.int32, (1, hd), 1) == 0).astype(jnp.float32)
    width = float(xf.shape[1])
    mean_x = jnp.mean(xf * xf, axis=-1, keepdims=True)
    mean_h = jnp.mean(h * h, axis=-1, keepdims=True)
    for r, mean in ((0, mean_x), (1, mean_h)):
        square_out[r : r + 1, :] += jnp.sum(jnp.where(live, mean, 0.0), axis=0, keepdims=True) * width * first_lane
    for r, field in ((2, y), (3, attn_f), (4, mlp_f)):
        by_lane = jnp.sum(jnp.where(live, field * field, 0.0), axis=0, keepdims=True)
        folded = by_lane[:, :hd]
        for low in range(hd, by_lane.shape[1], hd):
            folded = folded + by_lane[:, low : low + hd]
        square_out[r : r + 1, :] += folded
    square_out[5:6, :] += jnp.sum(live.astype(jnp.float32), axis=0, keepdims=True) * first_lane
    rho = lax.rsqrt(mean_h + NORM_EPS)
    n = h * rho
    gs = g2[...].astype(jnp.float32) * gain_row(gain_two, 1)
    g_out = jnp.where(live, cot[...].astype(jnp.float32), 0.0)
    ghb = (g_out + rho * (gs - n * jnp.mean(gs * n, axis=-1, keepdims=True))).astype(jnp.bfloat16)
    ghb_out[...] = ghb
    g_og = nn(ghb, wo[...])
    sig = jax.nn.sigmoid(gate[...])
    of = o[...]
    og_out[...] = (of * sig).astype(jnp.bfloat16)
    g_o = (g_og * sig).astype(jnp.bfloat16)
    q_width, k_width = heads * hd, kv * hd
    gall_out[:, q_width : 2 * q_width] = (g_og * of * sig * (1.0 - sig)).astype(jnp.bfloat16)

    for i in range(steps):
        @pl.when(tile == i)
        def _(i=i):
            count = (i + 1) * TILE
            mask = allowed_keys(count, group * TILE, i * TILE, seq_length)
            for j in range(kv):
                cols = slice(j * hd, (j + 1) * hd)
                mine = [slice((j * group + g) * hd, (j * group + g + 1) * hd) for g in range(group)]
                stack = jnp.concatenate([qr[:, s] for s in mine], axis=0)
                g_stack = jnp.concatenate([g_o[:, s] for s in mine], axis=0)
                scores = nt(kr[:count, cols], stack) * scale
                probs = jnp.where(mask, jnp.exp(jnp.where(mask, scores, MASKED) - lse[0, j : j + 1, :]), 0.0)
                g_p = nt(v[:count, cols], g_stack)
                inner = jnp.sum(probs * g_p, axis=0, keepdims=True)
                g_s = (probs * (g_p - inner)).astype(jnp.bfloat16)
                gk[:count, cols] += nn(g_s, stack) * scale
                gv[:count, cols] += nn(probs.astype(jnp.bfloat16), g_stack)
                gqt = nn(krt[cols, :count], g_s) * scale
                back = gqt.T
                for g in range(group):
                    gq_s[:, mine[g]] = back[g * TILE : (g + 1) * TILE, :]

    def unrope(g, u, gain):
        g = g * cos[...] - pltpu.roll(g, hd // 2, 1) * sin[...]
        r = rms_scale(u)
        nu = u * r
        gain_grad = jnp.sum(g * nu, axis=0, keepdims=True)
        ga = g * gain[...].astype(jnp.float32)
        return r * (ga - nu * jnp.mean(ga * nu, axis=-1, keepdims=True)), gain_grad

    for head in range(heads):
        cols = slice(head * hd, (head + 1) * hd)
        g, gain_grad = unrope(gq_s[:, cols], q[:, cols], query_gain)
        gall_out[:, cols] = g.astype(jnp.bfloat16)
        small_out[0:1, :] += gain_grad
    rows = pl.ds(pl.multiple_of(tile * TILE, TILE), TILE)
    for j in range(kv):
        cols = slice(j * hd, (j + 1) * hd)
        g, gain_grad = unrope(gk[rows, cols], k[:, cols], key_gain)
        gall_out[:, 2 * q_width + j * hd : 2 * q_width + (j + 1) * hd] = g.astype(jnp.bfloat16)
        small_out[1:2, :] += gain_grad
    gall_out[:, 2 * q_width + k_width :] = gv[rows, :].astype(jnp.bfloat16)
    ga1 = (
        nt(gall_out[:, :q_width], wq[...])
        + nt(gall_out[:, q_width : 2 * q_width], wg[...])
        + nt(gall_out[:, 2 * q_width : 2 * q_width + k_width], wk[...])
        + nt(gall_out[:, 2 * q_width + k_width :], wv[...])
    )
    ga1_out[...] = ga1.astype(jnp.bfloat16)

    @pl.when(step == steps - 1)
    def _():
        square_out[...] = square_out[...] * (lax.axis_index("heads") == 0).astype(jnp.float32)

    gain_out[...] += jnp.sum(ga1 * (xf * lax.rsqrt(mean_x + NORM_EPS)), axis=0, keepdims=True)


def attn_backward(lengths, g2, x, attn, mlp, cot, gain_two, query_gain, key_gain, cos, sin,
                  qr, kr, v, q, k, gate, o, lse, wq, wg, wk, wv, wo):
    rows, width = x.shape
    steps = rows // TILE
    q_width, k_width = wq.shape[1], wk.shape[1]
    hd = query_gain.shape[1]
    tile = lambda w: pl.BlockSpec((TILE, w), lambda i: (steps - 1 - i, 0))
    bf, f32 = jnp.bfloat16, jnp.float32
    total = 2 * q_width + 2 * k_width
    return pl.pallas_call(
        attn_backward_kernel,
        grid=(steps,),
        out_shape=[
            jax.ShapeDtypeStruct((rows, width), bf), jax.ShapeDtypeStruct((rows, width), bf),
            jax.ShapeDtypeStruct((rows, q_width), bf), jax.ShapeDtypeStruct((rows, total), bf),
            jax.ShapeDtypeStruct((rows, width), bf), jax.ShapeDtypeStruct((1, width), f32),
            jax.ShapeDtypeStruct((2, hd), f32), jax.ShapeDtypeStruct((6, hd), f32),
        ],
        in_specs=[pl.BlockSpec(memory_space=pltpu.SMEM)] + [tile(width)] * 5
        + [whole(gain_two.shape), whole((1, hd)), whole((1, hd)), tile(hd), tile(hd),
                  tile(q_width), whole((rows, k_width)), whole((rows, k_width)), tile(q_width), tile(k_width),
                  tile(q_width), tile(q_width), pl.BlockSpec((1,) + lse.shape[1:], lambda i: (steps - 1 - i, 0, 0))]
        + [whole(w.shape) for w in (wq, wg, wk, wv, wo)],
        out_specs=[tile(width), tile(width), tile(q_width), tile(total), tile(width), whole((1, width)), whole((2, hd)), whole((6, hd))],
        scratch_shapes=[pltpu.VMEM((k_width, rows), bf), pltpu.VMEM((rows, k_width), f32),
                        pltpu.VMEM((rows, k_width), f32), pltpu.VMEM((TILE, q_width), f32)],
        compiler_params=pltpu.CompilerParams(vmem_limit_bytes=60 * 1024 * 1024),
        cost_estimate=pl.CostEstimate(flops=2 * rows * width * (3 * q_width + 2 * k_width) + (12 << 30), bytes_accessed=50 << 20, transcendentals=4 << 20),
        name="attn_backward",
    )(lengths, g2, x, attn, mlp, cot, gain_two, query_gain, key_gain, cos, sin,
      qr, kr, v, q, k, gate, o, lse, wq, wg, wk, wv, wo)


def finish_kernel(moves, count, x, gain, grad_hidden, grad_sum, *refs):
    ins, tokens_out, outs = refs[:count], refs[count], refs[count + 1 :]
    xf = x[...].astype(jnp.float32)
    rho = rms_scale(xf)
    n = xf * rho
    gs = grad_sum[...].astype(jnp.float32) * gain_row(gain, 0)
    back = rho * (gs - n * jnp.mean(gs * n, axis=-1, keepdims=True))
    tokens_out[...] = (grad_hidden[...].astype(jnp.float32) + back).astype(jnp.bfloat16)
    for source, low, width, target, place in moves:
        outs[target][:, place : place + width] = ins[source][:, low : low + width].astype(jnp.float32)


def finish(x, gain, grad_hidden, grad_sum, grads, moves, widths):
    rows, width = x.shape
    shard = grads[0].shape[0]
    steps = 4
    tile = pl.BlockSpec((rows // steps, width), lambda i: (i, 0))
    part = lambda w: pl.BlockSpec((shard // steps, w), lambda i: (i, 0))
    return pl.pallas_call(
        functools.partial(finish_kernel, moves, len(grads)),
        grid=(steps,),
        out_shape=[jax.ShapeDtypeStruct((rows, width), jnp.bfloat16)]
        + [jax.ShapeDtypeStruct((shard, w), jnp.float32) for w in widths],
        in_specs=[tile, whole(gain.shape), tile, tile] + [part(g.shape[1]) for g in grads],
        out_specs=[tile] + [part(w) for w in widths],
        compiler_params=pltpu.CompilerParams(vmem_limit_bytes=60 * 1024 * 1024),
        cost_estimate=pl.CostEstimate(flops=20 * rows * width, bytes_accessed=30 << 20, transcendentals=0),
        name="finish",
    )(x, gain, grad_hidden, grad_sum, *grads)


def scatter_kernel(units, sources, kept, lefts, count, A, B, H, small_count, sums, *refs):
    nu = len(units)
    left_refs, refs = refs[:lefts], refs[lefts:]
    ins, refs = refs[:count], refs[count:]
    kept_ins, refs = refs[: len(kept)], refs[len(kept) :]
    if H:
        pieces, refs = refs[:small_count], refs[small_count:]
    sum_ins, refs = refs[:sums], refs[sums:]
    outs, sum_outs, refs = refs[:count], refs[count : count + sums], refs[count + sums :]
    if H:
        small_out, refs = refs[0], refs[1:]
    kept_outs, refs = refs[: len(kept)], refs[len(kept) :]
    rest = list(refs)
    each = SUM_REFS - 2
    totals = [HeadSum((sum_ins[i], sum_outs[i]) + tuple(rest[i * each : (i + 1) * each])) for i in range(sums)]
    rest = rest[sums * each :]
    if H:
        small, row_in, col_in, row_send, row_recv, col_send, col_recv = rest[-7:]
        rest = rest[:-7]
    turned, rest = rest[:lefts], rest[lefts:]
    own, side_in, up_in, down_in, stage = (rest[k * nu:(k + 1) * nu] for k in range(5))
    side_send, side_recv, up_send, up_recv, down_send, down_recv = rest[5 * nu:]
    me = lax.axis_index("batch")
    a, b = me // B, me % B
    up_ok, down_ok = a < A - 1, a > 0

    R = own[0].shape[1]

    def product(u, blk, target):
        i, lo, width, _ = units[u]
        left = turned[sources[i]][pl.ds(pl.multiple_of(blk * R, R), R), :]
        target[...] = nn(left, ins[i][:, lo : lo + width]).astype(jnp.bfloat16)

    def turn(blk):
        for left, flat in zip(left_refs, turned):
            flat[pl.ds(pl.multiple_of(blk * R, R), R), :] = left[:, pl.ds(pl.multiple_of(blk * R, R), R)].T

    barrier = pltpu.get_barrier_semaphore()

    def greet(target):
        pl.semaphore_signal(barrier, inc=1, device_id={"batch": target}, device_id_type=MESH)

    n = A * B
    if H:
        head = lax.axis_index("heads")
        for k in range(1, n):
            greet((me + k) % n)
        for k in range(1, H):
            pl.semaphore_signal(barrier, inc=1, device_id={"heads": (head + k) % H}, device_id_type=MESH)
        guests = n - 1 + H - 1
    else:
        pl.when(up_ok)(lambda: greet(me + B))
        pl.when(down_ok)(lambda: greet(me - B))
        for k in range(1, B):
            greet(a * B + (b + k) % B)
        guests = up_ok.astype(jnp.int32) + down_ok.astype(jnp.int32) + (B - 1)
        if totals:
            totals[0].greet(barrier)
            guests = guests + 2

    def at_distance(d, fn):
        if d == 0:
            return

        @pl.when(a + d < A)
        def _():
            fn(a + d, True)

        @pl.when(a - d >= 0)
        def _():
            fn(a - d, False)

    if R % 128:
        for left, flat in zip(left_refs, turned):
            for low in range(0, flat.shape[0], 256):
                flat[low : low + 256, :] = left[:, low : low + 256].T
    pl.semaphore_wait(barrier, guests)
    for total in totals:
        total.start()

    def to_heads(k):
        return pltpu.make_async_remote_copy(
            small, row_in.at[head], row_send.at[k - 1], row_recv.at[head],
            device_id={"heads": (head + k) % H}, device_id_type=MESH)

    def to_batch(k):
        return pltpu.make_async_remote_copy(
            col_in.at[me], col_in.at[me], col_send.at[k - 1], col_recv.at[me],
            device_id={"batch": (me + k) % n}, device_id_type=MESH)

    if H:
        low = 0
        for piece_ref in pieces:
            rows = piece_ref.shape[0]
            small[low : low + rows, :] = piece_ref[...]
            low += rows
        for k in range(1, H):
            to_heads(k).start()
        row_in[head] = small[...]

    for d in range(A - 1, -1, -1):
        def start(dest, _=None):
            for k in range(1, B):
                bb = (b + k) % B
                if R % 128 == 0:
                    turn(dest * B + bb)
                for u in range(nu):
                    if units[u][3]:
                        continue
                    product(u, dest * B + bb, stage[u].at[k - 1, dest])
                    pltpu.make_async_remote_copy(
                        stage[u].at[k - 1, dest], side_in[u].at[k - 1, dest], side_send.at[u, k - 1, dest],
                        side_recv.at[u, k - 1, dest], device_id={"batch": a * B + bb}, device_id_type=MESH).start()

        at_distance(d, start) if d else start(a)
        if d == A - 1:
            for total in totals:
                total.cross()
    if R % 128 == 0:
        for dest in range(A):
            turn(dest * B + b)
    for which, right, whole_out in zip(kept, kept_ins, kept_outs):
        def keep(blk, carry, which=which, right=right, whole_out=whole_out):
            rows = pl.ds(pl.multiple_of(blk * R, R), R)
            whole_out[rows, :] = nn(turned[which][rows, :], right[...]).astype(jnp.bfloat16)
            return carry

        lax.fori_loop(0, n, keep, 0)

    def await_bytes(ref, sem):
        pltpu.make_async_copy(ref, ref, sem).wait()

    if H:
        for k in range(1, H):
            other = (head + k) % H
            await_bytes(row_in.at[other], row_recv.at[other])
        group_sum = row_in[0]
        for k in range(1, H):
            group_sum = group_sum + row_in[k]
        col_in[me] = group_sum
        for k in range(1, n):
            to_batch(k).start()

    step_rows = min(R, 32)

    def add_into(target, terms):
        def body(t, carry):
            rows = pl.ds(pl.multiple_of(t * step_rows, step_rows), step_rows)
            total = terms[0][rows, :].astype(jnp.float32)
            for term in terms[1:]:
                total = total + term[rows, :].astype(jnp.float32)
            target[rows, :] = total.astype(target.dtype)
            return carry

        lax.fori_loop(0, R // step_rows, body, 0)

    def local_terms(u, dest, bb):
        if units[u][3]:
            slot = dest * B + bb
            product(u, slot, own[u].at[slot])
            return [own[u].at[slot]], slot
        product(u, dest * B + b, own[u].at[dest])
        for k in range(1, B):
            await_bytes(side_in[u].at[k - 1, dest], side_recv.at[u, k - 1, dest])
        return [own[u].at[dest]] + [side_in[u].at[k - 1, dest] for k in range(1, B)], dest

    order = [u for u in range(nu) if units[u][3]] + [u for u in range(nu) if not units[u][3]]
    for d in range(A - 1, 0, -1):
        for u in order:
            def flow(dest, goes_up, u=u):
                for k in range(B if units[u][3] else 1):
                    terms, slot = local_terms(u, dest, (b + k) % B)
                    buf = (up_in if goes_up else down_in)[u].at[slot]
                    send, recv = (up_send, up_recv) if goes_up else (down_send, down_recv)
                    fed = down_ok if goes_up else up_ok

                    @pl.when(fed)
                    def _():
                        await_bytes(buf, recv.at[u, slot])
                        add_into(buf, [buf] + terms)

                    @pl.when(jnp.logical_not(fed))
                    def _():
                        add_into(buf, terms)

                    pltpu.make_async_remote_copy(
                        buf, buf, send.at[u, slot], recv.at[u, slot],
                        device_id={"batch": me + B if goes_up else me - B}, device_id_type=MESH).start()

            at_distance(d, flow)

    def out_piece(u):
        i, lo, width, _ = units[u]
        return outs[i].at[:, pl.ds(lo, width)]

    def arrive_home(u, bb, target):
        terms, slot = local_terms(u, a, bb)

        @pl.when(down_ok)
        def _():
            await_bytes(up_in[u].at[slot], up_recv.at[u, slot])

        @pl.when(up_ok)
        def _():
            await_bytes(down_in[u].at[slot], down_recv.at[u, slot])

        @pl.when(down_ok & up_ok)
        def _():
            add_into(target, terms + [up_in[u].at[slot], down_in[u].at[slot]])

        @pl.when(down_ok & jnp.logical_not(up_ok))
        def _():
            add_into(target, terms + [up_in[u].at[slot]])

        @pl.when(up_ok & jnp.logical_not(down_ok))
        def _():
            add_into(target, terms + [down_in[u].at[slot]])

    for total in totals:
        total.settle()
    for u in order:
        if units[u][3]:
            for k in range(1, B):
                bb = (b + k) % B
                slot = a * B + bb
                arrive_home(u, bb, own[u].at[slot])
                pltpu.make_async_remote_copy(
                    own[u].at[slot], side_in[u].at[k - 1, 0], side_send.at[u, k - 1, 0], side_recv.at[u, k - 1, 0],
                    device_id={"batch": slot}, device_id_type=MESH).start()
            arrive_home(u, b, own[u].at[a * B + b])
        else:
            arrive_home(u, b, out_piece(u))
    for u in order:
        if units[u][3]:
            for k in range(1, B):
                await_bytes(side_in[u].at[k - 1, 0], side_recv.at[u, k - 1, 0])
            add_into(out_piece(u), [own[u].at[a * B + b]] + [side_in[u].at[k - 1, 0] for k in range(1, B)])

    for total in totals:
        total.finish()
    if H:
        for k in range(1, n):
            other = (me + k) % n
            await_bytes(col_in.at[other], col_recv.at[other])
        whole_sum = col_in[0]
        for k in range(1, n):
            whole_sum = whole_sum + col_in[k]
        small_out[...] = whole_sum
        for k in range(1, H):
            to_heads(k).wait_send()
        for k in range(1, n):
            to_batch(k).wait_send()

    for u in range(nu):
        first = units[u][3]
        for k in range(1, B):
            if first:
                await_bytes(side_in[u].at[k - 1, 0], side_send.at[u, k - 1, 0])
            else:
                for dest in range(A):
                    await_bytes(side_in[u].at[k - 1, dest], side_send.at[u, k - 1, dest])
        for d in range(A - 1, 0, -1):
            def done(dest, goes_up, u=u, first=first):
                send = up_send if goes_up else down_send
                for k in range(B if first else 1):
                    slot = dest * B + k if first else dest
                    await_bytes(up_in[u].at[slot], send.at[u, slot])

            at_distance(d, done)


def scatter_all(lefts, rights, sources, units, cid, small=None, sums=(), kept=(), kept_rights=(), out_dtype=jnp.bfloat16):
    n = lax.axis_size("batch")
    A, B = grid_of(n)
    nu = len(units)
    R = lefts[0].shape[1] // n

    def slots(u):
        return n if units[u][3] else A

    scratch = [ref for s in sums for ref in head_sum_scratch(s)]
    scratch += [pltpu.VMEM(left.shape[::-1], left.dtype) for left in lefts]
    scratch += [pltpu.VMEM((slots(u), R, units[u][2]), jnp.bfloat16) for u in range(nu)]
    scratch += [pltpu.VMEM((B - 1, 1 if units[u][3] else A, R, units[u][2]), jnp.bfloat16) for u in range(nu)]
    scratch += [pltpu.VMEM((slots(u), R, units[u][2]), jnp.bfloat16) for u in range(nu)]
    scratch += [pltpu.VMEM((slots(u), R, units[u][2]), jnp.bfloat16) for u in range(nu)]
    scratch += [pltpu.VMEM((B - 1, 1 if units[u][3] else A, R, units[u][2]), jnp.bfloat16) for u in range(nu)]
    dma = pltpu.SemaphoreType.DMA
    scratch += [dma((nu, B - 1, A)), dma((nu, B - 1, A)), dma((nu, n)), dma((nu, n)), dma((nu, n)), dma((nu, n))]
    H = 0
    extra, small_outs = [], []
    if small is not None:
        H = lax.axis_size("heads")
        extra = list(small)
        small_shape = (sum(e.shape[0] for e in extra), extra[0].shape[1])
        small_outs = [jax.ShapeDtypeStruct(small_shape, jnp.float32)]
        scratch += [
            pltpu.VMEM(small_shape, jnp.float32),
            pltpu.VMEM((H,) + small_shape, jnp.float32), pltpu.VMEM((n,) + small_shape, jnp.float32),
            dma((H - 1,)), dma((H,)), dma((n - 1,)), dma((n,)),
        ]
    res = pl.pallas_call(
        functools.partial(scatter_kernel, units, sources, kept, len(lefts), len(rights), A, B, H, len(extra), len(sums)),
        out_shape=[jax.ShapeDtypeStruct((R, g.shape[1]), out_dtype) for g in rights]
        + [jax.ShapeDtypeStruct(s.shape, s.dtype) for s in sums]
        + small_outs
        + [jax.ShapeDtypeStruct((lefts[w].shape[1], g.shape[1]), out_dtype) for w, g in zip(kept, kept_rights)],
        in_specs=[pl.BlockSpec(memory_space=pltpu.VMEM)] * (len(lefts) + len(rights) + len(kept)) + [pl.BlockSpec(memory_space=pltpu.VMEM)] * len(extra) + [pl.BlockSpec(memory_space=pl.ANY)] * len(sums),
        out_specs=[pl.BlockSpec(memory_space=pltpu.VMEM)] * len(rights) + [pl.BlockSpec(memory_space=pl.ANY)] * len(sums)
        + [pl.BlockSpec(memory_space=pltpu.VMEM)] * (len(small_outs) + len(kept)),
        scratch_shapes=scratch,
        compiler_params=pltpu.CompilerParams(collective_id=cid, has_side_effects=True, vmem_limit_bytes=VMEM_LIMIT),
        cost_estimate=pl.CostEstimate(flops=0, bytes_accessed=sum(g.size for g in rights) * 16, transcendentals=0),
    )(*lefts, *rights, *kept_rights, *extra, *sums)
    return list(res)


def column_units(widths, side_first, chunk=512):
    units = []
    for index, width in enumerate(widths):
        for low in range(0, width, chunk):
            units.append((index, low, min(chunk, width - low), (index, low) in side_first))
    return units


def local(
    tokens,
    lengths,
    cotangent,
    attn_norm_gain,
    query_norm_gain,
    key_norm_gain,
    w_query,
    w_gate_attn,
    w_key,
    w_value,
    w_out,
    mlp_norm_gain,
    w_gate,
    w_up,
    w_down,
):
    row_count, model_width = tokens.shape
    head_width = query_norm_gain.shape[0]
    shard_rows = w_query.shape[0]
    attn_shards = [w_query, w_gate_attn, w_key, w_value, w_out]
    gain_shards = [jnp.stack([attn_norm_gain, mlp_norm_gain])]
    q_width, k_width = w_query.shape[1], w_key.shape[1]
    gather_units = [
        (5, None, None, False),
        (0, 0, q_width, False),
        (1, 0, q_width, False),
        (2, 0, k_width, True),
        (3, 0, k_width, False),
        (4, 0, q_width, False),
    ]
    query_full, gate_attn_full, key_full, value_full, out_full, gains, cos_table, sin_table = gather_all(
        attn_shards + gain_shards, gather_units, 0, tables=(row_count, head_width)
    )
    cut = w_down.shape[1] // 2
    down_first, down_last = w_down[:, :cut], w_down[:, cut:]
    down_first, query_full = lax.optimization_barrier((down_first, query_full))
    down_first = lax.all_gather(down_first, "batch", axis=0, tiled=True)
    gains = gains.reshape(-1, 2, shard_rows)
    query_gain = query_norm_gain.reshape(1, -1)
    key_gain = key_norm_gain.reshape(1, -1)
    attn_weights = (query_full, gate_attn_full, key_full, value_full, out_full)
    input_one, query_rot, key_rot, values, queries, keys_pre, gate_logit, attended, log_totals, attn_part = attn_forward(
        lengths, tokens, gains, query_gain, key_gain, cos_table, sin_table, *attn_weights
    )
    mlp_widths = [w_gate.shape[1], w_up.shape[1]]
    gate_full, up_full, attn_sum = gather_all(
        [w_gate, w_up], column_units(mlp_widths, {(1, 0)}, 384), 1, sums=[attn_part]
    )
    down_last, attn_sum = lax.optimization_barrier((down_last, attn_sum))
    down_last = lax.all_gather(down_last, "batch", axis=0, tiled=True)
    input_two, grad_mlp, activated, gate_pre, up_pre = mlp_forward(
        lengths, tokens, attn_sum, cotangent, gains, gate_full, up_full
    )
    grad_w_down = contract_rows(grad_mlp, activated).astype(jnp.bfloat16)
    grad_w_down, grad_mlp, activated = lax.optimization_barrier((grad_w_down, grad_mlp, activated))
    grad_down = lax.psum_scatter(grad_w_down, "batch", scatter_dimension=0, tiled=True)
    grad_gate_pre, grad_up_first, grad_up_last, mlp_part, grad_two_send, gain_two_part = mlp_backward(
        tokens, attn_sum, grad_mlp, activated, gate_pre, up_pre, gate_full, up_full, down_first, down_last
    )
    late_units = [
        (0, 0, 512, False),
        (0, 512, 512, False),
        (0, 1024, 512, False),
        (1, 0, cut // 2, False),
        (1, cut // 2, cut // 2, False),
    ]
    grad_gate, grad_up, grad_two_sum, mlp_sum, grad_w_late = scatter_all(
        [input_two],
        [grad_gate_pre, grad_up_first],
        (0, 0),
        late_units,
        2,
        sums=[grad_two_send, mlp_part],
        kept=(0,),
        kept_rights=[grad_up_last],
    )
    grad_late = lax.psum_scatter(grad_w_late, "batch", scatter_dimension=0, tiled=True)
    output, grad_hidden, gated, grad_all, grad_one_send, gain_one_part, head_gains, own_sums = attn_backward(
        lengths, grad_two_sum, tokens, attn_sum, mlp_sum, cotangent, gains, query_gain, key_gain,
        cos_table, sin_table, query_rot, key_rot, values, queries, keys_pre, gate_logit, attended, log_totals,
        *attn_weights,
    )
    small = [
        gain_one_part.reshape(-1, head_width), gain_two_part.reshape(-1, head_width), head_gains, own_sums,
    ]
    attn_units = [
        (0, 0, q_width, False),
        (0, q_width, q_width, False),
        (0, 2 * q_width, k_width, True),
        (0, 2 * q_width + k_width, k_width, False),
        (1, 0, q_width, False),
    ]
    grad_all_sum, grad_out_sum, grad_one_sum, sums = scatter_all(
        [input_one, grad_hidden],
        [grad_all, gated],
        (0, 1),
        attn_units,
        3,
        small,
        sums=[grad_one_send],
    )
    gain_rows = model_width // head_width
    mine = lax.axis_index("batch") * shard_rows
    gain_one_grad = lax.dynamic_slice(sums[:gain_rows].reshape(-1), (mine,), (shard_rows,))
    gain_two_grad = lax.dynamic_slice(sums[gain_rows : 2 * gain_rows].reshape(-1), (mine,), (shard_rows,))
    query_gain_all = sums[2 * gain_rows]
    key_gain_all = sums[2 * gain_rows + 1]
    squares_all = jnp.sum(sums[2 * gain_rows + 2 :], axis=1)
    block_rms = jnp.sqrt(squares_all[:5] / (squares_all[5] * model_width))
    widths = [w.shape[1] for w in attn_shards] + [w_gate.shape[1], w_up.shape[1], w_down.shape[1]]
    moves, low = [], 0
    for index in range(4):
        moves.append((0, low, widths[index], index, 0))
        low += widths[index]
    moves += [
        (1, 0, widths[4], 4, 0),
        (2, 0, widths[5], 5, 0),
        (3, 0, cut, 6, 0),
        (4, 0, widths[6] - cut, 6, cut),
        (5, 0, widths[7], 7, 0),
    ]
    grad_tokens, *weight_grads = finish(
        tokens, gains, grad_hidden, grad_one_sum,
        [grad_all_sum, grad_out_sum, grad_gate, grad_up, grad_late, grad_down], moves, widths,
    )
    return (
        output,
        grad_tokens,
        gain_one_grad,
        query_gain_all,
        key_gain_all,
        *weight_grads[:5],
        gain_two_grad,
        *weight_grads[5:],
        block_rms,
    )


def solution(mesh):
    return jax.shard_map(
        local,
        mesh=mesh,
        in_specs=(
            P("batch", None),
            P("batch"),
            P("batch", None),
            P("batch"),
            P(),
            P(),
            P("batch", "heads"),
            P("batch", "heads"),
            P("batch", "heads"),
            P("batch", "heads"),
            P("batch", "heads"),
            P("batch"),
            P("batch", "heads"),
            P("batch", "heads"),
            P("batch", "heads"),
        ),
        out_specs=(
            P("batch", None),
            P("batch", None),
            P("batch"),
            P(),
            P(),
            P("batch", "heads"),
            P("batch", "heads"),
            P("batch", "heads"),
            P("batch", "heads"),
            P("batch", "heads"),
            P("batch"),
            P("batch", "heads"),
            P("batch", "heads"),
            P("batch", "heads"),
            P(),
        ),
        check_vma=False,
    )
```

```python
import functools
import math

import jax
import jax.numpy as jnp
from jax import lax
from jax.experimental import pallas as pl
from jax.experimental.pallas import tpu as pltpu
from jax.sharding import PartitionSpec as P

SLOT_LEN = 1024
MESH = pl.DeviceIdType.MESH


NORM_EPS = 1e-06
ROPE_THETA = 1000000.0
MASKED = -1e30


def contract_rows(left_side, right_side):
    return lax.dot_general(
        left_side, right_side, (((0,), (0,)), ((), ())), preferred_element_type=jnp.float32
    )


VMEM_LIMIT = 64 * 1024 * 1024 - 65536


def grid_of(n):
    inner = 2 if n <= 8 else 4
    return (n // inner, inner)


class HeadSum:
    def __init__(self, refs):
        (self.src, self.out, self.core_in, self.mid, self.far_in,
         self.load_sem, self.core_send, self.core_recv, self.far_send, self.far_recv,
         self.back_send, self.back_recv, self.keep_sem) = refs
        head = lax.axis_index("heads")
        self.core = head % 2
        self.near = head + 1 - 2 * self.core
        self.far = (head + 2) % 4
        self.pieces, self.rows = self.mid.shape[0], self.mid.shape[1]

    def greet(self, barrier):
        for other in (self.near, self.far):
            pl.semaphore_signal(barrier, inc=1, device_id={"heads": other}, device_id_type=MESH)

    def part(self, ref, half, k):
        return ref.at[pl.ds(pl.multiple_of((half * self.pieces + k) * self.rows, self.rows), self.rows), :]

    def load(self, k):
        return pltpu.make_async_copy(self.part(self.src, self.core, k), self.mid.at[k], self.load_sem.at[k])

    def to_core(self, k):
        return pltpu.make_async_remote_copy(
            self.part(self.src, 1 - self.core, k), self.core_in.at[k], self.core_send.at[k], self.core_recv.at[k],
            device_id={"heads": self.near}, device_id_type=MESH)

    def to_far(self, k):
        return pltpu.make_async_remote_copy(
            self.mid.at[k], self.far_in.at[k], self.far_send.at[k], self.far_recv.at[k],
            device_id={"heads": self.far}, device_id_type=MESH)

    def keep(self, k):
        return pltpu.make_async_copy(self.far_in.at[k], self.part(self.out, self.core, k), self.keep_sem.at[k])

    def back(self, k):
        return pltpu.make_async_remote_copy(
            self.far_in.at[k], self.part(self.out, self.core, k), self.back_send.at[k], self.back_recv.at[k],
            device_id={"heads": self.near}, device_id_type=MESH)

    def start(self):
        for k in range(self.pieces):
            self.to_core(k).start()
            self.load(k).start()

    def add(self, target, other):
        tile = min(self.rows, 16)

        def body(t, carry):
            rows = pl.ds(pl.multiple_of(t * tile, tile), tile)
            total = target[rows, :].astype(jnp.float32) + other[rows, :].astype(jnp.float32)
            target[rows, :] = total.astype(target.dtype)
            return carry

        lax.fori_loop(0, self.rows // tile, body, 0)

    def cross(self):
        for k in range(self.pieces):
            self.load(k).wait()
            pltpu.make_async_copy(self.core_in.at[k], self.core_in.at[k], self.core_recv.at[k]).wait()
            self.add(self.mid.at[k], self.core_in.at[k])
            self.to_far(k).start()

    def settle(self):
        for k in range(self.pieces):
            pltpu.make_async_copy(self.far_in.at[k], self.far_in.at[k], self.far_recv.at[k]).wait()
            self.add(self.far_in.at[k], self.mid.at[k])
            self.keep(k).start()
            self.back(k).start()

    def finish(self):
        for k in range(self.pieces):
            other = self.part(self.out, 1 - self.core, k)
            pltpu.make_async_copy(other, other, self.back_recv.at[k]).wait()
            self.keep(k).wait()
            self.to_core(k).wait_send()
            self.to_far(k).wait_send()
            self.back(k).wait_send()


SUM_REFS = 13
SUM_PIECES = 4


def head_sum_scratch(array):
    rows, width = array.shape
    shape = (SUM_PIECES, rows // 2 // SUM_PIECES, width)
    return [pltpu.VMEM(shape, array.dtype)] * 3 + [pltpu.SemaphoreType.DMA((SUM_PIECES,))] * 8


def gather_kernel(plan, rows_n, cols_n, *refs):
    count, sums = plan["count"], plan["sums"]
    ins, sum_ins, refs = refs[:count], refs[count : count + sums], refs[count + sums :]
    outs, sum_outs, refs = refs[:count], refs[count : count + sums], refs[count + sums :]
    if plan["tables"]:
        cos_out, sin_out, refs = refs[0], refs[1], refs[2:]
    send_up, send_down, send_side, recv, local_sem = refs[:5]
    each = SUM_REFS - 2
    totals = [
        HeadSum((sum_ins[i], sum_outs[i]) + tuple(refs[5 + i * each : 5 + (i + 1) * each])) for i in range(sums)
    ]
    A, B = rows_n, cols_n
    me = lax.axis_index("batch")
    a, b = me // B, me % B
    units = plan["units"]

    def block(u, blk):
        i, lo, width = units[u][:3]
        ref = outs[i].at[blk]
        return ref if lo is None else ref.at[:, pl.ds(lo, width)]

    def own(u):
        i, lo, width = units[u][:3]
        return ins[i] if lo is None else ins[i].at[:, pl.ds(lo, width)]

    def put(u, src, blk, sem, target):
        pltpu.make_async_remote_copy(src, block(u, blk), sem, recv.at[u, blk], device_id={"batch": target}, device_id_type=pl.DeviceIdType.MESH).start()

    def arrived(u, blk):
        pltpu.make_async_copy(block(u, blk), block(u, blk), recv.at[u, blk]).wait()

    def sent(u, sem):
        pltpu.make_async_copy(own(u), own(u), sem).wait()

    barrier = pltpu.get_barrier_semaphore()

    def greet(target):
        pl.semaphore_signal(barrier, inc=1, device_id={"batch": target}, device_id_type=pl.DeviceIdType.MESH)

    up_ok, down_ok = a < A - 1, a > 0
    pl.when(up_ok)(lambda: greet(me + B))
    pl.when(down_ok)(lambda: greet(me - B))
    for k in range(1, B):
        greet(a * B + (b + k) % B)
    if totals:
        totals[0].greet(barrier)
    pl.semaphore_wait(barrier, up_ok.astype(jnp.int32) + down_ok.astype(jnp.int32) + (B - 1) + (2 if totals else 0))
    for total in totals:
        total.start()

    nu = len(units)

    def up(u, src, blk, slot):
        @pl.when(up_ok)
        def _():
            put(u, src, blk, send_up.at[u, slot], me + B)

    def down(u, src, blk, slot):
        @pl.when(down_ok)
        def _():
            put(u, src, blk, send_down.at[u, slot], me - B)

    def side(u, src, blk, step):
        for k in range(1, B):
            put(u, src, blk, send_side.at[u, step * (B - 1) + k - 1], a * B + (b + k) % B)

    for u in range(nu):
        up(u, own(u), me, b)
        down(u, own(u), me, b)
        side(u, own(u), me, 0)
    for i in range(count):
        pltpu.make_async_copy(ins[i], outs[i].at[me], local_sem.at[i]).start()

    for total in totals:
        total.cross()
    for u in range(nu):
        if units[u][3]:
            for k in range(1, B):
                bb = (b + k) % B
                blk = a * B + bb
                arrived(u, blk)
                up(u, block(u, blk), blk, bb)
                down(u, block(u, blk), blk, bb)
    for s in range(1, A):
        if s == A - 1:
            for total in totals:
                total.settle()
        for u in range(nu):
            first = units[u][3]

            @pl.when(a - s >= 0)
            def _(u=u, first=first):
                for k in range(B if first else 1):
                    bb = (b + k) % B
                    blk = (a - s) * B + bb
                    arrived(u, blk)
                    up(u, block(u, blk), blk, s * B + bb)
                    if not first:
                        side(u, block(u, blk), blk, 2 * s - 1)

            @pl.when(a + s < A)
            def _(u=u, first=first):
                for k in range(B if first else 1):
                    bb = (b + k) % B
                    blk = (a + s) * B + bb
                    arrived(u, blk)
                    down(u, block(u, blk), blk, s * B + bb)
                    if not first:
                        side(u, block(u, blk), blk, 2 * s)
    for total in totals:
        total.finish()
    if plan["tables"]:
        rows, width = cos_out.shape
        tile = min(rows, 128)
        lane = lax.broadcasted_iota(jnp.int32, (1, width), 1)
        column = (lane % (width // 2)).astype(jnp.float32)
        inverse = jnp.exp(column * (-2.0 * math.log(ROPE_THETA) / width))
        sign = jnp.where(lane < width // 2, -1.0, 1.0)

        def fill(t, carry):
            first = pl.multiple_of(t * tile, tile)
            place = (first + lax.broadcasted_iota(jnp.int32, (tile, 1), 0)) % SLOT_LEN
            angles = place.astype(jnp.float32) * inverse
            cos_out[pl.ds(first, tile), :] = jnp.cos(angles)
            sin_out[pl.ds(first, tile), :] = jnp.sin(angles) * sign
            return carry

        lax.fori_loop(0, rows // tile, fill, 0)
    for u in range(nu):
        if not units[u][3]:
            for s in range(A):
                for k in range(1, B):
                    bb = (b + k) % B

                    @pl.when(a - s >= 0)
                    def _(u=u, s=s, bb=bb):
                        arrived(u, (a - s) * B + bb)

                    if s:
                        @pl.when(a + s < A)
                        def _(u=u, s=s, bb=bb):
                            arrived(u, (a + s) * B + bb)
    for u in range(nu):
        first = units[u][3]
        for s in range(A):
            for k in range(B if first else 1):
                bb = (b + k) % B

                @pl.when((a - s >= 0) & up_ok)
                def _(u=u, s=s, bb=bb):
                    sent(u, send_up.at[u, s * B + bb])

                @pl.when((a + s < A) & down_ok)
                def _(u=u, s=s, bb=bb):
                    sent(u, send_down.at[u, s * B + bb])
            if s == 0 or not first:
                for k in range(1, B):
                    if s == 0:
                        sent(u, send_side.at[u, k - 1])
                    else:
                        @pl.when(a - s >= 0)
                        def _(u=u, s=s, k=k):
                            sent(u, send_side.at[u, (2 * s - 1) * (B - 1) + k - 1])

                        @pl.when(a + s < A)
                        def _(u=u, s=s, k=k):
                            sent(u, send_side.at[u, (2 * s) * (B - 1) + k - 1])
    for i in range(count):
        pltpu.make_async_copy(ins[i], outs[i].at[me], local_sem.at[i]).wait()


def gather_all(shards, plan_units, cid, sums=(), tables=None):
    n = lax.axis_size("batch")
    A, B = grid_of(n)
    nu = len(plan_units)
    plan = {"count": len(shards), "units": plan_units, "sums": len(sums), "tables": tables is not None}
    outs = [jax.ShapeDtypeStruct((n,) + s.shape, s.dtype) for s in shards]
    outs += [jax.ShapeDtypeStruct(s.shape, s.dtype) for s in sums]
    table_outs = [jax.ShapeDtypeStruct(tables, jnp.float32)] * 2 if tables else []
    sum_scratch = [ref for s in sums for ref in head_sum_scratch(s)]
    res = pl.pallas_call(
        functools.partial(gather_kernel, plan, A, B),
        out_shape=outs + table_outs,
        in_specs=[pl.BlockSpec(memory_space=pltpu.VMEM)] * len(shards) + [pl.BlockSpec(memory_space=pl.ANY)] * len(sums),
        out_specs=[pl.BlockSpec(memory_space=pl.ANY)] * len(outs) + [pl.BlockSpec(memory_space=pltpu.VMEM)] * len(table_outs),
        scratch_shapes=[
            pltpu.SemaphoreType.DMA((nu, A * B)),
            pltpu.SemaphoreType.DMA((nu, A * B)),
            pltpu.SemaphoreType.DMA((nu, (2 * A - 1) * (B - 1))),
            pltpu.SemaphoreType.DMA((nu, n)),
            pltpu.SemaphoreType.DMA((len(shards),)),
        ] + sum_scratch,
        compiler_params=pltpu.CompilerParams(collective_id=cid, has_side_effects=True, vmem_limit_bytes=VMEM_LIMIT),
        cost_estimate=pl.CostEstimate(flops=0, bytes_accessed=sum(s.size for s in shards) * 60, transcendentals=0),
    )(*shards, *sums)
    full = [r.reshape((n * r.shape[1],) + r.shape[2:]) if r.shape[1] > 1 else r.reshape(-1) for r in res[: len(shards)]]
    return full + list(res[len(shards) :])


TILE = 256


def nt(left_side, right_side):
    return lax.dot_general(left_side, right_side, (((1,), (1,)), ((), ())), preferred_element_type=jnp.float32)


def nn(left_side, right_side):
    return lax.dot_general(left_side, right_side, (((1,), (0,)), ((), ())), preferred_element_type=jnp.float32)


def rms_scale(value):
    return lax.rsqrt(jnp.mean(value * value, axis=-1, keepdims=True) + NORM_EPS)


def gain_row(gains, which):
    return jnp.concatenate(
        [gains[blk, which : which + 1, :].astype(jnp.float32) for blk in range(gains.shape[0])], axis=1
    )


def allowed_keys(key_count, lane_count, first_query, seq_length):
    keys = lax.broadcasted_iota(jnp.int32, (key_count, lane_count), 0)
    queries = first_query + lax.broadcasted_iota(jnp.int32, (key_count, lane_count), 1) % TILE
    return (keys <= queries) & (keys < seq_length)


def attn_forward_kernel(
    lengths, x, gain, query_gain, key_gain, cos, sin, wq, wg, wk, wv, wo,
    a1_out, qr_out, kr_out, v_out, q_out, k_out, gate_out, o_out, lse_out, part_out,
    kr_all, vt_all,
):
    step = pl.program_id(0)
    hd = query_gain.shape[1]
    heads, kv = wq.shape[1] // hd, wk.shape[1] // hd
    group = heads // kv
    xf = x[...].astype(jnp.float32)
    a1 = (xf * rms_scale(xf) * gain_row(gain, 0)).astype(jnp.bfloat16)
    a1_out[...] = a1
    k = nn(a1, wk[...])
    k_out[...] = k
    v = nn(a1, wv[...])
    v_out[...] = v.astype(jnp.bfloat16)
    q = nn(a1, wq[...])
    q_out[...] = q
    gate = nn(a1, wg[...])
    gate_out[...] = gate

    def rope(u, g):
        n = u * rms_scale(u) * g[...].astype(jnp.float32)
        return (n * cos[...] + pltpu.roll(n, hd // 2, 1) * sin[...]).astype(jnp.bfloat16)

    rows = pl.ds(pl.multiple_of(step * TILE, TILE), TILE)
    for j in range(kv):
        cols = slice(j * hd, (j + 1) * hd)
        kr = rope(k[:, cols], key_gain)
        kr_out[:, cols] = kr
        kr_all[rows, cols] = kr
    vt_all[:, rows] = v.T.astype(jnp.bfloat16)
    qr = [rope(q[:, h * hd : (h + 1) * hd], query_gain) for h in range(heads)]
    for h in range(heads):
        qr_out[:, h * hd : (h + 1) * hd] = qr[h]
    seq_length = lengths[0]
    scale = hd ** -0.5
    for i in range(SLOT_LEN // TILE):
        @pl.when(step == i)
        def _(i=i):
            count = (i + 1) * TILE
            mask = allowed_keys(count, group * TILE, i * TILE, seq_length)
            for j in range(kv):
                cols = slice(j * hd, (j + 1) * hd)
                stack = jnp.concatenate(qr[j * group : (j + 1) * group], axis=0)
                scores = jnp.where(mask, nt(kr_all[:count, cols], stack) * scale, MASKED)
                top = jnp.max(scores, axis=0, keepdims=True)
                weights = jnp.exp(scores - top)
                total = jnp.sum(weights, axis=0, keepdims=True)
                lse_out[0, j : j + 1, :] = top + jnp.log(total)
                probs = (weights * (1.0 / total)).astype(jnp.bfloat16)
                ot = nn(vt_all[cols, :count], probs)
                o = ot.T
                for g in range(group):
                    h = j * group + g
                    o_out[:, h * hd : (h + 1) * hd] = o[g * TILE : (g + 1) * TILE, :]
    og = (o_out[...] * jax.nn.sigmoid(gate)).astype(jnp.bfloat16)
    part_out[...] = nt(og, wo[...]).astype(jnp.bfloat16)


def whole(shape):
    return pl.BlockSpec(shape, lambda i: (0,) * len(shape), pipeline_mode=pl.Buffered(1))


def attn_forward(lengths, x, gain, query_gain, key_gain, cos, sin, wq, wg, wk, wv, wo):
    rows, width = x.shape
    steps = rows // TILE
    q_width, k_width = wq.shape[1], wk.shape[1]
    hd = query_gain.shape[1]
    tile = lambda w: pl.BlockSpec((TILE, w), lambda i: (i, 0))
    kv = k_width // hd
    lanes = q_width // k_width * TILE
    bf, f32 = jnp.bfloat16, jnp.float32
    shapes = [
        ((rows, width), bf), ((rows, q_width), bf), ((rows, k_width), bf), ((rows, k_width), bf),
        ((rows, q_width), f32), ((rows, k_width), f32), ((rows, q_width), f32), ((rows, q_width), f32),
        ((steps, kv, lanes), f32), ((rows, width), bf),
    ]
    out_specs = [tile(s[1]) for s, _ in shapes]
    out_specs[8] = pl.BlockSpec((1, kv, lanes), lambda i: (i, 0, 0))
    return pl.pallas_call(
        attn_forward_kernel,
        grid=(steps,),
        out_shape=[jax.ShapeDtypeStruct(*s) for s in shapes],
        in_specs=[pl.BlockSpec(memory_space=pltpu.SMEM), tile(width), whole(gain.shape), whole((1, hd)), whole((1, hd)),
                  tile(hd), tile(hd)] + [whole(w.shape) for w in (wq, wg, wk, wv, wo)],
        out_specs=out_specs,
        scratch_shapes=[pltpu.VMEM((rows, k_width), bf), pltpu.VMEM((k_width, rows), bf)],
        compiler_params=pltpu.CompilerParams(vmem_limit_bytes=60 * 1024 * 1024),
        cost_estimate=pl.CostEstimate(flops=2 * rows * width * (3 * q_width + 2 * k_width), bytes_accessed=40 << 20, transcendentals=4 << 20),
        name="attn_forward",
    )(lengths, x, gain, query_gain, key_gain, cos, sin, wq, wg, wk, wv, wo)


def mlp_forward_kernel(lengths, x, attn, cot, gain, wg, wu, a2_out, gm_out, hid_out, gu_out, up_out):
    t, c = pl.program_id(0), pl.program_id(1)
    rows = x.shape[0]

    @pl.when(c == 0)
    def _():
        h = x[...].astype(jnp.float32) + attn[...].astype(jnp.float32)
        a2_out[...] = (h * rms_scale(h) * gain_row(gain, 1)).astype(jnp.bfloat16)
        places = t * rows + lax.broadcasted_iota(jnp.int32, (rows, 1), 0)
        gm_out[...] = jnp.where(places < lengths[0], cot[...], 0.0).astype(jnp.bfloat16)

    a2 = a2_out[...]
    gu = nn(a2, wg[...])
    up = nn(a2, wu[...])
    gu_out[...] = gu.astype(jnp.bfloat16)
    up_out[...] = up.astype(jnp.bfloat16)
    hid_out[...] = (gu * jax.nn.sigmoid(gu) * up).astype(jnp.bfloat16)


def mlp_backward_kernel(last, gm, hid, gu_in, up_in, wg, wu, wd, *refs):
    gu, up = gu_in[...].astype(jnp.float32), up_in[...].astype(jnp.float32)
    sg = jax.nn.sigmoid(gu)
    g_hid = nn(gm[...], wd[...])
    g_gu = (g_hid * up * sg * (1.0 + gu * (1.0 - sg))).astype(jnp.bfloat16)
    g_up = (g_hid * (gu * sg)).astype(jnp.bfloat16)
    part = nt(hid[...], wd[...])
    ga2 = nt(g_gu, wg[...]) + nt(g_up, wu[...])
    if not last:
        ggu_out, gup_out, part_out, ga2_out = refs
        ggu_out[...] = g_gu
        gup_out[...] = g_up
        part_out[...] = part
        ga2_out[...] = ga2
        return
    x, attn, part_in, ga2_in, ggu_out, gup_out, part_out, ga2_out, gain_out = refs
    ggu_out[...] = g_gu
    gup_out[...] = g_up
    part_out[...] = (part_in[...] + part).astype(jnp.bfloat16)
    ga2 = ga2_in[...] + ga2
    ga2_out[...] = ga2.astype(jnp.bfloat16)
    h = x[...].astype(jnp.float32) + attn[...].astype(jnp.float32)

    @pl.when(pl.program_id(0) == 0)
    def _():
        gain_out[...] = jnp.zeros_like(gain_out)

    gain_out[...] += jnp.sum(ga2 * (h * rms_scale(h)), axis=0, keepdims=True)


def mlp_specs(width, row_tile, col_tile):
    wide = pl.BlockSpec((row_tile, width), lambda t, c: (t, 0))
    wcol = pl.BlockSpec((width, col_tile), lambda t, c: (0, c))
    narrow = pl.BlockSpec((row_tile, col_tile), lambda t, c: (t, c))
    one = pl.BlockSpec((1, width), lambda t, c: (0, 0))
    return wide, wcol, narrow, one


def mlp_forward(lengths, x, attn, cot, gain, wg, wu, row_tile=512, col_tile=512):
    rows, width = x.shape
    ff = wg.shape[1]
    wide, wcol, narrow, _ = mlp_specs(width, row_tile, col_tile)
    return pl.pallas_call(
        mlp_forward_kernel,
        grid=(rows // row_tile, ff // col_tile),
        out_shape=[jax.ShapeDtypeStruct((rows, width), jnp.bfloat16)] * 2
        + [jax.ShapeDtypeStruct((rows, ff), jnp.bfloat16)] * 3,
        in_specs=[pl.BlockSpec(memory_space=pltpu.SMEM), wide, wide, wide,
                  pl.BlockSpec(gain.shape, lambda t, c: (0, 0, 0)), wcol, wcol],
        out_specs=[wide, wide, narrow, narrow, narrow],
        compiler_params=pltpu.CompilerParams(vmem_limit_bytes=60 * 1024 * 1024),
        cost_estimate=pl.CostEstimate(flops=4 * rows * width * ff, bytes_accessed=50 << 20, transcendentals=rows * ff),
        name="mlp_forward",
    )(lengths, x, attn, cot, gain, wg, wu)


def mlp_backward(which, gm, hid, gu, up, wg, wu, wd, rest=()):
    rows, width = gm.shape
    half = wd.shape[1]
    wide = pl.BlockSpec((TILE, width), lambda t: (t, 0))
    narrow = pl.BlockSpec((TILE, half), lambda t: (t, which))
    alone = pl.BlockSpec((TILE, half), lambda t: (t, 0))
    weight = pl.BlockSpec((width, half), lambda t: (0, which), pipeline_mode=pl.Buffered(1))
    bf, f32 = jnp.bfloat16, jnp.float32
    kind = bf if rest else f32
    shapes = [((rows, half), bf)] * 2 + [((rows, width), kind)] * 2
    out_specs = [alone, alone, wide, wide]
    if rest:
        shapes.append(((1, width), f32))
        out_specs.append(whole((1, width)))
    return pl.pallas_call(
        functools.partial(mlp_backward_kernel, bool(rest)),
        grid=(rows // TILE,),
        out_shape=[jax.ShapeDtypeStruct(*s) for s in shapes],
        in_specs=[wide, narrow, narrow, narrow, weight, weight, whole(wd.shape)] + [wide] * len(rest),
        out_specs=out_specs,
        compiler_params=pltpu.CompilerParams(vmem_limit_bytes=60 * 1024 * 1024),
        cost_estimate=pl.CostEstimate(flops=8 * rows * width * half, bytes_accessed=40 << 20, transcendentals=rows * half),
        name="mlp_backward",
    )(gm, hid, gu, up, wg, wu, wd, *rest)


def attn_backward_kernel(
    lengths, g2, x, attn, mlp, cot, gain_two, query_gain, key_gain, cos, sin,
    qr, kr, v, q, k, gate, o, lse, wq, wg, wk, wv, wo,
    y_out, ghb_out, og_out, gall_out, ga1_out, gain_out, small_out, square_out,
    krt, gk, gv, gq_s,
):
    step = pl.program_id(0)
    steps = SLOT_LEN // TILE
    tile = steps - 1 - step
    hd = query_gain.shape[1]
    heads, kv = wq.shape[1] // hd, wk.shape[1] // hd
    group = heads // kv
    seq_length = lengths[0]
    scale = hd ** -0.5

    @pl.when(step == 0)
    def _():
        krt[...] = kr[...].astype(jnp.float32).T.astype(jnp.bfloat16)
        gk[...] = jnp.zeros_like(gk)
        gv[...] = jnp.zeros_like(gv)
        gain_out[...] = jnp.zeros_like(gain_out)
        small_out[...] = jnp.zeros_like(small_out)
        square_out[...] = jnp.zeros_like(square_out)

    places = tile * TILE + lax.broadcasted_iota(jnp.int32, (TILE, 1), 0)
    live = places < seq_length
    xf = x[...].astype(jnp.float32)
    attn_f = attn[...].astype(jnp.float32)
    mlp_f = mlp[...].astype(jnp.float32)
    h = xf + attn_f
    y = h + mlp_f
    y_out[...] = jnp.where(live, y, 0.0).astype(jnp.bfloat16)
    first_lane = (lax.broadcasted_iota(jnp.int32, (1, hd), 1) == 0).astype(jnp.float32)
    width = float(xf.shape[1])
    mean_x = jnp.mean(xf * xf, axis=-1, keepdims=True)
    mean_h = jnp.mean(h * h, axis=-1, keepdims=True)
    for r, mean in ((0, mean_x), (1, mean_h)):
        square_out[r : r + 1, :] += jnp.sum(jnp.where(live, mean, 0.0), axis=0, keepdims=True) * width * first_lane
    for r, field in ((2, y), (3, attn_f), (4, mlp_f)):
        by_lane = jnp.sum(jnp.where(live, field * field, 0.0), axis=0, keepdims=True)
        folded = by_lane[:, :hd]
        for low in range(hd, by_lane.shape[1], hd):
            folded = folded + by_lane[:, low : low + hd]
        square_out[r : r + 1, :] += folded
    square_out[5:6, :] += jnp.sum(live.astype(jnp.float32), axis=0, keepdims=True) * first_lane
    rho = lax.rsqrt(mean_h + NORM_EPS)
    n = h * rho
    gs = g2[...].astype(jnp.float32) * gain_row(gain_two, 1)
    g_out = jnp.where(live, cot[...].astype(jnp.float32), 0.0)
    ghb = (g_out + rho * (gs - n * jnp.mean(gs * n, axis=-1, keepdims=True))).astype(jnp.bfloat16)
    ghb_out[...] = ghb
    g_og = nn(ghb, wo[...])
    sig = jax.nn.sigmoid(gate[...])
    of = o[...]
    og_out[...] = (of * sig).astype(jnp.bfloat16)
    g_o = (g_og * sig).astype(jnp.bfloat16)
    q_width, k_width = heads * hd, kv * hd
    gall_out[:, q_width : 2 * q_width] = (g_og * of * sig * (1.0 - sig)).astype(jnp.bfloat16)

    for i in range(steps):
        @pl.when(tile == i)
        def _(i=i):
            count = (i + 1) * TILE
            mask = allowed_keys(count, group * TILE, i * TILE, seq_length)
            for j in range(kv):
                cols = slice(j * hd, (j + 1) * hd)
                mine = [slice((j * group + g) * hd, (j * group + g + 1) * hd) for g in range(group)]
                stack = jnp.concatenate([qr[:, s] for s in mine], axis=0)
                g_stack = jnp.concatenate([g_o[:, s] for s in mine], axis=0)
                scores = nt(kr[:count, cols], stack) * scale
                probs = jnp.where(mask, jnp.exp(jnp.where(mask, scores, MASKED) - lse[0, j : j + 1, :]), 0.0)
                g_p = nt(v[:count, cols], g_stack)
                inner = jnp.sum(probs * g_p, axis=0, keepdims=True)
                g_s = (probs * (g_p - inner)).astype(jnp.bfloat16)
                gk[:count, cols] += nn(g_s, stack) * scale
                gv[:count, cols] += nn(probs.astype(jnp.bfloat16), g_stack)
                gqt = nn(krt[cols, :count], g_s) * scale
                back = gqt.T
                for g in range(group):
                    gq_s[:, mine[g]] = back[g * TILE : (g + 1) * TILE, :]

    def unrope(g, u, gain):
        g = g * cos[...] - pltpu.roll(g, hd // 2, 1) * sin[...]
        r = rms_scale(u)
        nu = u * r
        gain_grad = jnp.sum(g * nu, axis=0, keepdims=True)
        ga = g * gain[...].astype(jnp.float32)
        return r * (ga - nu * jnp.mean(ga * nu, axis=-1, keepdims=True)), gain_grad

    for head in range(heads):
        cols = slice(head * hd, (head + 1) * hd)
        g, gain_grad = unrope(gq_s[:, cols], q[:, cols], query_gain)
        gall_out[:, cols] = g.astype(jnp.bfloat16)
        small_out[0:1, :] += gain_grad
    rows = pl.ds(pl.multiple_of(tile * TILE, TILE), TILE)
    for j in range(kv):
        cols = slice(j * hd, (j + 1) * hd)
        g, gain_grad = unrope(gk[rows, cols], k[:, cols], key_gain)
        gall_out[:, 2 * q_width + j * hd : 2 * q_width + (j + 1) * hd] = g.astype(jnp.bfloat16)
        small_out[1:2, :] += gain_grad
    gall_out[:, 2 * q_width + k_width :] = gv[rows, :].astype(jnp.bfloat16)
    ga1 = (
        nt(gall_out[:, :q_width], wq[...])
        + nt(gall_out[:, q_width : 2 * q_width], wg[...])
        + nt(gall_out[:, 2 * q_width : 2 * q_width + k_width], wk[...])
        + nt(gall_out[:, 2 * q_width + k_width :], wv[...])
    )
    ga1_out[...] = ga1.astype(jnp.bfloat16)

    @pl.when(step == steps - 1)
    def _():
        square_out[...] = square_out[...] * (lax.axis_index("heads") == 0).astype(jnp.float32)

    gain_out[...] += jnp.sum(ga1 * (xf * lax.rsqrt(mean_x + NORM_EPS)), axis=0, keepdims=True)


def attn_backward(lengths, g2, x, attn, mlp, cot, gain_two, query_gain, key_gain, cos, sin,
                  qr, kr, v, q, k, gate, o, lse, wq, wg, wk, wv, wo):
    rows, width = x.shape
    steps = rows // TILE
    q_width, k_width = wq.shape[1], wk.shape[1]
    hd = query_gain.shape[1]
    tile = lambda w: pl.BlockSpec((TILE, w), lambda i: (steps - 1 - i, 0))
    bf, f32 = jnp.bfloat16, jnp.float32
    total = 2 * q_width + 2 * k_width
    return pl.pallas_call(
        attn_backward_kernel,
        grid=(steps,),
        out_shape=[
            jax.ShapeDtypeStruct((rows, width), bf), jax.ShapeDtypeStruct((rows, width), bf),
            jax.ShapeDtypeStruct((rows, q_width), bf), jax.ShapeDtypeStruct((rows, total), bf),
            jax.ShapeDtypeStruct((rows, width), bf), jax.ShapeDtypeStruct((1, width), f32),
            jax.ShapeDtypeStruct((2, hd), f32), jax.ShapeDtypeStruct((6, hd), f32),
        ],
        in_specs=[pl.BlockSpec(memory_space=pltpu.SMEM)] + [tile(width)] * 5
        + [whole(gain_two.shape), whole((1, hd)), whole((1, hd)), tile(hd), tile(hd),
                  tile(q_width), whole((rows, k_width)), whole((rows, k_width)), tile(q_width), tile(k_width),
                  tile(q_width), tile(q_width), pl.BlockSpec((1,) + lse.shape[1:], lambda i: (steps - 1 - i, 0, 0))]
        + [whole(w.shape) for w in (wq, wg, wk, wv, wo)],
        out_specs=[tile(width), tile(width), tile(q_width), tile(total), tile(width), whole((1, width)), whole((2, hd)), whole((6, hd))],
        scratch_shapes=[pltpu.VMEM((k_width, rows), bf), pltpu.VMEM((rows, k_width), f32),
                        pltpu.VMEM((rows, k_width), f32), pltpu.VMEM((TILE, q_width), f32)],
        compiler_params=pltpu.CompilerParams(vmem_limit_bytes=60 * 1024 * 1024),
        cost_estimate=pl.CostEstimate(flops=2 * rows * width * (3 * q_width + 2 * k_width) + (12 << 30), bytes_accessed=50 << 20, transcendentals=4 << 20),
        name="attn_backward",
    )(lengths, g2, x, attn, mlp, cot, gain_two, query_gain, key_gain, cos, sin,
      qr, kr, v, q, k, gate, o, lse, wq, wg, wk, wv, wo)


def finish_kernel(moves, count, x, gain, grad_hidden, grad_sum, *refs):
    ins, tokens_out, outs = refs[:count], refs[count], refs[count + 1 :]
    xf = x[...].astype(jnp.float32)
    rho = rms_scale(xf)
    n = xf * rho
    gs = grad_sum[...].astype(jnp.float32) * gain_row(gain, 0)
    back = rho * (gs - n * jnp.mean(gs * n, axis=-1, keepdims=True))
    tokens_out[...] = (grad_hidden[...].astype(jnp.float32) + back).astype(jnp.bfloat16)
    for source, low, width, target, place in moves:
        outs[target][:, place : place + width] = ins[source][:, low : low + width].astype(jnp.float32)


def finish(x, gain, grad_hidden, grad_sum, grads, moves, widths):
    rows, width = x.shape
    shard = grads[0].shape[0]
    steps = 4
    tile = pl.BlockSpec((rows // steps, width), lambda i: (i, 0))
    part = lambda w: pl.BlockSpec((shard // steps, w), lambda i: (i, 0))
    return pl.pallas_call(
        functools.partial(finish_kernel, moves, len(grads)),
        grid=(steps,),
        out_shape=[jax.ShapeDtypeStruct((rows, width), jnp.bfloat16)]
        + [jax.ShapeDtypeStruct((shard, w), jnp.float32) for w in widths],
        in_specs=[tile, whole(gain.shape), tile, tile] + [part(g.shape[1]) for g in grads],
        out_specs=[tile] + [part(w) for w in widths],
        compiler_params=pltpu.CompilerParams(vmem_limit_bytes=60 * 1024 * 1024),
        cost_estimate=pl.CostEstimate(flops=20 * rows * width, bytes_accessed=30 << 20, transcendentals=0),
        name="finish",
    )(x, gain, grad_hidden, grad_sum, *grads)


def scatter_kernel(units, sources, kept, lefts, count, A, B, H, small_count, sums, *refs):
    nu = len(units)
    left_refs, refs = refs[:lefts], refs[lefts:]
    ins, refs = refs[:count], refs[count:]
    kept_ins, refs = refs[: len(kept)], refs[len(kept) :]
    if H:
        pieces, refs = refs[:small_count], refs[small_count:]
    sum_ins, refs = refs[:sums], refs[sums:]
    outs, sum_outs, refs = refs[:count], refs[count : count + sums], refs[count + sums :]
    if H:
        small_out, refs = refs[0], refs[1:]
    kept_outs, refs = refs[: len(kept)], refs[len(kept) :]
    rest = list(refs)
    each = SUM_REFS - 2
    totals = [HeadSum((sum_ins[i], sum_outs[i]) + tuple(rest[i * each : (i + 1) * each])) for i in range(sums)]
    rest = rest[sums * each :]
    if H:
        small, row_in, col_in, row_send, row_recv, col_send, col_recv = rest[-7:]
        rest = rest[:-7]
    turned, rest = rest[:lefts], rest[lefts:]
    own, side_in, up_in, down_in, stage = (rest[k * nu:(k + 1) * nu] for k in range(5))
    side_send, side_recv, up_send, up_recv, down_send, down_recv = rest[5 * nu:]
    me = lax.axis_index("batch")
    a, b = me // B, me % B
    up_ok, down_ok = a < A - 1, a > 0

    R = own[0].shape[1]

    def product(u, blk, target):
        i, lo, width, _ = units[u]
        left = turned[sources[i]][pl.ds(pl.multiple_of(blk * R, R), R), :]
        target[...] = nn(left, ins[i][:, lo : lo + width]).astype(jnp.bfloat16)

    def turn(blk):
        for left, flat in zip(left_refs, turned):
            flat[pl.ds(pl.multiple_of(blk * R, R), R), :] = left[:, pl.ds(pl.multiple_of(blk * R, R), R)].T

    barrier = pltpu.get_barrier_semaphore()

    def greet(target):
        pl.semaphore_signal(barrier, inc=1, device_id={"batch": target}, device_id_type=MESH)

    n = A * B
    if H:
        head = lax.axis_index("heads")
        for k in range(1, n):
            greet((me + k) % n)
        for k in range(1, H):
            pl.semaphore_signal(barrier, inc=1, device_id={"heads": (head + k) % H}, device_id_type=MESH)
        guests = n - 1 + H - 1
    else:
        pl.when(up_ok)(lambda: greet(me + B))
        pl.when(down_ok)(lambda: greet(me - B))
        for k in range(1, B):
            greet(a * B + (b + k) % B)
        guests = up_ok.astype(jnp.int32) + down_ok.astype(jnp.int32) + (B - 1)
        if totals:
            totals[0].greet(barrier)
            guests = guests + 2

    def at_distance(d, fn):
        if d == 0:
            return

        @pl.when(a + d < A)
        def _():
            fn(a + d, True)

        @pl.when(a - d >= 0)
        def _():
            fn(a - d, False)

    if R % 128:
        for left, flat in zip(left_refs, turned):
            for low in range(0, flat.shape[0], 256):
                flat[low : low + 256, :] = left[:, low : low + 256].T
    pl.semaphore_wait(barrier, guests)
    for total in totals:
        total.start()

    def to_heads(k):
        return pltpu.make_async_remote_copy(
            small, row_in.at[head], row_send.at[k - 1], row_recv.at[head],
            device_id={"heads": (head + k) % H}, device_id_type=MESH)

    def to_batch(k):
        return pltpu.make_async_remote_copy(
            col_in.at[me], col_in.at[me], col_send.at[k - 1], col_recv.at[me],
            device_id={"batch": (me + k) % n}, device_id_type=MESH)

    if H:
        low = 0
        for piece_ref in pieces:
            rows = piece_ref.shape[0]
            small[low : low + rows, :] = piece_ref[...]
            low += rows
        for k in range(1, H):
            to_heads(k).start()
        row_in[head] = small[...]

    for d in range(A - 1, -1, -1):
        def start(dest, _=None):
            for k in range(1, B):
                bb = (b + k) % B
                if R % 128 == 0:
                    turn(dest * B + bb)
                for u in range(nu):
                    if units[u][3]:
                        continue
                    product(u, dest * B + bb, stage[u].at[k - 1, dest])
                    pltpu.make_async_remote_copy(
                        stage[u].at[k - 1, dest], side_in[u].at[k - 1, dest], side_send.at[u, k - 1, dest],
                        side_recv.at[u, k - 1, dest], device_id={"batch": a * B + bb}, device_id_type=MESH).start()

        at_distance(d, start) if d else start(a)
        if d == A - 1:
            for total in totals:
                total.cross()
    if R % 128 == 0:
        for dest in range(A):
            turn(dest * B + b)
    for which, right, whole_out in zip(kept, kept_ins, kept_outs):
        def keep(blk, carry, which=which, right=right, whole_out=whole_out):
            rows = pl.ds(pl.multiple_of(blk * R, R), R)
            whole_out[rows, :] = nn(turned[which][rows, :], right[...]).astype(jnp.bfloat16)
            return carry

        lax.fori_loop(0, n, keep, 0)

    def await_bytes(ref, sem):
        pltpu.make_async_copy(ref, ref, sem).wait()

    if H:
        for k in range(1, H):
            other = (head + k) % H
            await_bytes(row_in.at[other], row_recv.at[other])
        group_sum = row_in[0]
        for k in range(1, H):
            group_sum = group_sum + row_in[k]
        col_in[me] = group_sum
        for k in range(1, n):
            to_batch(k).start()

    step_rows = min(R, 32)

    def add_into(target, terms):
        def body(t, carry):
            rows = pl.ds(pl.multiple_of(t * step_rows, step_rows), step_rows)
            total = terms[0][rows, :].astype(jnp.float32)
            for term in terms[1:]:
                total = total + term[rows, :].astype(jnp.float32)
            target[rows, :] = total.astype(target.dtype)
            return carry

        lax.fori_loop(0, R // step_rows, body, 0)

    def local_terms(u, dest, bb):
        if units[u][3]:
            slot = dest * B + bb
            product(u, slot, own[u].at[slot])
            return [own[u].at[slot]], slot
        product(u, dest * B + b, own[u].at[dest])
        for k in range(1, B):
            await_bytes(side_in[u].at[k - 1, dest], side_recv.at[u, k - 1, dest])
        return [own[u].at[dest]] + [side_in[u].at[k - 1, dest] for k in range(1, B)], dest

    order = [u for u in range(nu) if units[u][3]] + [u for u in range(nu) if not units[u][3]]
    for d in range(A - 1, 0, -1):
        for u in order:
            def flow(dest, goes_up, u=u):
                for k in range(B if units[u][3] else 1):
                    terms, slot = local_terms(u, dest, (b + k) % B)
                    buf = (up_in if goes_up else down_in)[u].at[slot]
                    send, recv = (up_send, up_recv) if goes_up else (down_send, down_recv)
                    fed = down_ok if goes_up else up_ok

                    @pl.when(fed)
                    def _():
                        await_bytes(buf, recv.at[u, slot])
                        add_into(buf, [buf] + terms)

                    @pl.when(jnp.logical_not(fed))
                    def _():
                        add_into(buf, terms)

                    pltpu.make_async_remote_copy(
                        buf, buf, send.at[u, slot], recv.at[u, slot],
                        device_id={"batch": me + B if goes_up else me - B}, device_id_type=MESH).start()

            at_distance(d, flow)

    def out_piece(u):
        i, lo, width, _ = units[u]
        return outs[i].at[:, pl.ds(lo, width)]

    def arrive_home(u, bb, target):
        terms, slot = local_terms(u, a, bb)

        @pl.when(down_ok)
        def _():
            await_bytes(up_in[u].at[slot], up_recv.at[u, slot])

        @pl.when(up_ok)
        def _():
            await_bytes(down_in[u].at[slot], down_recv.at[u, slot])

        @pl.when(down_ok & up_ok)
        def _():
            add_into(target, terms + [up_in[u].at[slot], down_in[u].at[slot]])

        @pl.when(down_ok & jnp.logical_not(up_ok))
        def _():
            add_into(target, terms + [up_in[u].at[slot]])

        @pl.when(up_ok & jnp.logical_not(down_ok))
        def _():
            add_into(target, terms + [down_in[u].at[slot]])

    for total in totals:
        total.settle()
    for u in order:
        if units[u][3]:
            for k in range(1, B):
                bb = (b + k) % B
                slot = a * B + bb
                arrive_home(u, bb, own[u].at[slot])
                pltpu.make_async_remote_copy(
                    own[u].at[slot], side_in[u].at[k - 1, 0], side_send.at[u, k - 1, 0], side_recv.at[u, k - 1, 0],
                    device_id={"batch": slot}, device_id_type=MESH).start()
            arrive_home(u, b, own[u].at[a * B + b])
        else:
            arrive_home(u, b, out_piece(u))
    for u in order:
        if units[u][3]:
            for k in range(1, B):
                await_bytes(side_in[u].at[k - 1, 0], side_recv.at[u, k - 1, 0])
            add_into(out_piece(u), [own[u].at[a * B + b]] + [side_in[u].at[k - 1, 0] for k in range(1, B)])

    for total in totals:
        total.finish()
    if H:
        for k in range(1, n):
            other = (me + k) % n
            await_bytes(col_in.at[other], col_recv.at[other])
        whole_sum = col_in[0]
        for k in range(1, n):
            whole_sum = whole_sum + col_in[k]
        small_out[...] = whole_sum
        for k in range(1, H):
            to_heads(k).wait_send()
        for k in range(1, n):
            to_batch(k).wait_send()

    for u in range(nu):
        first = units[u][3]
        for k in range(1, B):
            if first:
                await_bytes(side_in[u].at[k - 1, 0], side_send.at[u, k - 1, 0])
            else:
                for dest in range(A):
                    await_bytes(side_in[u].at[k - 1, dest], side_send.at[u, k - 1, dest])
        for d in range(A - 1, 0, -1):
            def done(dest, goes_up, u=u, first=first):
                send = up_send if goes_up else down_send
                for k in range(B if first else 1):
                    slot = dest * B + k if first else dest
                    await_bytes(up_in[u].at[slot], send.at[u, slot])

            at_distance(d, done)


def scatter_all(lefts, rights, sources, units, cid, small=None, sums=(), kept=(), kept_rights=(), out_dtype=jnp.bfloat16):
    n = lax.axis_size("batch")
    A, B = grid_of(n)
    nu = len(units)
    R = lefts[0].shape[1] // n

    def slots(u):
        return n if units[u][3] else A

    scratch = [ref for s in sums for ref in head_sum_scratch(s)]
    scratch += [pltpu.VMEM(left.shape[::-1], left.dtype) for left in lefts]
    scratch += [pltpu.VMEM((slots(u), R, units[u][2]), jnp.bfloat16) for u in range(nu)]
    scratch += [pltpu.VMEM((B - 1, 1 if units[u][3] else A, R, units[u][2]), jnp.bfloat16) for u in range(nu)]
    scratch += [pltpu.VMEM((slots(u), R, units[u][2]), jnp.bfloat16) for u in range(nu)]
    scratch += [pltpu.VMEM((slots(u), R, units[u][2]), jnp.bfloat16) for u in range(nu)]
    scratch += [pltpu.VMEM((B - 1, 1 if units[u][3] else A, R, units[u][2]), jnp.bfloat16) for u in range(nu)]
    dma = pltpu.SemaphoreType.DMA
    scratch += [dma((nu, B - 1, A)), dma((nu, B - 1, A)), dma((nu, n)), dma((nu, n)), dma((nu, n)), dma((nu, n))]
    H = 0
    extra, small_outs = [], []
    if small is not None:
        H = lax.axis_size("heads")
        extra = list(small)
        small_shape = (sum(e.shape[0] for e in extra), extra[0].shape[1])
        small_outs = [jax.ShapeDtypeStruct(small_shape, jnp.float32)]
        scratch += [
            pltpu.VMEM(small_shape, jnp.float32),
            pltpu.VMEM((H,) + small_shape, jnp.float32), pltpu.VMEM((n,) + small_shape, jnp.float32),
            dma((H - 1,)), dma((H,)), dma((n - 1,)), dma((n,)),
        ]
    res = pl.pallas_call(
        functools.partial(scatter_kernel, units, sources, kept, len(lefts), len(rights), A, B, H, len(extra), len(sums)),
        out_shape=[jax.ShapeDtypeStruct((R, g.shape[1]), out_dtype) for g in rights]
        + [jax.ShapeDtypeStruct(s.shape, s.dtype) for s in sums]
        + small_outs
        + [jax.ShapeDtypeStruct((lefts[w].shape[1], g.shape[1]), out_dtype) for w, g in zip(kept, kept_rights)],
        in_specs=[pl.BlockSpec(memory_space=pltpu.VMEM)] * (len(lefts) + len(rights) + len(kept)) + [pl.BlockSpec(memory_space=pltpu.VMEM)] * len(extra) + [pl.BlockSpec(memory_space=pl.ANY)] * len(sums),
        out_specs=[pl.BlockSpec(memory_space=pltpu.VMEM)] * len(rights) + [pl.BlockSpec(memory_space=pl.ANY)] * len(sums)
        + [pl.BlockSpec(memory_space=pltpu.VMEM)] * (len(small_outs) + len(kept)),
        scratch_shapes=scratch,
        compiler_params=pltpu.CompilerParams(collective_id=cid, has_side_effects=True, vmem_limit_bytes=VMEM_LIMIT),
        cost_estimate=pl.CostEstimate(flops=0, bytes_accessed=sum(g.size for g in rights) * 16, transcendentals=0),
    )(*lefts, *rights, *kept_rights, *extra, *sums)
    return list(res)


def column_units(widths, side_first, chunk=512):
    units = []
    for index, width in enumerate(widths):
        for low in range(0, width, chunk):
            units.append((index, low, min(chunk, width - low), (index, low) in side_first))
    return units


def local(
    tokens,
    lengths,
    cotangent,
    attn_norm_gain,
    query_norm_gain,
    key_norm_gain,
    w_query,
    w_gate_attn,
    w_key,
    w_value,
    w_out,
    mlp_norm_gain,
    w_gate,
    w_up,
    w_down,
):
    row_count, model_width = tokens.shape
    head_width = query_norm_gain.shape[0]
    shard_rows = w_query.shape[0]
    attn_shards = [w_query, w_gate_attn, w_key, w_value, w_out]
    gain_shards = [jnp.stack([attn_norm_gain, mlp_norm_gain])]
    q_width, k_width = w_query.shape[1], w_key.shape[1]
    gather_units = [
        (5, None, None, False),
        (0, 0, q_width, False),
        (1, 0, q_width, False),
        (2, 0, k_width, True),
        (3, 0, k_width, False),
        (4, 0, q_width, False),
    ]
    query_full, gate_attn_full, key_full, value_full, out_full, gains, cos_table, sin_table = gather_all(
        attn_shards + gain_shards, gather_units, 0, tables=(row_count, head_width)
    )
    cut = w_down.shape[1] // 2
    down_first, down_last = w_down[:, :cut], w_down[:, cut:]
    down_first, query_full = lax.optimization_barrier((down_first, query_full))
    down_first = lax.all_gather(down_first, "batch", axis=0, tiled=True)
    gains = gains.reshape(-1, 2, shard_rows)
    query_gain = query_norm_gain.reshape(1, -1)
    key_gain = key_norm_gain.reshape(1, -1)
    attn_weights = (query_full, gate_attn_full, key_full, value_full, out_full)
    input_one, query_rot, key_rot, values, queries, keys_pre, gate_logit, attended, log_totals, attn_part = attn_forward(
        lengths, tokens, gains, query_gain, key_gain, cos_table, sin_table, *attn_weights
    )
    mlp_widths = [w_gate.shape[1], w_up.shape[1]]
    gate_full, up_full, attn_sum = gather_all(
        [w_gate, w_up], column_units(mlp_widths, {(1, 0)}, 384), 1, sums=[attn_part]
    )
    down_last, attn_sum = lax.optimization_barrier((down_last, attn_sum))
    down_last = lax.all_gather(down_last, "batch", axis=0, tiled=True)
    input_two, grad_mlp, activated, gate_pre, up_pre = mlp_forward(
        lengths, tokens, attn_sum, cotangent, gains, gate_full, up_full
    )
    grad_w_down = contract_rows(grad_mlp, activated).astype(jnp.bfloat16)
    grad_w_down, grad_mlp, activated = lax.optimization_barrier((grad_w_down, grad_mlp, activated))
    grad_down = lax.psum_scatter(grad_w_down, "batch", scatter_dimension=0, tiled=True)
    halves = (activated, gate_pre, up_pre, gate_full, up_full)
    grad_gate_first, grad_up_first, part_first, grad_two_first = mlp_backward(0, grad_mlp, *halves, down_first)
    grad_gate_last, grad_up_last, mlp_part, grad_two_send, gain_two_part = mlp_backward(
        1, grad_mlp, *halves, down_last, (tokens, attn_sum, part_first, grad_two_first)
    )
    grad_gate_one, grad_gate_two, grad_up, grad_two_sum, mlp_sum, grad_w_late = scatter_all(
        [input_two],
        [grad_gate_first, grad_gate_last, grad_up_first],
        (0, 0, 0),
        column_units([cut] * 3, ()),
        2,
        sums=[grad_two_send, mlp_part],
        kept=(0,),
        kept_rights=[grad_up_last],
    )
    grad_late = lax.psum_scatter(grad_w_late, "batch", scatter_dimension=0, tiled=True)
    output, grad_hidden, gated, grad_all, grad_one_send, gain_one_part, head_gains, own_sums = attn_backward(
        lengths, grad_two_sum, tokens, attn_sum, mlp_sum, cotangent, gains, query_gain, key_gain,
        cos_table, sin_table, query_rot, key_rot, values, queries, keys_pre, gate_logit, attended, log_totals,
        *attn_weights,
    )
    small = [
        gain_one_part.reshape(-1, head_width), gain_two_part.reshape(-1, head_width), head_gains, own_sums,
    ]
    attn_units = [
        (0, 0, q_width, False),
        (0, q_width, q_width, False),
        (0, 2 * q_width, k_width, True),
        (0, 2 * q_width + k_width, k_width, False),
        (1, 0, q_width, False),
    ]
    grad_all_sum, grad_out_sum, grad_one_sum, sums = scatter_all(
        [input_one, grad_hidden],
        [grad_all, gated],
        (0, 1),
        attn_units,
        3,
        small,
        sums=[grad_one_send],
    )
    gain_rows = model_width // head_width
    mine = lax.axis_index("batch") * shard_rows
    gain_one_grad = lax.dynamic_slice(sums[:gain_rows].reshape(-1), (mine,), (shard_rows,))
    gain_two_grad = lax.dynamic_slice(sums[gain_rows : 2 * gain_rows].reshape(-1), (mine,), (shard_rows,))
    query_gain_all = sums[2 * gain_rows]
    key_gain_all = sums[2 * gain_rows + 1]
    squares_all = jnp.sum(sums[2 * gain_rows + 2 :], axis=1)
    block_rms = jnp.sqrt(squares_all[:5] / (squares_all[5] * model_width))
    widths = [w.shape[1] for w in attn_shards] + [w_gate.shape[1], w_up.shape[1], w_down.shape[1]]
    moves, low = [], 0
    for index in range(4):
        moves.append((0, low, widths[index], index, 0))
        low += widths[index]
    moves += [
        (1, 0, widths[4], 4, 0),
        (2, 0, cut, 5, 0),
        (3, 0, widths[5] - cut, 5, cut),
        (4, 0, cut, 6, 0),
        (5, 0, widths[6] - cut, 6, cut),
        (6, 0, widths[7], 7, 0),
    ]
    grad_tokens, *weight_grads = finish(
        tokens, gains, grad_hidden, grad_one_sum,
        [grad_all_sum, grad_out_sum, grad_gate_one, grad_gate_two, grad_up, grad_late, grad_down], moves, widths,
    )
    return (
        output,
        grad_tokens,
        gain_one_grad,
        query_gain_all,
        key_gain_all,
        *weight_grads[:5],
        gain_two_grad,
        *weight_grads[5:],
        block_rms,
    )


def solution(mesh):
    return jax.shard_map(
        local,
        mesh=mesh,
        in_specs=(
            P("batch", None),
            P("batch"),
            P("batch", None),
            P("batch"),
            P(),
            P(),
            P("batch", "heads"),
            P("batch", "heads"),
            P("batch", "heads"),
            P("batch", "heads"),
            P("batch", "heads"),
            P("batch"),
            P("batch", "heads"),
            P("batch", "heads"),
            P("batch", "heads"),
        ),
        out_specs=(
            P("batch", None),
            P("batch", None),
            P("batch"),
            P(),
            P(),
            P("batch", "heads"),
            P("batch", "heads"),
            P("batch", "heads"),
            P("batch", "heads"),
            P("batch", "heads"),
            P("batch"),
            P("batch", "heads"),
            P("batch", "heads"),
            P("batch", "heads"),
            P(),
        ),
        check_vma=False,
    )
```
